32 devices in a mesh: batch: 8 (over z, x), tensor: 4 (over y, core).
Axes of the slice: x: 2, y: 2, z: 4, core: 2. Of those that a mesh axis runs over, the one named last changes fastest.
Arguments:
- tokens: bfloat16 [2, 8192, 768], P(None, 'batch'), may hold values from -6 to 6
- lengths: int32 [2, 8, 1024], P(None, 'batch'), may hold values from 0 to 512, as said below
- quarters: int32 [2], replicated, may hold values from 1 to 4, as said below
- query_weight: bfloat16 [768, 768], P(None, 'tensor'), may hold values from -0.3125 to 0.3125
- query_bias: float32 [768], P('tensor'), may hold values from -4 to 4
- key_weight: bfloat16 [768, 768], P(None, 'tensor'), may hold values from -0.3125 to 0.3125
- value_weight: bfloat16 [768, 768], P(None, 'tensor'), may hold values from -0.21875 to 0.21875
- value_bias: float32 [768], P('tensor'), may hold values from -6 to 6
- out_weight: bfloat16 [768, 768], P('tensor'), may hold values from -0.625 to 0.625
- out_bias: float32 [768], replicated, may hold values from -6 to 6
- norm1_gain: float32 [768], replicated, may hold values from 0.5 to 1.5
- norm1_shift: float32 [768], replicated, may hold values from -4 to 4
- in_weight: bfloat16 [768, 3072], P(None, 'tensor'), may hold values from -0.21875 to 0.21875
- in_bias: float32 [3072], P('tensor'), may hold values from -6 to 6
- down_weight: bfloat16 [3072, 768], P('tensor'), may hold values from -0.109375 to 0.109375
- down_bias: float32 [768], replicated, may hold values from -6 to 6
- norm2_gain: float32 [768], replicated, may hold values from 0.5 to 1.5
- norm2_shift: float32 [768], replicated, may hold values from -4 to 4
- cotangent: bfloat16 [2, 8192, 768], P(None, 'batch'), may hold values from -6 to 6
Outputs:
- layer_out: bfloat16 [2, 8192, 768], P(None, ('batch', 'tensor'))
- input_grad: float32 [2, 8192, 768], P(None, ('batch', 'tensor'))
- query_weight_grad: float32 [768, 768], P(None, 'tensor')
- query_bias_grad: float32 [768], P('tensor')
- key_weight_grad: float32 [768, 768], P(None, 'tensor')
- value_weight_grad: float32 [768, 768], P(None, 'tensor')
- value_bias_grad: float32 [768], P('tensor')
- out_weight_grad: float32 [768, 768], P('tensor')
- out_bias_grad: float32 [768], replicated
- norm1_gain_grad: float32 [768], replicated
- norm1_shift_grad: float32 [768], replicated
- in_weight_grad: float32 [768, 3072], P(None, 'tensor')
- in_bias_grad: float32 [3072], P('tensor')
- down_weight_grad: float32 [3072, 768], P('tensor')
- down_bias_grad: float32 [768], replicated
- norm2_gain_grad: float32 [768], replicated
- norm2_shift_grad: float32 [768], replicated
The draws below stay inside these ranges and needn't reach their ends.
Inputs may be any that keep to these rules, and one draw needn't show every extreme that they name: Row lengths[m, b] lists, in order, the lengths of the sequences packed into block b of micro-batch m; they sum to 1024, and 0 marks an unused slot. In every micro-batch one block holds a sequence of exactly 512 tokens. Micro-batch m keeps the first 12 * quarters[m] / 4 heads and the first 3072 * quarters[m] / 4 units; exactly one micro-batch has quarters 4.
All inputs are finite; a program needn't handle non-finite values.
Results may differ from the reference program's by a relative error of at most 0.013.
The reference program's roundings to bfloat16 on the way count: a program that leaves them out, or rounds other values in their place, can miss the bound.
Values may be sent and summed in bfloat16 or wider, within the bound.
A program may use at most 128 MiB of HBM per device.

```python
import jax
import jax.numpy as jnp
from jax import lax

D = 768
HEADS = 12
HEAD_DIM = 64
FF = 3072
ROWS = 1024
MB = 2
LONG = 512
BLOCKS = 8
TOKENS = 8192


def draw_lengths(key, part):
    half_long = max(LONG // 2, 1)
    key_list = jax.random.split(key, 4)
    shape_all = (MB, BLOCKS, ROWS)
    factor_one = jax.random.randint(key_list[0], shape_all, 1, half_long + 1)
    factor_two = jax.random.randint(key_list[1], shape_all, 1, half_long + 1)
    factor_three = jax.random.randint(key_list[2], shape_all, 1, half_long + 1)
    raw_lengths = jnp.maximum(factor_one * factor_two // half_long * factor_three // half_long, 1)
    chosen = jax.random.randint(key_list[3], (MB, 1, 1), 0, BLOCKS)
    block_ids = jnp.arange(BLOCKS, dtype=jnp.int32)[None, :, None]
    slot_ids = jnp.arange(ROWS, dtype=jnp.int32)[None, None, :]
    raw_lengths = jnp.where((block_ids == chosen) & (slot_ids == 0), LONG, raw_lengths).astype(jnp.int32)
    ends_at = jnp.minimum(jnp.cumsum(raw_lengths, axis=2).astype(jnp.int32), ROWS)
    ends_at = jnp.where(slot_ids == ROWS - 1, ROWS, ends_at)
    starts_at = jnp.concatenate([jnp.zeros((MB, BLOCKS, 1), jnp.int32), ends_at[:, :, :-1]], axis=2)
    return (ends_at - starts_at).astype(jnp.int32)


def draw_quarters(key, part):
    key_list = jax.random.split(key, 2)
    drawn = jax.random.randint(key_list[0], (MB,), 1, 4)
    full_one = jax.random.randint(key_list[1], (), 0, MB)
    return jnp.where(jnp.arange(MB, dtype=jnp.int32) == full_one, 4, drawn).astype(jnp.int32)


def shard_levels(stream_key, shape, pieces, least, largest):
    level, own = 1.0, jax.random.fold_in(stream_key, 6)
    for axis_at, shards_of in pieces:
        draws = jnp.exp(jax.random.uniform(jax.random.fold_in(own, axis_at), (shards_of,), jnp.float32, least / len(pieces), largest / len(pieces)))
        level = level * jnp.repeat(draws, shape[axis_at] // shards_of).reshape([-1 if axis == axis_at else 1 for axis in range(len(shape))])
    return level


def noise(rng, shape, spread, most, cuts=(), kind=jnp.bfloat16):
    values = jax.random.normal(rng, shape, jnp.float32) * spread
    if len(cuts) > 0:
        values = shard_levels(rng, shape, cuts, -0.22, 0.18) * values
    return jnp.clip(values, min=-most, max=most).astype(kind)


def setup_inputs(seed: int = 0) -> dict:
    arg_keys = jax.random.split(jax.random.key(seed), 20)
    return {
        "tokens": noise(arg_keys[0], (MB, TOKENS, D), 1.0, 6.0, ((1, 8),)),
        "lengths": draw_lengths(jax.random.fold_in(arg_keys[19], 71), 0),
        "quarters": draw_quarters(jax.random.fold_in(arg_keys[19], 71), 0),
        "query_weight": noise(arg_keys[3], (D, D), (D // 2) ** -0.5, 0.3125, ((1, 4),)),
        "query_bias": noise(arg_keys[4], (D,), 0.3, 4.0, ((0, 4),), jnp.float32),
        "key_weight": noise(arg_keys[5], (D, D), (D // 2) ** -0.5, 0.3125, ((1, 4),)),
        "value_weight": noise(arg_keys[6], (D, D), D ** -0.5, 0.21875, ((1, 4),)),
        "value_bias": noise(arg_keys[7], (D,), 0.5, 6.0, ((0, 4),), jnp.float32),
        "out_weight": noise(arg_keys[8], (D, D), (D // 8) ** -0.5, 0.625, ((0, 4),)),
        "out_bias": noise(arg_keys[9], (D,), 0.5, 6.0, (), jnp.float32),
        "norm1_gain": jnp.clip(1.0 + 0.1 * jax.random.normal(arg_keys[10], (D,), jnp.float32), 0.5, 1.5),
        "norm1_shift": noise(arg_keys[11], (D,), 0.3, 4.0, (), jnp.float32),
        "in_weight": noise(arg_keys[12], (D, FF), D ** -0.5, 0.21875, ((1, 4),)),
        "in_bias": noise(arg_keys[13], (FF,), 0.5, 6.0, ((0, 4),), jnp.float32),
        "down_weight": noise(arg_keys[14], (FF, D), FF ** -0.5, 0.109375, ((0, 4),)),
        "down_bias": noise(arg_keys[15], (D,), 0.5, 6.0, (), jnp.float32),
        "norm2_gain": jnp.clip(1.0 + 0.1 * jax.random.normal(arg_keys[16], (D,), jnp.float32), 0.5, 1.5),
        "norm2_shift": noise(arg_keys[17], (D,), 0.3, 4.0, (), jnp.float32),
        "cotangent": noise(arg_keys[18], (MB, TOKENS, D), 1.0, 6.0, ((1, 8),)),
    }


EPSILON = 1e-12
PRECISE = lax.Precision.HIGHEST

@jax.custom_vjp
def low(v):
    return lax.optimization_barrier(v.astype(jnp.bfloat16)).astype(jnp.float32)

@jax.custom_vjp
def low_back(v):
    return v

def low_keep(v):
    return (low(v), None)

def low_pass(kept, grad):
    return (grad,)

def back_keep(v):
    return (v, None)

def back_low(kept, grad):
    return (low(grad),)
low.defvjp(low_keep, low_pass)
low_back.defvjp(back_keep, back_low)

def precise_dot(left, right):
    return jnp.dot(left, right, precision=PRECISE, preferred_element_type=jnp.float32)

def normalize(values_in, gain, shift):
    row_mean = lax.optimization_barrier(jnp.mean(values_in, axis=-1, keepdims=True))
    centred = values_in - row_mean
    variance = lax.optimization_barrier(jnp.mean(centred * centred, axis=-1, keepdims=True))
    return centred * lax.rsqrt(variance + EPSILON) * gain + shift

def segment_of(slot_lengths):
    ends_at = jnp.cumsum(slot_lengths).astype(jnp.int32)
    places = jnp.arange(slot_lengths.shape[0], dtype=jnp.int32)
    return lax.optimization_barrier(jnp.sum((ends_at[None, :] <= places[:, None]).astype(jnp.int32), axis=1)).astype(jnp.int32)

def layer_block(params, block_tokens, segment, head_live, unit_live):
    query_weight, query_bias, key_weight, value_weight, value_bias, out_weight, out_bias, norm1_gain, norm1_shift, in_weight, in_bias, down_weight, down_bias, norm2_gain, norm2_shift = params
    row_count = block_tokens.shape[0]
    queries = low(low_back(precise_dot(block_tokens, query_weight) + query_bias)).reshape(row_count, HEADS, HEAD_DIM)
    key_heads = low(low_back(precise_dot(block_tokens, key_weight))).reshape(row_count, HEADS, HEAD_DIM)
    value_heads = low(low_back(precise_dot(block_tokens, value_weight) + value_bias)).reshape(row_count, HEADS, HEAD_DIM)
    scores = low_back(jnp.einsum('qhd,khd->hqk', queries, key_heads, precision=PRECISE) * 0.125)
    scores = jnp.where((segment[:, None] == segment[None, :])[None], scores, -1e+30)
    shifted = jnp.exp(scores - lax.optimization_barrier(jnp.max(scores, axis=-1, keepdims=True)))
    weights = low(shifted / lax.optimization_barrier(jnp.sum(shifted, axis=-1, keepdims=True)))
    context = jnp.einsum('hqk,khd->qhd', weights, value_heads, precision=PRECISE)
    context = low(low_back(context * head_live[None, :, None])).reshape(row_count, HEADS * HEAD_DIM)
    attended = low_back(precise_dot(context, out_weight))
    hidden = normalize(block_tokens + attended + out_bias, norm1_gain, norm1_shift)
    pre_act = low_back(precise_dot(low(hidden), in_weight) + in_bias)
    active = low(jax.nn.gelu(pre_act, approximate=False) * unit_live)
    mixed = low_back(precise_dot(active, down_weight))
    return normalize(hidden + mixed + down_bias, norm2_gain, norm2_shift)

def forward(params, tokens_wide, lengths, quarters):
    block_tokens = tokens_wide.reshape(MB * BLOCKS, ROWS, D)
    slot_lengths = lengths.reshape(MB * BLOCKS, ROWS)
    block_quarter = jnp.repeat(quarters, BLOCKS)
    head_ids = jnp.arange(HEADS, dtype=jnp.int32)
    unit_ids = jnp.arange(FF, dtype=jnp.int32)
    checked = jax.checkpoint(layer_block)

    def one_block(carry_in, item):
        these_tokens, these_lengths, quarter = item
        head_live = (4 * head_ids < HEADS * quarter).astype(jnp.float32)
        unit_live = (4 * unit_ids < FF * quarter).astype(jnp.float32)
        return (carry_in, checked(params, these_tokens, segment_of(these_lengths), head_live, unit_live))
    carry_out, block_outs = lax.scan(one_block, jnp.zeros((), jnp.float32), (block_tokens, slot_lengths, block_quarter))
    return block_outs.reshape(MB, TOKENS, D)

def reference(tokens, lengths, quarters, query_weight, query_bias, key_weight, value_weight, value_bias, out_weight, out_bias, norm1_gain, norm1_shift, in_weight, in_bias, down_weight, down_bias, norm2_gain, norm2_shift, cotangent):
    params = (query_weight.astype(jnp.float32), query_bias.astype(jnp.float32), key_weight.astype(jnp.float32), value_weight.astype(jnp.float32), value_bias.astype(jnp.float32), out_weight.astype(jnp.float32), out_bias.astype(jnp.float32), norm1_gain.astype(jnp.float32), norm1_shift.astype(jnp.float32), in_weight.astype(jnp.float32), in_bias.astype(jnp.float32), down_weight.astype(jnp.float32), down_bias.astype(jnp.float32), norm2_gain.astype(jnp.float32), norm2_shift.astype(jnp.float32))
    tokens_wide = tokens.astype(jnp.float32)

    def run_layer(layer_params, layer_input):
        return forward(layer_params, layer_input, lengths, quarters)
    layer_output, pull_back = jax.vjp(run_layer, params, tokens_wide)
    param_grads, token_grads = pull_back(cotangent.astype(jnp.float32))
    return (layer_output.astype(jnp.bfloat16), token_grads, param_grads[0], param_grads[1], param_grads[2], param_grads[3], param_grads[4], param_grads[5], param_grads[6], param_grads[7], param_grads[8], param_grads[9], param_grads[10], param_grads[11], param_grads[12], param_grads[13], param_grads[14])
```

```python
import functools

import jax
import jax.numpy as jnp
from jax import lax
from jax.experimental import pallas as pl
from jax.experimental.pallas import tpu as pltpu
from jax.sharding import PartitionSpec as P

HEADS = 12
HEAD_DIM = 64
FF = 3072
EPSILON = 1e-12
ROOT_HALF = 0.7071067811865476
DENSITY_SCALE = 0.3989422804014327
QB = 256
WIDE = 256


BF = jnp.bfloat16
F32 = jnp.float32


def core_swap(value):
    return lax.ppermute(value, "tensor", [(0, 1), (1, 0), (2, 3), (3, 2)])


def chip_swap(value):
    return lax.ppermute(value, "tensor", [(0, 2), (2, 0), (1, 3), (3, 1)])


def batch_swap(value, bit):
    size = lax.axis_size("batch")
    return lax.ppermute(value, "batch", [(i, i ^ (1 << bit)) for i in range(size)])


def sum_rows(partial):
    far = core_swap(partial[3])
    near = core_swap(partial[1])
    far_sum = (partial[2].astype(F32) + far.astype(F32)).astype(BF)
    crossed = chip_swap(far_sum)
    return partial[0].astype(F32) + near.astype(F32) + crossed.astype(F32)


def gather_rows(own):
    crossed = chip_swap(own)
    near = core_swap(own)
    far = core_swap(crossed)
    return (own, near, crossed, far)


def batch_sum(value, order):
    place = lax.axis_index("batch")
    part = value
    for bit in order:
        mine = (place >> bit) & 1
        half = part.shape[0] // 2
        keep = lax.dynamic_slice_in_dim(part, mine * half, half, 0)
        give = lax.dynamic_slice_in_dim(part, (1 - mine) * half, half, 0)
        got = batch_swap(give.astype(BF), bit)
        part = keep + got.astype(F32)
    own = part.astype(BF)
    for bit in reversed(order):
        mine = (place >> bit) & 1
        got = batch_swap(own, bit)
        own = jnp.where(
            mine == 0, jnp.concatenate([own, got]), jnp.concatenate([got, own])
        )
    return own.astype(F32)


def small_sum(value, over_tensor):
    size = lax.axis_size("batch")
    bit = 0
    while (1 << bit) < size:
        value = value + batch_swap(value, bit)
        bit += 1
    if over_tensor:
        value = value + core_swap(value)
        value = value + chip_swap(value)
    return value


def layer_norm(values_in, gain, shift):
    row_mean = jnp.mean(values_in, axis=-1, keepdims=True)
    centred = values_in - row_mean
    inverse = lax.rsqrt(jnp.mean(centred * centred, axis=-1, keepdims=True) + EPSILON)
    normed = centred * inverse
    return (normed * gain + shift, normed, inverse)


def norm_back(grad_in, normed, inverse, gain):
    spread = grad_in * gain
    return inverse * (
        spread
        - jnp.mean(spread, axis=-1, keepdims=True)
        - normed * jnp.mean(spread * normed, axis=-1, keepdims=True)
    )


def gelu_slope(values_in):
    return (
        0.5 * (1.0 + lax.erf(values_in * ROOT_HALF))
        + values_in * jnp.exp(-0.5 * values_in * values_in) * DENSITY_SCALE
    )


def segment_of(slot_lengths):
    ends_at = jnp.cumsum(slot_lengths)
    places = jnp.arange(slot_lengths.shape[0], dtype=jnp.int32)
    return jnp.sum((ends_at[None, :] <= places[:, None]).astype(jnp.int32), axis=1)


def cross_dot(left, right):
    return lax.dot_general(left, right, (((0,), (0,)), ((), ())), preferred_element_type=F32)


def back_dot(left, right):
    return lax.dot_general(left, right, (((1,), (1,)), ((), ())), preferred_element_type=F32)


def lane_half(tile, which):
    lane = lax.broadcasted_iota(jnp.int32, tile.shape, 1)
    return jnp.where((lane >= HEAD_DIM) == (which == 1), tile, jnp.zeros_like(tile))


def attend_kernel(
    place, live, tokens, weight, bias, seg_col, seg_row, out_weight,
    qkv, log_total, context, partial, value_t
):
    step = pl.program_id(0)
    rows_all = tokens.shape[0]

    @pl.when(step == 0)
    def _():
        def project(index, carry):
            rows = pl.ds(pl.multiple_of(index * QB, QB), QB)
            qkv[rows, :] = (
                jnp.dot(tokens[rows, :], weight[...], preferred_element_type=F32) + bias[...]
            ).astype(BF)
            value_t[:, rows] = jnp.transpose(qkv[rows, 2 * WIDE : 3 * WIDE])
            return carry

        lax.fori_loop(0, rows_all // QB, project, 0)

    rows = pl.ds(pl.multiple_of(step * QB, QB), QB)
    same = seg_col[...] == seg_row[:, rows]
    outs = []
    logs = []
    for head in range(3):
        tile = head // 2
        query = qkv[rows, 128 * tile : 128 * tile + 128] * jnp.asarray(0.125, BF)
        query = lane_half(query, head % 2)
        keys = qkv[:, WIDE + 128 * tile : WIDE + 128 * tile + 128]
        scores = jnp.where(same, back_dot(keys, query), -1e30)
        top = jnp.max(scores, axis=0, keepdims=True)
        expo = jnp.exp(scores - top)
        total = jnp.sum(expo, axis=0, keepdims=True)
        probs = (expo * (1.0 / total)).astype(BF)
        outs.append(
            jnp.dot(
                value_t[64 * head : 64 * head + 64, :], probs, preferred_element_type=F32
            )
        )
        logs.append(top + jnp.log(total))
    context_t = jnp.concatenate(outs, axis=0) * live[0].astype(F32)
    low = jnp.transpose(context_t).astype(BF)
    context[...] = low
    log_total[...] = jnp.concatenate(logs + [jnp.zeros((5, QB), F32)], axis=0)
    partial[0] = jnp.dot(low, out_weight[...], preferred_element_type=F32).astype(BF)


def attend(place, live, tokens, weight, bias, seg_col, seg_row, out_weight):
    rows, width = tokens.shape
    full = lambda shape: pl.BlockSpec(shape, lambda i, *_: (0,) * len(shape))
    return pl.pallas_call(
        attend_kernel,
        grid_spec=pltpu.PrefetchScalarGridSpec(
            num_scalar_prefetch=2,
            grid=(rows // QB,),
            in_specs=[
                full((rows, width)),
                full(weight.shape),
                full(bias.shape),
                full((rows, 1)),
                full((1, rows)),
                full(out_weight.shape),
            ],
            out_specs=[
                full((rows, 3 * WIDE)),
                pl.BlockSpec((8, QB), lambda i, *_: (0, i)),
                pl.BlockSpec((QB, 192), lambda i, *_: (i, 0)),
                pl.BlockSpec((1, QB, width), lambda i, p, l: (i ^ p[0], 0, 0)),
            ],
            scratch_shapes=[pltpu.VMEM((WIDE, rows), BF)],
        ),
        out_shape=[
            jax.ShapeDtypeStruct((rows, 3 * WIDE), BF),
            jax.ShapeDtypeStruct((8, rows), F32),
            jax.ShapeDtypeStruct((rows, 192), BF),
            jax.ShapeDtypeStruct((rows // QB, QB, width), BF),
        ],
        compiler_params=pltpu.CompilerParams(
            dimension_semantics=("arbitrary",), vmem_limit_bytes=48 << 20
        ),
        cost_estimate=pl.CostEstimate(
            flops=8_000_000_000, bytes_accessed=8_000_000, transcendentals=3_000_000
        ),
        name="attend",
    )(place, live, tokens, weight, bias, seg_col, seg_row, out_weight)


def attend_back_kernel(
    live, qkv, seg_col, seg_row, log_total, grad_mid, out_weight, grads, key_t, key_acc, value_acc
):
    step = pl.program_id(0)
    last = pl.num_programs(0) - 1
    rows = pl.ds(pl.multiple_of(step * QB, QB), QB)

    @pl.when(step == 0)
    def _():
        key_t[...] = jnp.transpose(qkv[:, WIDE : 2 * WIDE])
        key_acc[...] = jnp.zeros_like(key_acc)
        value_acc[...] = jnp.zeros_like(value_acc)

    grad_context = back_dot(grad_mid[...], out_weight[...]).astype(BF) * live[0].astype(BF)
    same = seg_col[...] == seg_row[:, rows]
    query_parts = []
    for head in range(3):
        tile = head // 2
        lanes = slice(128 * tile, 128 * tile + 128)
        query = qkv[rows, lanes] * jnp.asarray(0.125, BF)
        query = lane_half(query, head % 2)
        grad_tile = lane_half(grad_context[:, lanes], head % 2)
        keys = qkv[:, WIDE + 128 * tile : WIDE + 128 * tile + 128]
        values = qkv[:, 2 * WIDE + 128 * tile : 2 * WIDE + 128 * tile + 128]
        scores = jnp.where(same, back_dot(keys, query), -1e30)
        probs = jnp.exp(scores - log_total[head : head + 1, :])
        grad_probs = back_dot(values, grad_tile)
        mean = jnp.sum(probs * grad_probs, axis=0, keepdims=True)
        grad_scores = (probs * (grad_probs - mean)).astype(BF)
        value_acc[:, lanes] += jnp.dot(probs.astype(BF), grad_tile, preferred_element_type=F32)
        key_acc[:, lanes] += jnp.dot(grad_scores, query, preferred_element_type=F32)
        query_parts.append(
            jnp.dot(
                key_t[64 * head : 64 * head + 64, :], grad_scores, preferred_element_type=F32
            )
        )
    query_t = jnp.concatenate(query_parts + [jnp.zeros((64, QB), F32)], axis=0) * 0.125
    grads[rows, 0:WIDE] = jnp.transpose(query_t).astype(BF)

    @pl.when(step == last)
    def _():
        grads[:, WIDE : 2 * WIDE] = key_acc[...].astype(BF)
        grads[:, 2 * WIDE : 3 * WIDE] = value_acc[...].astype(BF)


def attend_back(live, qkv, seg_col, seg_row, log_total, grad_mid, out_weight):
    rows, width = grad_mid.shape
    full = lambda shape: pl.BlockSpec(shape, lambda i, *_: (0,) * len(shape))
    return pl.pallas_call(
        attend_back_kernel,
        grid_spec=pltpu.PrefetchScalarGridSpec(
            num_scalar_prefetch=1,
            grid=(rows // QB,),
            in_specs=[
                full((rows, 3 * WIDE)),
                full((rows, 1)),
                full((1, rows)),
                pl.BlockSpec((8, QB), lambda i, *_: (0, i)),
                pl.BlockSpec((QB, width), lambda i, *_: (i, 0)),
                full(out_weight.shape),
            ],
            out_specs=full((rows, 3 * WIDE)),
            scratch_shapes=[
                pltpu.VMEM((WIDE, rows), BF),
                pltpu.VMEM((rows, WIDE), F32),
                pltpu.VMEM((rows, WIDE), F32),
            ],
        ),
        out_shape=jax.ShapeDtypeStruct((rows, 3 * WIDE), BF),
        compiler_params=pltpu.CompilerParams(
            dimension_semantics=("arbitrary",), vmem_limit_bytes=48 << 20
        ),
        cost_estimate=pl.CostEstimate(
            flops=8_000_000_000, bytes_accessed=8_000_000, transcendentals=3_000_000
        ),
        name="attend_back",
    )(live, qkv, seg_col, seg_row, log_total, grad_mid, out_weight)


def local(
    tokens,
    lengths,
    quarters,
    query_weight,
    query_bias,
    key_weight,
    value_weight,
    value_bias,
    out_weight,
    out_bias,
    norm1_gain,
    norm1_shift,
    in_weight,
    in_bias,
    down_weight,
    down_bias,
    norm2_gain,
    norm2_shift,
    cotangent,
):
    place = lax.axis_index("tensor")
    micro_count, row_count, width = tokens.shape
    share = row_count // 4
    inner = query_weight.shape[1]
    batch_bits = max(lax.axis_size("batch").bit_length() - 1, 0)
    up = tuple(range(batch_bits))
    turned = up[1:] + up[:1]

    def pad(matrix):
        return jnp.pad(matrix, ((0, 0), (0, WIDE - inner)))

    weight_all = jnp.concatenate([pad(query_weight), pad(key_weight), pad(value_weight)], axis=1)
    bias_all = jnp.concatenate(
        [pad(query_bias[None]), jnp.zeros((1, WIDE), F32), pad(value_bias[None])], axis=1
    )
    out_wide = jnp.pad(out_weight, ((0, WIDE - inner), (0, 0)))
    place_arr = place.astype(jnp.int32)[None]
    head_first = place * (inner // HEAD_DIM)
    lives = [
        (4 * head_first < HEADS * quarters[m]).astype(jnp.int32)[None]
        for m in range(micro_count)
    ]
    unit_ids = place * in_weight.shape[1] + jnp.arange(in_weight.shape[1], dtype=jnp.int32)
    unit_lives = [(4 * unit_ids < FF * quarters[m]).astype(F32) for m in range(micro_count)]

    def own(array_in):
        return lax.dynamic_slice_in_dim(array_in, place * share, share, 0)

    micro = range(micro_count)
    segments = [segment_of(lengths[m, 0]) for m in micro]
    seg_cols = [s[:, None] for s in segments]
    seg_rows = [s[None, :] for s in segments]
    saved = [
        attend(
            place_arr, lives[m], tokens[m], weight_all, bias_all, seg_cols[m], seg_rows[m], out_weight
        )
        for m in micro
    ]
    attended = [sum_rows(saved[m][3]) for m in micro]
    hidden = [
        layer_norm(own(tokens[m]).astype(F32) + attended[m] + out_bias, norm1_gain, norm1_shift)
        for m in micro
    ]
    hidden_low = [
        jnp.concatenate(gather_rows(hidden[m][0].astype(BF)), axis=0) for m in micro
    ]
    pre_act = [
        jnp.dot(hidden_low[m], in_weight, preferred_element_type=F32) + in_bias for m in micro
    ]
    active = [
        (jax.nn.gelu(pre_act[m], approximate=False) * unit_lives[m]).astype(BF) for m in micro
    ]
    mixed = [
        sum_rows(
            jnp.dot(active[m], down_weight, preferred_element_type=F32)
            .astype(BF)
            .reshape(4, share, width)
        )
        for m in micro
    ]
    final = [
        layer_norm(hidden[m][0] + mixed[m] + down_bias, norm2_gain, norm2_shift) for m in micro
    ]
    grad_y = [own(cotangent[m]).astype(F32) for m in micro]
    grad_mid2 = [norm_back(grad_y[m], final[m][1], final[m][2], norm2_gain) for m in micro]
    grad_mid2_low = [
        jnp.concatenate(gather_rows(grad_mid2[m].astype(BF)), axis=0) for m in micro
    ]
    grad_pre = [
        (
            back_dot(grad_mid2_low[m], down_weight) * unit_lives[m] * gelu_slope(pre_act[m])
        ).astype(BF)
        for m in micro
    ]
    hidden_part = [
        sum_rows(back_dot(grad_pre[m], in_weight).astype(BF).reshape(4, share, width))
        for m in micro
    ]
    grad_hidden = [grad_mid2[m] + hidden_part[m] for m in micro]
    grad_mid1 = [
        norm_back(grad_hidden[m], hidden[m][1], hidden[m][2], norm1_gain) for m in micro
    ]

    def in_order(slots):
        stacked = jnp.zeros((4, share, width), BF)
        for index, slot in enumerate(slots):
            stacked = lax.dynamic_update_slice(stacked, slot[None], (place ^ index, 0, 0))
        return stacked.reshape(row_count, width)

    grad_mid1_low = [in_order(gather_rows(grad_mid1[m].astype(BF))) for m in micro]
    grads_low = [
        attend_back(
            lives[m], saved[m][0], seg_cols[m], seg_rows[m], saved[m][1], grad_mid1_low[m], out_wide
        )
        for m in micro
    ]

    def slots_of(array_in):
        parts = array_in.reshape(4, share, array_in.shape[1])
        return jnp.concatenate(
            [lax.dynamic_slice_in_dim(parts, place ^ k, 1, 0) for k in range(4)]
        )

    input_part = [
        sum_rows(
            back_dot(slots_of(grads_low[m]).reshape(row_count, 3 * WIDE), weight_all)
            .astype(BF)
            .reshape(4, share, width)
        )
        for m in micro
    ]
    input_grad = [grad_mid1[m] + input_part[m] for m in micro]

    def add(terms):
        total = terms[0]
        for term in terms[1:]:
            total = total + term
        return total

    down_term = add([cross_dot(active[m], grad_mid2_low[m]) for m in micro])
    in_term = add([cross_dot(hidden_low[m], grad_pre[m]) for m in micro])
    out_term = add([cross_dot(saved[m][2], grad_mid1_low[m]) for m in micro])
    qkv_term = add([cross_dot(tokens[m], grads_low[m]) for m in micro])
    shared = jnp.stack(
        [
            add([jnp.sum(grad_mid1[m], axis=0) for m in micro]),
            add([jnp.sum(grad_hidden[m] * hidden[m][1], axis=0) for m in micro]),
            add([jnp.sum(grad_hidden[m], axis=0) for m in micro]),
            add([jnp.sum(grad_mid2[m], axis=0) for m in micro]),
            add([jnp.sum(grad_y[m] * final[m][1], axis=0) for m in micro]),
            add([jnp.sum(grad_y[m], axis=0) for m in micro]),
        ]
    )
    in_bias_term = add([jnp.sum(grad_pre[m].astype(F32), axis=0) for m in micro])
    qkv_bias_term = add([jnp.sum(grads_low[m].astype(F32), axis=0) for m in micro])
    shared = small_sum(shared, True)
    in_bias_sum = small_sum(in_bias_term[None], False)[0]
    qkv_bias_sum = small_sum(qkv_bias_term[None], False)[0]
    down_sum = batch_sum(down_term, up)
    in_sum = batch_sum(in_term, turned)
    out_sum = batch_sum(out_term, up)
    qkv_slim = jnp.concatenate(
        [qkv_term[:, k * WIDE : k * WIDE + inner] for k in range(3)], axis=1
    )
    qkv_sum = batch_sum(qkv_slim, up)
    return (
        jnp.stack([final[m][0].astype(BF) for m in micro]),
        jnp.stack(input_grad),
        qkv_sum[:, :inner],
        qkv_bias_sum[:inner],
        qkv_sum[:, inner : 2 * inner],
        qkv_sum[:, 2 * inner :],
        qkv_bias_sum[2 * WIDE : 2 * WIDE + inner],
        out_sum,
        shared[0],
        shared[1],
        shared[2],
        in_sum,
        in_bias_sum,
        down_sum,
        shared[3],
        shared[4],
        shared[5],
    )


def solution(mesh):
    in_specs = (
        P(None, "batch", None),
        P(None, "batch", None),
        P(),
        P(None, "tensor"),
        P("tensor"),
        P(None, "tensor"),
        P(None, "tensor"),
        P("tensor"),
        P("tensor", None),
        P(),
        P(),
        P(),
        P(None, "tensor"),
        P("tensor"),
        P("tensor", None),
        P(),
        P(),
        P(),
        P(None, "batch", None),
    )
    out_specs = (
        P(None, ("batch", "tensor"), None),
        P(None, ("batch", "tensor"), None),
        P(None, "tensor"),
        P("tensor"),
        P(None, "tensor"),
        P(None, "tensor"),
        P("tensor"),
        P("tensor", None),
        P(),
        P(),
        P(),
        P(None, "tensor"),
        P("tensor"),
        P("tensor", None),
        P(),
        P(),
        P(),
    )
    return jax.shard_map(local, mesh=mesh, in_specs=in_specs, out_specs=out_specs, check_vma=False)
```

```python
import functools

import jax
import jax.numpy as jnp
from jax import lax
from jax.experimental import pallas as pl
from jax.experimental.pallas import tpu as pltpu
from jax.sharding import PartitionSpec as P

HEADS = 12
HEAD_DIM = 64
FF = 3072
EPSILON = 1e-12
ROOT_HALF = 0.7071067811865476
DENSITY_SCALE = 0.3989422804014327
QB = 256
WIDE = 256


BF = jnp.bfloat16
F32 = jnp.float32


def core_swap(value):
    return lax.ppermute(value, "tensor", [(0, 1), (1, 0), (2, 3), (3, 2)])


def chip_swap(value):
    return lax.ppermute(value, "tensor", [(0, 2), (2, 0), (1, 3), (3, 1)])


def batch_swap(value, bit):
    size = lax.axis_size("batch")
    return lax.ppermute(value, "batch", [(i, i ^ (1 << bit)) for i in range(size)])


def sum_rows(partial):
    far = core_swap(partial[3])
    near = core_swap(partial[1])
    far_sum = (partial[2].astype(F32) + far.astype(F32)).astype(BF)
    crossed = chip_swap(far_sum)
    return partial[0].astype(F32) + near.astype(F32) + crossed.astype(F32)


def gather_rows(own):
    crossed = chip_swap(own)
    near = core_swap(own)
    far = core_swap(crossed)
    return (own, near, crossed, far)


def batch_sum(value, order):
    place = lax.axis_index("batch")
    part = value
    for bit in order:
        mine = (place >> bit) & 1
        half = part.shape[0] // 2
        keep = lax.dynamic_slice_in_dim(part, mine * half, half, 0)
        give = lax.dynamic_slice_in_dim(part, (1 - mine) * half, half, 0)
        got = batch_swap(give.astype(BF), bit)
        part = keep + got.astype(F32)
    own = part.astype(BF)
    for bit in reversed(order):
        mine = (place >> bit) & 1
        got = batch_swap(own, bit)
        own = jnp.where(
            mine == 0, jnp.concatenate([own, got]), jnp.concatenate([got, own])
        )
    return own.astype(F32)


def small_sum(value, over_tensor):
    size = lax.axis_size("batch")
    bit = 0
    while (1 << bit) < size:
        value = value + batch_swap(value, bit)
        bit += 1
    if over_tensor:
        value = value + core_swap(value)
        value = value + chip_swap(value)
    return value


def layer_norm(values_in, gain, shift):
    row_mean = jnp.mean(values_in, axis=-1, keepdims=True)
    centred = values_in - row_mean
    inverse = lax.rsqrt(jnp.mean(centred * centred, axis=-1, keepdims=True) + EPSILON)
    normed = centred * inverse
    return (normed * gain + shift, normed, inverse)


def norm_back(grad_in, normed, inverse, gain):
    spread = grad_in * gain
    return inverse * (
        spread
        - jnp.mean(spread, axis=-1, keepdims=True)
        - normed * jnp.mean(spread * normed, axis=-1, keepdims=True)
    )


def gelu_slope(values_in):
    return (
        0.5 * (1.0 + lax.erf(values_in * ROOT_HALF))
        + values_in * jnp.exp(-0.5 * values_in * values_in) * DENSITY_SCALE
    )


def segment_of(slot_lengths):
    ends_at = jnp.cumsum(slot_lengths)
    places = jnp.arange(slot_lengths.shape[0], dtype=jnp.int32)
    return jnp.sum((ends_at[None, :] <= places[:, None]).astype(jnp.int32), axis=1)


def cross_dot(left, right):
    return lax.dot_general(left, right, (((0,), (0,)), ((), ())), preferred_element_type=F32)


def back_dot(left, right):
    return lax.dot_general(left, right, (((1,), (1,)), ((), ())), preferred_element_type=F32)


def lane_half(tile, which):
    lane = lax.broadcasted_iota(jnp.int32, tile.shape, 1)
    return jnp.where((lane >= HEAD_DIM) == (which == 1), tile, jnp.zeros_like(tile))


def attend_kernel(
    place, live, tokens, weight, bias, seg_col, seg_row, out_weight,
    qkv, log_total, context, partial, value_t
):
    step = pl.program_id(0)
    rows_all = tokens.shape[0]

    @pl.when(step == 0)
    def _():
        def project(index, carry):
            rows = pl.ds(pl.multiple_of(index * QB, QB), QB)
            qkv[rows, :] = (
                jnp.dot(tokens[rows, :], weight[...], preferred_element_type=F32) + bias[...]
            ).astype(BF)
            value_t[:, rows] = jnp.transpose(qkv[rows, 2 * WIDE : 3 * WIDE])
            return carry

        lax.fori_loop(0, rows_all // QB, project, 0)

    rows = pl.ds(pl.multiple_of(step * QB, QB), QB)
    same = seg_col[...] == seg_row[:, rows]
    outs = []
    logs = []
    for head in range(3):
        tile = head // 2
        query = qkv[rows, 128 * tile : 128 * tile + 128] * jnp.asarray(0.125, BF)
        query = lane_half(query, head % 2)
        keys = qkv[:, WIDE + 128 * tile : WIDE + 128 * tile + 128]
        scores = jnp.where(same, back_dot(keys, query), -1e30)
        top = jnp.max(scores, axis=0, keepdims=True)
        expo = jnp.exp(scores - top)
        total = jnp.sum(expo, axis=0, keepdims=True)
        probs = (expo * (1.0 / total)).astype(BF)
        outs.append(
            jnp.dot(
                value_t[64 * head : 64 * head + 64, :], probs, preferred_element_type=F32
            )
        )
        logs.append(top + jnp.log(total))
    context_t = jnp.concatenate(outs, axis=0) * live[0].astype(F32)
    low = jnp.transpose(context_t).astype(BF)
    context[...] = low
    log_total[...] = jnp.concatenate(logs + [jnp.zeros((5, QB), F32)], axis=0)
    partial[...] = jnp.dot(low, out_weight[...], preferred_element_type=F32).astype(BF)


def attend(place, live, tokens, weight, bias, seg_col, seg_row, out_weight):
    rows, width = tokens.shape
    full = lambda shape: pl.BlockSpec(shape, lambda i, *_: (0,) * len(shape))
    return pl.pallas_call(
        attend_kernel,
        grid_spec=pltpu.PrefetchScalarGridSpec(
            num_scalar_prefetch=2,
            grid=(rows // QB,),
            in_specs=[
                full((rows, width)),
                full(weight.shape),
                full(bias.shape),
                full((rows, 1)),
                full((1, rows)),
                full(out_weight.shape),
            ],
            out_specs=[
                full((rows, 3 * WIDE)),
                pl.BlockSpec((8, QB), lambda i, *_: (0, i)),
                pl.BlockSpec((QB, 192), lambda i, *_: (i, 0)),
                pl.BlockSpec((QB, width), lambda i, p, l: (i ^ p[0], 0)),
            ],
            scratch_shapes=[pltpu.VMEM((WIDE, rows), BF)],
        ),
        out_shape=[
            jax.ShapeDtypeStruct((rows, 3 * WIDE), BF),
            jax.ShapeDtypeStruct((8, rows), F32),
            jax.ShapeDtypeStruct((rows, 192), BF),
            jax.ShapeDtypeStruct((rows, width), BF),
        ],
        compiler_params=pltpu.CompilerParams(
            dimension_semantics=("arbitrary",), vmem_limit_bytes=48 << 20
        ),
        cost_estimate=pl.CostEstimate(
            flops=8_000_000_000, bytes_accessed=8_000_000, transcendentals=3_000_000
        ),
        name="attend",
    )(place, live, tokens, weight, bias, seg_col, seg_row, out_weight)


def attend_back_kernel(
    live, qkv, seg_col, seg_row, log_total, grad_mid, out_weight, grads, key_t, key_acc, value_acc
):
    step = pl.program_id(0)
    last = pl.num_programs(0) - 1
    rows = pl.ds(pl.multiple_of(step * QB, QB), QB)

    @pl.when(step == 0)
    def _():
        key_t[...] = jnp.transpose(qkv[:, WIDE : 2 * WIDE])
        key_acc[...] = jnp.zeros_like(key_acc)
        value_acc[...] = jnp.zeros_like(value_acc)

    grad_context = back_dot(grad_mid[...], out_weight[...]).astype(BF) * live[0].astype(BF)
    same = seg_col[...] == seg_row[:, rows]
    query_parts = []
    for head in range(3):
        tile = head // 2
        lanes = slice(128 * tile, 128 * tile + 128)
        query = qkv[rows, lanes] * jnp.asarray(0.125, BF)
        query = lane_half(query, head % 2)
        grad_tile = lane_half(grad_context[:, lanes], head % 2)
        keys = qkv[:, WIDE + 128 * tile : WIDE + 128 * tile + 128]
        values = qkv[:, 2 * WIDE + 128 * tile : 2 * WIDE + 128 * tile + 128]
        scores = jnp.where(same, back_dot(keys, query), -1e30)
        probs = jnp.exp(scores - log_total[head : head + 1, :])
        grad_probs = back_dot(values, grad_tile)
        mean = jnp.sum(probs * grad_probs, axis=0, keepdims=True)
        grad_scores = (probs * (grad_probs - mean)).astype(BF)
        value_acc[:, lanes] += jnp.dot(probs.astype(BF), grad_tile, preferred_element_type=F32)
        key_acc[:, lanes] += jnp.dot(grad_scores, query, preferred_element_type=F32)
        query_parts.append(
            jnp.dot(
                key_t[64 * head : 64 * head + 64, :], grad_scores, preferred_element_type=F32
            )
        )
    query_t = jnp.concatenate(query_parts + [jnp.zeros((64, QB), F32)], axis=0) * 0.125
    grads[rows, 0:WIDE] = jnp.transpose(query_t).astype(BF)

    @pl.when(step == last)
    def _():
        grads[:, WIDE : 2 * WIDE] = key_acc[...].astype(BF)
        grads[:, 2 * WIDE : 3 * WIDE] = value_acc[...].astype(BF)


def attend_back(live, qkv, seg_col, seg_row, log_total, grad_mid, out_weight):
    rows, width = grad_mid.shape
    full = lambda shape: pl.BlockSpec(shape, lambda i, *_: (0,) * len(shape))
    return pl.pallas_call(
        attend_back_kernel,
        grid_spec=pltpu.PrefetchScalarGridSpec(
            num_scalar_prefetch=1,
            grid=(rows // QB,),
            in_specs=[
                full((rows, 3 * WIDE)),
                full((rows, 1)),
                full((1, rows)),
                pl.BlockSpec((8, QB), lambda i, *_: (0, i)),
                pl.BlockSpec((QB, width), lambda i, *_: (i, 0)),
                full(out_weight.shape),
            ],
            out_specs=full((rows, 3 * WIDE)),
            scratch_shapes=[
                pltpu.VMEM((WIDE, rows), BF),
                pltpu.VMEM((rows, WIDE), F32),
                pltpu.VMEM((rows, WIDE), F32),
            ],
        ),
        out_shape=jax.ShapeDtypeStruct((rows, 3 * WIDE), BF),
        compiler_params=pltpu.CompilerParams(
            dimension_semantics=("arbitrary",), vmem_limit_bytes=48 << 20
        ),
        cost_estimate=pl.CostEstimate(
            flops=8_000_000_000, bytes_accessed=8_000_000, transcendentals=3_000_000
        ),
        name="attend_back",
    )(live, qkv, seg_col, seg_row, log_total, grad_mid, out_weight)


def shuffle_kernel(
    live, part_a, part_b, token_rows, cot_rows, in_weight, down_weight, vectors,
    grad_low, result, grad_mid1, in_term, down_term, in_bias_term, shared,
    far, near, cross, sums, hid, gm2, act, slope, gpre, pbuf,
    hidden_rows, normed_rows, inverse_rows, mid2_rows, send_sem, recv_sem,
):
    place = lax.axis_index("tensor")
    core_id = {"tensor": place ^ 1}
    chip_id = {"tensor": place ^ 2}
    share = token_rows.shape[1]

    def slot(buf, micro, index):
        start = (micro * 4 + index) * share
        if not isinstance(start, int):
            start = pl.multiple_of(start, share)
        return buf.at[pl.ds(start, share), :]

    def landing(buf, micro, phase):
        start = (micro * 3 + phase) * share
        if not isinstance(start, int):
            start = pl.multiple_of(start, share)
        return buf.at[pl.ds(start, share), :]

    def copy(src, dst, micro, phase, kind, target):
        index = (micro * 3 + phase) * 6 + kind
        return pltpu.make_async_remote_copy(
            src_ref=src,
            dst_ref=dst,
            send_sem=send_sem.at[index],
            recv_sem=recv_sem.at[index],
            device_id=target,
            device_id_type=pl.DeviceIdType.MESH,
        )

    def far_copy(parts, micro, phase):
        return copy(parts(micro, 3), landing(far, micro, phase), micro, phase, 0, core_id)

    def near_copy(parts, micro, phase):
        return copy(parts(micro, 1), landing(near, micro, phase), micro, phase, 1, core_id)

    def cross_copy(micro, phase):
        return copy(
            landing(sums, micro, phase), landing(cross, micro, phase), micro, phase, 2, chip_id
        )

    def crossing_copy(buf, micro, phase):
        return copy(slot(buf, micro, 0), slot(buf, micro, 2), micro, phase, 3, chip_id)

    def beside_copy(buf, micro, phase):
        return copy(slot(buf, micro, 0), slot(buf, micro, 1), micro, phase, 4, core_id)

    def onward_copy(buf, micro, phase):
        return copy(slot(buf, micro, 2), slot(buf, micro, 3), micro, phase, 5, core_id)

    def scatter_start(parts, micro, phase):
        far_copy(parts, micro, phase).start()
        near_copy(parts, micro, phase).start()

    def scatter_mid(parts, micro, phase):
        far_copy(parts, micro, phase).wait_recv()
        landing(sums, micro, phase)[...] = (
            parts(micro, 2)[...].astype(F32) + landing(far, micro, phase)[...].astype(F32)
        ).astype(BF)
        cross_copy(micro, phase).start()

    def scatter_end(parts, micro, phase):
        near_copy(parts, micro, phase).wait_recv()
        cross_copy(micro, phase).wait_recv()
        return (
            parts(micro, 0)[...].astype(F32)
            + landing(near, micro, phase)[...].astype(F32)
            + landing(cross, micro, phase)[...].astype(F32)
        )

    def gather_start(buf, micro, phase):
        crossing_copy(buf, micro, phase).start()
        beside_copy(buf, micro, phase).start()

    def gather_pass(buf, micro, phase):
        crossing_copy(buf, micro, phase).wait_recv()
        onward_copy(buf, micro, phase).start()

    def gather_end(buf, micro, phase):
        onward_copy(buf, micro, phase).wait_recv()

    def vector(index):
        return vectors[index : index + 1, :]

    def tally(index, value):
        shared[index : index + 1, :] += jnp.sum(value, axis=0, keepdims=True)

    def own_rows(buf, micro):
        start = pl.multiple_of(micro * share, share)
        return buf.at[pl.ds(start, share), :]

    barrier = pltpu.get_barrier_semaphore()
    for target in (core_id, chip_id):
        pl.semaphore_signal(
            barrier, inc=1, device_id=target, device_id_type=pl.DeviceIdType.MESH
        )
    shared[...] = jnp.zeros_like(shared)
    in_bias_term[...] = jnp.zeros_like(in_bias_term)
    pl.semaphore_wait(barrier, 2)

    inputs = (part_a, part_b)

    def first_parts(micro, index):
        return inputs[micro].at[index * share : (index + 1) * share, :]

    def later_parts(micro, index):
        return slot(pbuf, micro, index)

    for micro in range(2):
        scatter_start(first_parts, micro, 0)
    for micro in range(2):
        scatter_mid(first_parts, micro, 0)

    for micro in range(2):
        total = scatter_end(first_parts, micro, 0)
        hidden, normed, inverse = layer_norm(
            token_rows[micro].astype(F32) + total + vector(0), vector(1), vector(2)
        )
        own_rows(hidden_rows, micro)[...] = hidden
        own_rows(normed_rows, micro)[...] = normed
        own_rows(inverse_rows, micro)[...] = jnp.broadcast_to(inverse, (share, 128))
        slot(hid, micro, 0)[...] = hidden.astype(BF)
        gather_start(hid, micro, 0)

    def forward(index, carry):
        micro, which = index // 4, index % 4

        @pl.when(which == 1)
        def _():
            beside_copy(hid, micro, 0).wait_recv()

        @pl.when(which == 2)
        def _():
            gather_pass(hid, micro, 0)

        @pl.when(which == 3)
        def _():
            gather_end(hid, micro, 0)

        pre = (
            jnp.dot(slot(hid, micro, which)[...], in_weight[...], preferred_element_type=F32)
            + vector(3)
        )
        alive = live[micro].astype(F32)
        below = 0.5 * (1.0 + lax.erf(pre * ROOT_HALF)) * alive
        low = (pre * below).astype(BF)
        slot(act, micro, which)[...] = low
        slot(slope, micro, which)[...] = below + pre * jnp.exp(-0.5 * pre * pre) * (
            DENSITY_SCALE * alive
        )
        slot(pbuf, micro, which)[...] = jnp.dot(
            low, down_weight[...], preferred_element_type=F32
        ).astype(BF)

        @pl.when(which == 3)
        def _():
            scatter_start(later_parts, micro, 1)

        @pl.when(index == 4)
        def _():
            scatter_mid(later_parts, 0, 1)

        return carry

    lax.fori_loop(0, 8, forward, 0)
    scatter_mid(later_parts, 1, 1)

    def middle(micro, carry):
        total = scatter_end(later_parts, micro, 1)
        final, normed, inverse = layer_norm(
            own_rows(hidden_rows, micro)[...] + total + vector(4), vector(5), vector(6)
        )
        result[micro] = final.astype(BF)
        grad_y = cot_rows[micro].astype(F32)
        grad_mid2 = norm_back(grad_y, normed, inverse, vector(5))
        own_rows(mid2_rows, micro)[...] = grad_mid2
        slot(gm2, micro, 0)[...] = grad_mid2.astype(BF)
        gather_start(gm2, micro, 1)
        tally(3, grad_mid2)
        tally(4, grad_y * normed)
        tally(5, grad_y)
        return carry

    lax.fori_loop(0, 2, middle, 0)
    for micro in range(2):
        for phase in (1,):
            far_copy(later_parts, micro, phase).wait_send()
            near_copy(later_parts, micro, phase).wait_send()

    def backward(index, carry):
        micro, which = index // 4, index % 4

        @pl.when(which == 1)
        def _():
            beside_copy(gm2, micro, 1).wait_recv()

        @pl.when(which == 2)
        def _():
            gather_pass(gm2, micro, 1)

        @pl.when(which == 3)
        def _():
            gather_end(gm2, micro, 1)

        grad_pre = (
            back_dot(slot(gm2, micro, which)[...], down_weight[...])
            * slot(slope, micro, which)[...]
        ).astype(BF)
        slot(gpre, micro, which)[...] = grad_pre
        in_bias_term[...] += jnp.sum(grad_pre.astype(F32), axis=0, keepdims=True)
        slot(pbuf, micro, which)[...] = back_dot(grad_pre, in_weight[...]).astype(BF)

        @pl.when(which == 3)
        def _():
            scatter_start(later_parts, micro, 2)

        @pl.when(index == 4)
        def _():
            scatter_mid(later_parts, 0, 2)

        return carry

    lax.fori_loop(0, 8, backward, 0)
    scatter_mid(later_parts, 1, 2)

    def closing(micro, carry):
        total = scatter_end(later_parts, micro, 2)
        grad_hidden = own_rows(mid2_rows, micro)[...] + total
        normed = own_rows(normed_rows, micro)[...]
        inverse = own_rows(inverse_rows, micro)[:, 0:1]
        grad = norm_back(grad_hidden, normed, inverse, vector(1))
        grad_mid1[micro] = grad
        slot(grad_low, micro, 0)[...] = grad.astype(BF)
        gather_start(grad_low, micro, 2)
        tally(0, grad)
        tally(1, grad_hidden * normed)
        tally(2, grad_hidden)
        return carry

    lax.fori_loop(0, 2, closing, 0)

    def weigh(left, right, out):
        def block(index, carry):
            lanes = pl.ds(pl.multiple_of(index * 256, 256), 256)
            out[lanes, :] = cross_dot(left[:, lanes], right[...])
            return carry

        lax.fori_loop(0, out.shape[0] // 256, block, 0)

    weigh(act, gm2, down_term)
    gather_pass(grad_low, 0, 2)
    weigh(hid, gpre, in_term)
    gather_pass(grad_low, 1, 2)
    for micro in range(2):
        beside_copy(grad_low, micro, 2).wait_recv()
        gather_end(grad_low, micro, 2)
    for micro in range(2):
        for phase in range(3):
            parts = first_parts if phase == 0 else later_parts
            if phase != 1:
                far_copy(parts, micro, phase).wait_send()
                near_copy(parts, micro, phase).wait_send()
            cross_copy(micro, phase).wait_send()
            buf = (hid, gm2, grad_low)[phase]
            crossing_copy(buf, micro, phase).wait_send()
            beside_copy(buf, micro, phase).wait_send()
            onward_copy(buf, micro, phase).wait_send()


def shuffle(live, part_a, part_b, token_rows, cot_rows, in_weight, down_weight, vectors):
    micro_count, share, width = token_rows.shape
    units = in_weight.shape[1]
    rows = 8 * share
    vm = lambda: pl.BlockSpec(memory_space=pltpu.VMEM)
    return pl.pallas_call(
        shuffle_kernel,
        in_specs=[pl.BlockSpec(memory_space=pltpu.SMEM)] + [vm() for _ in range(7)],
        out_specs=[vm() for _ in range(7)],
        out_shape=[
            jax.ShapeDtypeStruct((rows, width), BF),
            jax.ShapeDtypeStruct((2, share, width), BF),
            jax.ShapeDtypeStruct((2, share, width), F32),
            jax.ShapeDtypeStruct((width, units), F32),
            jax.ShapeDtypeStruct((units, width), F32),
            jax.ShapeDtypeStruct((1, units), F32),
            jax.ShapeDtypeStruct((8, width), F32),
        ],
        scratch_shapes=[
            pltpu.VMEM((6 * share, width), BF),
            pltpu.VMEM((6 * share, width), BF),
            pltpu.VMEM((6 * share, width), BF),
            pltpu.VMEM((6 * share, width), BF),
            pltpu.VMEM((rows, width), BF),
            pltpu.VMEM((rows, width), BF),
            pltpu.VMEM((rows, units), BF),
            pltpu.VMEM((rows, units), F32),
            pltpu.VMEM((rows, units), BF),
            pltpu.VMEM((rows, width), BF),
            pltpu.VMEM((2 * share, width), F32),
            pltpu.VMEM((2 * share, width), F32),
            pltpu.VMEM((2 * share, 128), F32),
            pltpu.VMEM((2 * share, width), F32),
            pltpu.SemaphoreType.DMA((36,)),
            pltpu.SemaphoreType.DMA((36,)),
        ],
        compiler_params=pltpu.CompilerParams(
            collective_id=1, has_side_effects=True, vmem_limit_bytes=67_000_000
        ),
        name="shuffle",
    )(live, part_a, part_b, token_rows, cot_rows, in_weight, down_weight, vectors)


def local(
    tokens,
    lengths,
    quarters,
    query_weight,
    query_bias,
    key_weight,
    value_weight,
    value_bias,
    out_weight,
    out_bias,
    norm1_gain,
    norm1_shift,
    in_weight,
    in_bias,
    down_weight,
    down_bias,
    norm2_gain,
    norm2_shift,
    cotangent,
):
    place = lax.axis_index("tensor")
    micro_count, row_count, width = tokens.shape
    share = row_count // 4
    inner = query_weight.shape[1]
    batch_bits = max(lax.axis_size("batch").bit_length() - 1, 0)
    up = tuple(range(batch_bits))
    turned = up[1:] + up[:1]

    def pad(matrix):
        return jnp.pad(matrix, ((0, 0), (0, WIDE - inner)))

    weight_all = jnp.concatenate([pad(query_weight), pad(key_weight), pad(value_weight)], axis=1)
    bias_all = jnp.concatenate(
        [pad(query_bias[None]), jnp.zeros((1, WIDE), F32), pad(value_bias[None])], axis=1
    )
    out_wide = jnp.pad(out_weight, ((0, WIDE - inner), (0, 0)))
    place_arr = place.astype(jnp.int32)[None]
    head_first = place * (inner // HEAD_DIM)
    lives = [
        (4 * head_first < HEADS * quarters[m]).astype(jnp.int32)[None]
        for m in range(micro_count)
    ]
    unit_ids = place * in_weight.shape[1] + jnp.arange(in_weight.shape[1], dtype=jnp.int32)
    unit_lives = [(4 * unit_ids < FF * quarters[m]).astype(F32) for m in range(micro_count)]

    def own(array_in):
        return lax.dynamic_slice_in_dim(array_in, place * share, share, 0)

    micro = range(micro_count)
    segments = [segment_of(lengths[m, 0]) for m in micro]
    seg_cols = [s[:, None] for s in segments]
    seg_rows = [s[None, :] for s in segments]
    saved = [
        attend(
            place_arr, lives[m], tokens[m], weight_all, bias_all, seg_cols[m], seg_rows[m], out_weight
        )
        for m in micro
    ]
    vectors = jnp.stack(
        [out_bias, norm1_gain, norm1_shift, in_bias, down_bias, norm2_gain, norm2_shift, out_bias]
    )
    own_tokens = lax.dynamic_slice_in_dim(tokens, place * share, share, 1)
    own_cots = lax.dynamic_slice_in_dim(cotangent, place * share, share, 1)
    grad_slots, result, grad_mid1, in_term, down_term, in_bias_term, shared = shuffle(
        jnp.concatenate(lives),
        saved[0][3],
        saved[1][3],
        own_tokens,
        own_cots,
        in_weight,
        down_weight,
        vectors,
    )
    grad_slots = grad_slots.reshape(micro_count, 4, share, width)
    grad_mid1_low = [
        jnp.concatenate(
            [lax.dynamic_slice_in_dim(grad_slots[m], place ^ k, 1, 0)[0] for k in range(4)]
        )
        for m in micro
    ]
    grads_low = [
        attend_back(
            lives[m], saved[m][0], seg_cols[m], seg_rows[m], saved[m][1], grad_mid1_low[m], out_wide
        )
        for m in micro
    ]

    def slots_of(array_in):
        parts = array_in.reshape(4, share, array_in.shape[1])
        return jnp.concatenate(
            [lax.dynamic_slice_in_dim(parts, place ^ k, 1, 0) for k in range(4)]
        )

    input_part = [
        sum_rows(
            back_dot(slots_of(grads_low[m]).reshape(row_count, 3 * WIDE), weight_all)
            .astype(BF)
            .reshape(4, share, width)
        )
        for m in micro
    ]
    input_grad = [grad_mid1[m] + input_part[m] for m in micro]

    def add(terms):
        total = terms[0]
        for term in terms[1:]:
            total = total + term
        return total

    out_term = add([cross_dot(saved[m][2], grad_mid1_low[m]) for m in micro])
    qkv_term = add([cross_dot(tokens[m], grads_low[m]) for m in micro])
    qkv_bias_term = add([jnp.sum(grads_low[m].astype(F32), axis=0) for m in micro])
    shared = small_sum(shared, True)
    in_bias_sum = small_sum(in_bias_term, False)[0]
    qkv_bias_sum = small_sum(qkv_bias_term[None], False)[0]
    down_sum = batch_sum(down_term, up)
    in_sum = batch_sum(in_term, turned)
    out_sum = batch_sum(out_term, up)
    qkv_slim = jnp.concatenate(
        [qkv_term[:, k * WIDE : k * WIDE + inner] for k in range(3)], axis=1
    )
    qkv_sum = batch_sum(qkv_slim, up)
    return (
        result,
        jnp.stack(input_grad),
        qkv_sum[:, :inner],
        qkv_bias_sum[:inner],
        qkv_sum[:, inner : 2 * inner],
        qkv_sum[:, 2 * inner :],
        qkv_bias_sum[2 * WIDE : 2 * WIDE + inner],
        out_sum,
        shared[0],
        shared[1],
        shared[2],
        in_sum,
        in_bias_sum,
        down_sum,
        shared[3],
        shared[4],
        shared[5],
    )


def solution(mesh):
    in_specs = (
        P(None, "batch", None),
        P(None, "batch", None),
        P(),
        P(None, "tensor"),
        P("tensor"),
        P(None, "tensor"),
        P(None, "tensor"),
        P("tensor"),
        P("tensor", None),
        P(),
        P(),
        P(),
        P(None, "tensor"),
        P("tensor"),
        P("tensor", None),
        P(),
        P(),
        P(),
        P(None, "batch", None),
    )
    out_specs = (
        P(None, ("batch", "tensor"), None),
        P(None, ("batch", "tensor"), None),
        P(None, "tensor"),
        P("tensor"),
        P(None, "tensor"),
        P(None, "tensor"),
        P("tensor"),
        P("tensor", None),
        P(),
        P(),
        P(),
        P(None, "tensor"),
        P("tensor"),
        P("tensor", None),
        P(),
        P(),
        P(),
    )
    return jax.shard_map(local, mesh=mesh, in_specs=in_specs, out_specs=out_specs, check_vma=False)
```

```python
import functools

import jax
import jax.numpy as jnp
from jax import lax
from jax.experimental import pallas as pl
from jax.experimental.pallas import tpu as pltpu
from jax.sharding import PartitionSpec as P

HEADS = 12
HEAD_DIM = 64
FF = 3072
EPSILON = 1e-12
ROOT_HALF = 0.7071067811865476
DENSITY_SCALE = 0.3989422804014327
QB = 256
WIDE = 256

BF = jnp.bfloat16
F32 = jnp.float32
MESH = pl.DeviceIdType.MESH


def layer_norm(values_in, gain, shift):
    row_mean = jnp.mean(values_in, axis=-1, keepdims=True)
    centred = values_in - row_mean
    inverse = lax.rsqrt(jnp.mean(centred * centred, axis=-1, keepdims=True) + EPSILON)
    normed = centred * inverse
    return (normed * gain + shift, normed, inverse)


def norm_back(grad_in, normed, inverse, gain):
    spread = grad_in * gain
    return inverse * (
        spread
        - jnp.mean(spread, axis=-1, keepdims=True)
        - normed * jnp.mean(spread * normed, axis=-1, keepdims=True)
    )


def cross_dot(left, right):
    return lax.dot_general(left, right, (((0,), (0,)), ((), ())), preferred_element_type=F32)


def back_dot(left, right):
    return lax.dot_general(left, right, (((1,), (1,)), ((), ())), preferred_element_type=F32)


def lane_half(tile, which):
    lane = lax.broadcasted_iota(jnp.int32, tile.shape, 1)
    return jnp.where((lane >= HEAD_DIM) == (which == 1), tile, jnp.zeros_like(tile))


def tile_lanes(kind, tile):
    start = 128 * kind + 384 * tile
    return slice(start, start + 128)


def column_of(row):
    return jnp.transpose(jnp.broadcast_to(row, (8, row.shape[1])))[:, 0:1]


def attend_kernel(
    place, live, tokens, lengths, query_weight, key_weight, value_weight, query_bias,
    value_bias, out_weight,
    qkv, log_total, context, partial, segment, weight,
    value_t, bias, seg_col,
):
    micro, step = pl.program_id(0), pl.program_id(1)
    rows_all = tokens.shape[1]

    @pl.when((micro == 0) & (step == 0))
    def _():
        bias[...] = jnp.zeros_like(bias)
        for kind, ref in enumerate((query_weight, key_weight, value_weight)):
            weight[:, 128 * kind : 128 * kind + 128] = ref[:, 0:128]
            weight[:, 384 + 128 * kind : 448 + 128 * kind] = ref[:, 128:192]
            weight[:, 448 + 128 * kind : 512 + 128 * kind] = jnp.zeros_like(ref[:, 128:192])
        for kind, ref in ((0, query_bias), (2, value_bias)):
            bias[0:1, 128 * kind : 128 * kind + 128] = ref[0:1, 0:128]
            bias[0:1, 384 + 128 * kind : 448 + 128 * kind] = ref[0:1, 128:192]

    @pl.when(step == 0)
    def _():
        def project(index, carry):
            rows = pl.ds(pl.multiple_of(index * QB, QB), QB)
            qkv[rows, :] = (
                jnp.dot(tokens[0, rows, :], weight[...], preferred_element_type=F32)
                + bias[0:1, :]
            ).astype(BF)
            for tile in range(2):
                value_t[128 * tile : 128 * tile + 128, rows] = jnp.transpose(
                    qkv[rows, tile_lanes(2, tile)]
                )
            return carry

        lax.fori_loop(0, rows_all // QB, project, 0)
        ends = jnp.broadcast_to(lengths[0], (8, rows_all))
        lane = lax.broadcasted_iota(jnp.int32, (8, rows_all), 1)
        shift = 1
        while shift < rows_all:
            ends = ends + jnp.where(lane >= shift, pltpu.roll(ends, shift, 1), 0)
            shift *= 2
        ends_col = column_of(ends[0:1, :].astype(F32))
        places = lax.broadcasted_iota(jnp.int32, (rows_all, rows_all), 1).astype(F32)
        count = jnp.sum(jnp.where(ends_col <= places, 1.0, 0.0), axis=0, keepdims=True)
        segment[...] = jnp.broadcast_to(count, (8, rows_all))
        seg_col[...] = column_of(count)

    rows = pl.ds(pl.multiple_of(step * QB, QB), QB)
    same = seg_col[...] == segment[0:1, rows]
    outs = []
    logs = []
    for head in range(3):
        tile = head // 2
        query = qkv[rows, tile_lanes(0, tile)] * jnp.asarray(0.125, BF)
        query = lane_half(query, head % 2)
        keys = qkv[:, tile_lanes(1, tile)]
        scores = jnp.where(same, back_dot(keys, query), -1e30)
        top = jnp.max(scores, axis=0, keepdims=True)
        expo = jnp.exp(scores - top)
        total = jnp.sum(expo, axis=0, keepdims=True)
        probs = (expo * (1.0 / total)).astype(BF)
        outs.append(
            jnp.dot(
                value_t[64 * head : 64 * head + 64, :], probs, preferred_element_type=F32
            )
        )
        logs.append(top + jnp.log(total))
    context_t = jnp.concatenate(outs, axis=0) * live[micro].astype(F32)
    low = jnp.transpose(context_t).astype(BF)
    context[...] = low
    log_total[...] = jnp.concatenate(logs + [jnp.zeros((5, QB), F32)], axis=0)
    partial[...] = jnp.dot(low, out_weight[...], preferred_element_type=F32).astype(BF)


def attend(
    place, live, tokens, lengths, query_weight, key_weight, value_weight, query_bias,
    value_bias, out_weight,
):
    micro_count, rows, width = tokens.shape
    steps = rows // QB
    full = lambda array: pl.BlockSpec(array.shape, lambda m, i, *_: (0,) * array.ndim)
    return pl.pallas_call(
        attend_kernel,
        grid_spec=pltpu.PrefetchScalarGridSpec(
            num_scalar_prefetch=2,
            grid=(micro_count, steps),
            in_specs=[
                pl.BlockSpec((1, rows, width), lambda m, i, *_: (m, 0, 0)),
                pl.BlockSpec((1, 1, rows), lambda m, i, *_: (m, 0, 0)),
                full(query_weight),
                full(key_weight),
                full(value_weight),
                full(query_bias),
                full(value_bias),
                full(out_weight),
            ],
            out_specs=[
                pl.BlockSpec((rows, 3 * WIDE), lambda m, i, *_: (m, 0)),
                pl.BlockSpec((8, QB), lambda m, i, *_: (m, i)),
                pl.BlockSpec((QB, 192), lambda m, i, *_: (m * steps + i, 0)),
                pl.BlockSpec((QB, width), lambda m, i, p, l: (m * steps + (i ^ p[0]), 0)),
                pl.BlockSpec((8, rows), lambda m, i, *_: (m, 0)),
                pl.BlockSpec((width, 3 * WIDE), lambda m, i, *_: (0, 0)),
            ],
            scratch_shapes=[
                pltpu.VMEM((WIDE, rows), BF),
                pltpu.VMEM((8, 3 * WIDE), F32),
                pltpu.VMEM((rows, 1), F32),
            ],
        ),
        out_shape=[
            jax.ShapeDtypeStruct((micro_count * rows, 3 * WIDE), BF),
            jax.ShapeDtypeStruct((micro_count * 8, rows), F32),
            jax.ShapeDtypeStruct((micro_count * rows, 192), BF),
            jax.ShapeDtypeStruct((micro_count * rows, width), BF),
            jax.ShapeDtypeStruct((micro_count * 8, rows), F32),
            jax.ShapeDtypeStruct((width, 3 * WIDE), BF),
        ],
        compiler_params=pltpu.CompilerParams(
            dimension_semantics=("arbitrary", "arbitrary"), vmem_limit_bytes=48 << 20
        ),
        name="attend",
    )(
        place, live, tokens, lengths, query_weight, key_weight, value_weight, query_bias,
        value_bias, out_weight,
    )


CHUNK = 48


def by_chunks(count, body):
    def one(index, carry):
        body(pl.multiple_of(index * CHUNK, CHUNK))
        return carry

    lax.fori_loop(0, count // CHUNK, one, 0)


def reduce_plan(rows, order):
    plan = []
    length, offset = rows, 0
    for bit in order:
        halving = length % (2 * CHUNK) == 0
        if halving:
            length //= 2
        plan.append((bit, halving, length, offset))
        offset += length
    return plan, offset


class BatchSum:
    def __init__(self, term, first, rows, columns, order, give, take, whole, sems, base):
        self.term, self.first, self.rows, self.columns = term, first, rows, columns
        self.give, self.take, self.whole = give, take, whole
        self.send_sem, self.recv_sem = sems
        self.base = base
        self.plan, _ = reduce_plan(rows, order)
        self.place = lax.axis_index("batch")
        self.starts = [0]
        for bit, halving, length, _ in self.plan:
            start = self.starts[-1]
            if halving:
                start = start + ((self.place >> bit) & 1) * length
            self.starts.append(start)

    def rows_at(self, ref, start, length, lift=0):
        return ref.at[pl.ds(pl.multiple_of(start + lift, CHUNK), length), 0 : self.columns]

    def copy(self, src, dst, index, bit):
        return pltpu.make_async_remote_copy(
            src_ref=src,
            dst_ref=dst,
            send_sem=self.send_sem.at[self.base + index],
            recv_sem=self.recv_sem.at[self.base + index],
            device_id={"batch": self.place ^ (1 << bit)},
            device_id_type=MESH,
        )

    def reduce_copy(self, step):
        bit, _, length, offset = self.plan[step]
        return self.copy(
            self.rows_at(self.give, offset, length),
            self.rows_at(self.take, offset, length),
            step,
            bit,
        )

    def reduce_start(self, step):
        bit, halving, length, offset = self.plan[step]
        start = self.starts[step]
        if halving:
            start = start + (1 - ((self.place >> bit) & 1)) * length

        def pack(at):
            self.rows_at(self.give, offset + at, CHUNK)[...] = self.rows_at(
                self.term, start + at, CHUNK, self.first
            )[...].astype(BF)

        by_chunks(length, pack)
        self.reduce_copy(step).start()

    def reduce_finish(self, step):
        _, halving, length, offset = self.plan[step]
        self.reduce_copy(step).wait_recv()
        start = self.starts[step + 1]

        def merge(at):
            mine = self.rows_at(self.term, start + at, CHUNK, self.first)
            got = self.rows_at(self.take, offset + at, CHUNK)[...].astype(F32)
            if halving:
                mine[...] = mine[...] + got
            else:
                mine[...] = self.rows_at(self.give, offset + at, CHUNK)[...].astype(F32) + got

        by_chunks(length, merge)

    def settle(self):
        length, start = self.plan[-1][2], self.starts[-1]

        def pack(at):
            self.rows_at(self.whole, start + at, CHUNK)[...] = self.rows_at(
                self.term, start + at, CHUNK, self.first
            )[...].astype(BF)

        by_chunks(length, pack)

    def gather_copy(self, step):
        bit, _, length, _ = self.plan[step]
        region = self.rows_at(self.whole, self.starts[step + 1], length)
        return self.copy(region, region, len(self.plan) + step, bit)

    def gather_start(self, step):
        if self.plan[step][1]:
            self.gather_copy(step).start()

    def gather_finish(self, step):
        if self.plan[step][1]:
            self.gather_copy(step).wait_recv()

    def advance(self, index):
        count = len(self.plan)
        if index == 0:
            self.reduce_start(0)
        elif index < count:
            self.reduce_finish(index - 1)
            self.reduce_start(index)
        elif index == count:
            self.reduce_finish(count - 1)
            self.settle()
            self.gather_start(count - 1)
        elif index < 2 * count:
            self.gather_finish(2 * count - index)
            self.gather_start(2 * count - index - 1)
        else:
            self.gather_finish(0)

            def widen(at):
                self.rows_at(self.term, at, CHUNK, self.first)[...] = self.rows_at(
                    self.whole, at, CHUNK
                )[...].astype(F32)

            by_chunks(self.rows, widen)

    def drain(self):
        for step in range(len(self.plan)):
            self.reduce_copy(step).wait_send()
            if self.plan[step][1]:
                self.gather_copy(step).wait_send()


class VectorSum:
    def __init__(self, values, take, targets, sems, base):
        self.values, self.take, self.targets = values, take, targets
        self.send_sem, self.recv_sem = sems
        self.base = base

    def at(self, ref, step):
        return ref.at[8 * step : 8 * step + 8, :]

    def copy(self, step):
        return pltpu.make_async_remote_copy(
            src_ref=self.at(self.values, step),
            dst_ref=self.at(self.take, step),
            send_sem=self.send_sem.at[self.base + step],
            recv_sem=self.recv_sem.at[self.base + step],
            device_id=self.targets[step],
            device_id_type=MESH,
        )

    def advance(self, index):
        if index > 0:
            self.copy(index - 1).wait_recv()
            self.at(self.values, index)[...] = (
                self.at(self.values, index - 1)[...] + self.at(self.take, index - 1)[...]
            )
        if index < len(self.targets):
            self.copy(index).start()

    def drain(self):
        for step in range(len(self.targets)):
            self.copy(step).wait_send()


def layer_kernel(
    live, partials, token_hbm, cot_hbm, qkv_hbm, in_weight, down_weight, weight_all, out_weight,
    context, log_total, segment, vectors,
    result, input_grad, in_term, down_term, qkv_term, out_term, sums_out, bias_out,
    far, near, cross, sums, hid, gm2, act, slope, gpre, pbuf, grad_low,
    hidden_rows, normed_rows, inverse_rows, key_t, key_acc, value_acc, seg_col, out_wide,
    down_take, down_whole, in_take, in_whole, low_take, low_whole, high_take, high_whole,
    out_take, out_whole, vec_values, vec_take, bias_values, bias_take,
    send_sem, recv_sem, batch_send, batch_recv, load_sem,
):
    place = lax.axis_index("tensor")
    batch_place = lax.axis_index("batch")
    batch_bits = lax.axis_size("batch").bit_length() - 1
    core_id = {"tensor": place ^ 1}
    chip_id = {"tensor": place ^ 2}
    share = input_grad.shape[1]
    rows_all = 4 * share

    def slot(buf, micro, index):
        start = (micro * 4 + index) * share
        if not isinstance(start, int):
            start = pl.multiple_of(start, share)
        return buf.at[pl.ds(start, share), :]

    def own_rows(buf, micro):
        start = micro * share
        if not isinstance(start, int):
            start = pl.multiple_of(start, share)
        return buf.at[pl.ds(start, share), :]

    def copy(src, dst, micro, phase, kind, target):
        index = (micro * 4 + phase) * 6 + kind
        return pltpu.make_async_remote_copy(
            src_ref=src,
            dst_ref=dst,
            send_sem=send_sem.at[index],
            recv_sem=recv_sem.at[index],
            device_id=target,
            device_id_type=MESH,
        )

    def far_copy(parts, micro, phase):
        return copy(slot(parts, micro, 3), own_rows(far, micro), micro, phase, 0, core_id)

    def near_copy(parts, micro, phase):
        return copy(slot(parts, micro, 1), own_rows(near, micro), micro, phase, 1, core_id)

    def cross_copy(micro, phase):
        return copy(own_rows(sums, micro), own_rows(cross, micro), micro, phase, 2, chip_id)

    def crossing_copy(buf, micro, phase):
        return copy(slot(buf, micro, 0), slot(buf, micro, 2), micro, phase, 3, chip_id)

    def beside_copy(buf, micro, phase):
        return copy(slot(buf, micro, 0), slot(buf, micro, 1), micro, phase, 4, core_id)

    def onward_copy(buf, micro, phase):
        return copy(slot(buf, micro, 2), slot(buf, micro, 3), micro, phase, 5, core_id)

    def scatter_start(parts, micro, phase):
        far_copy(parts, micro, phase).start()
        near_copy(parts, micro, phase).start()

    def scatter_mid(parts, micro, phase):
        far_copy(parts, micro, phase).wait_recv()
        own_rows(sums, micro)[...] = (
            slot(parts, micro, 2)[...].astype(F32) + own_rows(far, micro)[...].astype(F32)
        ).astype(BF)
        cross_copy(micro, phase).start()

    def scatter_end(parts, micro, phase):
        near_copy(parts, micro, phase).wait_recv()
        cross_copy(micro, phase).wait_recv()
        cross_copy(micro, phase).wait_send()
        return (
            slot(parts, micro, 0)[...].astype(F32)
            + own_rows(near, micro)[...].astype(F32)
            + own_rows(cross, micro)[...].astype(F32)
        )

    def scatter_drain(parts, micro, phase):
        far_copy(parts, micro, phase).wait_send()
        near_copy(parts, micro, phase).wait_send()

    def gather_start(buf, micro, phase):
        crossing_copy(buf, micro, phase).start()
        beside_copy(buf, micro, phase).start()

    def gather_step(buf, micro, phase, which):
        @pl.when(which == 1)
        def _():
            beside_copy(buf, micro, phase).wait_recv()

        @pl.when(which == 2)
        def _():
            crossing_copy(buf, micro, phase).wait_recv()
            onward_copy(buf, micro, phase).start()

        @pl.when(which == 3)
        def _():
            onward_copy(buf, micro, phase).wait_recv()

    def gather_drain(buf, micro, phase):
        crossing_copy(buf, micro, phase).wait_send()
        beside_copy(buf, micro, phase).wait_send()
        onward_copy(buf, micro, phase).wait_send()

    def vector(index):
        return vectors[index : index + 1, :]

    def tally(index, value):
        vec_values[index : index + 1, :] += jnp.sum(value, axis=0, keepdims=True)

    def load_rows(hbm, target, micro, index):
        start = pl.multiple_of(place * share, share)
        return pltpu.make_async_copy(
            hbm.at[micro, pl.ds(start, share), :], target, load_sem.at[index]
        )

    token_loads = [load_rows(token_hbm, slot(grad_low, m, 0), m, m) for m in range(2)]
    cot_loads = [load_rows(cot_hbm, result.at[m], m, 2 + m) for m in range(2)]
    for load in token_loads + cot_loads:
        load.start()

    sems = (batch_send, batch_recv)
    up = tuple(range(batch_bits))
    turned = up[1:] + up[:1]
    stride = 2 * batch_bits

    def carve(buf, sizes):
        start = 0
        views = []
        for size in sizes:
            views.append(buf.at[start : start + size, :])
            start += size
        return views

    down_give, in_give, out_give = carve(
        slope, (down_take.shape[0], in_take.shape[0], out_take.shape[0])
    )
    low_give, high_give = carve(hid, (low_take.shape[0], high_take.shape[0]))
    down_sum = BatchSum(
        down_term, 0, 768, 768, up, down_give, down_take, down_whole, sems, 0
    )
    in_sum = BatchSum(in_term, 0, 768, 768, turned, in_give, in_take, in_whole, sems, stride)
    low_sum = BatchSum(
        qkv_term, 0, 384, 640, up, low_give, low_take, low_whole, sems, 2 * stride
    )
    high_sum = BatchSum(
        qkv_term, 384, 384, 640, turned, high_give, high_take, high_whole, sems, 3 * stride
    )
    out_sum = BatchSum(
        out_term, 0, 192, 768, turned, out_give, out_take, out_whole, sems, 4 * stride
    )
    batch_targets = [{"batch": batch_place ^ (1 << bit)} for bit in up]
    shared_sum = VectorSum(
        vec_values, vec_take, batch_targets + [core_id, chip_id], sems, 5 * stride
    )
    bias_sum = VectorSum(bias_values, bias_take, batch_targets, sems, 6 * stride + 2)

    barrier = pltpu.get_barrier_semaphore()
    partners = [core_id, chip_id] + batch_targets
    for target in partners:
        pl.semaphore_signal(barrier, inc=1, device_id=target, device_id_type=MESH)
    vec_values[0:8, :] = jnp.zeros((8, vec_values.shape[1]), F32)
    bias_values[0:8, :] = jnp.zeros((8, bias_values.shape[1]), F32)
    out_term[...] = jnp.zeros_like(out_term)
    out_wide[0:192, :] = out_weight[...]
    out_wide[192:256, :] = jnp.zeros((64, out_wide.shape[1]), BF)
    pl.semaphore_wait(barrier, len(partners))

    for micro in range(2):
        scatter_start(partials, micro, 0)
    for micro in range(2):
        scatter_mid(partials, micro, 0)
    for load in token_loads + cot_loads:
        load.wait()

    def opening(micro, carry):
        total = scatter_end(partials, micro, 0)
        hidden, normed, inverse = layer_norm(
            slot(grad_low, micro, 0)[...].astype(F32) + total + vector(0), vector(1), vector(2)
        )
        own_rows(hidden_rows, micro)[...] = hidden
        own_rows(normed_rows, micro)[...] = normed
        own_rows(inverse_rows, micro)[...] = jnp.broadcast_to(inverse, (share, 128))
        slot(hid, micro, 0)[...] = hidden.astype(BF)
        gather_start(hid, micro, 0)
        return carry

    lax.fori_loop(0, 2, opening, 0)

    def forward(index, carry):
        micro, which = index // 4, index % 4
        gather_step(hid, micro, 0, which)
        pre = (
            jnp.dot(slot(hid, micro, which)[...], in_weight[...], preferred_element_type=F32)
            + vector(3)
        )
        alive = live[micro].astype(F32)
        below = 0.5 * (1.0 + lax.erf(pre * ROOT_HALF)) * alive
        low = (pre * below).astype(BF)
        slot(act, micro, which)[...] = low
        slot(slope, micro, which)[...] = (
            below + pre * jnp.exp(-0.5 * pre * pre) * (DENSITY_SCALE * alive)
        ).astype(BF)
        slot(pbuf, micro, which)[...] = jnp.dot(
            low, down_weight[...], preferred_element_type=F32
        ).astype(BF)

        @pl.when(which == 3)
        def _():
            scatter_start(pbuf, micro, 1)

        @pl.when(index == 4)
        def _():
            scatter_mid(pbuf, 0, 1)

        return carry

    lax.fori_loop(0, 8, forward, 0)
    scatter_mid(pbuf, 1, 1)

    def middle(micro, carry):
        total = scatter_end(pbuf, micro, 1)
        final, normed, inverse = layer_norm(
            own_rows(hidden_rows, micro)[...] + total + vector(4), vector(5), vector(6)
        )
        grad_y = result[micro].astype(F32)
        result[micro] = final.astype(BF)
        grad_mid2 = norm_back(grad_y, normed, inverse, vector(5))
        own_rows(hidden_rows, micro)[...] = grad_mid2
        slot(gm2, micro, 0)[...] = grad_mid2.astype(BF)
        gather_start(gm2, micro, 1)
        tally(3, grad_mid2)
        tally(4, grad_y * normed)
        tally(5, grad_y)
        return carry

    lax.fori_loop(0, 2, middle, 0)
    for micro in range(2):
        scatter_drain(pbuf, micro, 1)

    def backward(index, carry):
        micro, which = index // 4, index % 4
        gather_step(gm2, micro, 1, which)
        grad_pre = (
            back_dot(slot(gm2, micro, which)[...], down_weight[...])
            * slot(slope, micro, which)[...].astype(F32)
        ).astype(BF)
        slot(gpre, micro, which)[...] = grad_pre
        tally(6, grad_pre.astype(F32))
        slot(pbuf, micro, which)[...] = back_dot(grad_pre, in_weight[...]).astype(BF)

        @pl.when(which == 3)
        def _():
            scatter_start(pbuf, micro, 2)

        @pl.when(index == 4)
        def _():
            scatter_mid(pbuf, 0, 2)

        return carry

    lax.fori_loop(0, 8, backward, 0)
    scatter_mid(pbuf, 1, 2)

    def weigh(left, right, out):
        def block(index, carry):
            lanes = pl.ds(pl.multiple_of(index * 256, 256), 256)
            out[lanes, :] = cross_dot(left[:, lanes], right[...])
            return carry

        lax.fori_loop(0, out.shape[0] // 256, block, 0)

    weigh(act, gm2, down_term)
    down_sum.advance(0)
    for micro in range(2):
        gather_drain(hid, micro, 0)
        gather_drain(gm2, micro, 1)
    token_all = [
        pltpu.make_async_copy(
            token_hbm.at[m], act.at[pl.ds(m * rows_all, rows_all), :], load_sem.at[4 + m]
        )
        for m in range(2)
    ]
    qkv_all = pltpu.make_async_copy(qkv_hbm, gm2, load_sem.at[6])
    for load in token_all:
        load.start()
    qkv_all.start()
    weigh(hid, gpre, in_term)
    in_sum.advance(0)

    def closing(micro, carry):
        total = scatter_end(pbuf, micro, 2)
        grad_hidden = own_rows(hidden_rows, micro)[...] + total
        normed = own_rows(normed_rows, micro)[...]
        inverse = own_rows(inverse_rows, micro)[:, 0:1]
        grad = norm_back(grad_hidden, normed, inverse, vector(1))
        input_grad[micro] = grad
        slot(grad_low, micro, 0)[...] = grad.astype(BF)
        gather_start(grad_low, micro, 2)
        tally(0, grad)
        tally(1, grad_hidden * normed)
        tally(2, grad_hidden)
        return carry

    lax.fori_loop(0, 2, closing, 0)
    for micro in range(2):
        scatter_drain(pbuf, micro, 2)
    shared_sum.advance(0)
    for load in token_all:
        load.wait()
    qkv_all.wait()
    qkv, tokens, grads = gm2, act, gpre

    def micro_rows(micro):
        return pl.ds(pl.multiple_of(micro * rows_all, rows_all), rows_all)

    def finish_micro(micro):
        block = micro_rows(micro)
        for tile in range(2):
            lanes = slice(128 * tile, 128 * tile + 128)
            grads[block, tile_lanes(1, tile)] = key_acc[:, lanes].astype(BF)
            grads[block, tile_lanes(2, tile)] = value_acc[:, lanes].astype(BF)
        bias_values[0:1, :] += jnp.sum(grads[block, :].astype(F32), axis=0, keepdims=True)

        def send_slot(index, carry):
            start = pl.multiple_of(micro * rows_all + (index ^ place) * share, share)
            slot(pbuf, micro, index)[...] = back_dot(
                grads[pl.ds(start, share), :], weight_all[...]
            ).astype(BF)
            return carry

        lax.fori_loop(0, 4, send_slot, 0)
        scatter_start(pbuf, micro, 3)

    def attend_back(index, carry):
        micro, which = index // 4, index % 4
        gather_step(grad_low, micro, 2, which)
        step = which ^ place
        block = micro_rows(micro)
        rows = pl.ds(pl.multiple_of(micro * rows_all + step * share, share), share)

        @pl.when(which == 0)
        def _():
            for tile in range(2):
                key_t[128 * tile : 128 * tile + 128, :] = jnp.transpose(
                    qkv[block, tile_lanes(1, tile)]
                )
            key_acc[...] = jnp.zeros_like(key_acc)
            value_acc[...] = jnp.zeros_like(value_acc)
            seg_col[...] = column_of(
                segment[pl.ds(pl.multiple_of(micro * 8, 8), 8), :][0:1, :]
            )

        eight = pl.ds(pl.multiple_of(micro * 8, 8), 8)
        columns = pl.ds(pl.multiple_of(step * share, share), share)
        seg_row = segment[eight, columns][0:1, :]
        logs = log_total[eight, columns]
        grad_slot = slot(grad_low, micro, which)[...]
        out_term[...] += cross_dot(context[rows, :], grad_slot)

        @pl.when(index == 7)
        def _():
            out_sum.advance(0)

        alive = live[micro].astype(BF)
        grad_context = back_dot(grad_slot, out_wide[...]).astype(BF) * alive
        same = seg_col[...] == seg_row
        query_parts = []
        for head in range(3):
            tile = head // 2
            lanes = slice(128 * tile, 128 * tile + 128)
            query = qkv[rows, tile_lanes(0, tile)] * jnp.asarray(0.125, BF)
            query = lane_half(query, head % 2)
            grad_tile = lane_half(grad_context[:, lanes], head % 2)
            keys = qkv[block, tile_lanes(1, tile)]
            values = qkv[block, tile_lanes(2, tile)]
            scores = jnp.where(same, back_dot(keys, query), -1e30)
            probs = jnp.exp(scores - logs[head : head + 1, :])
            grad_probs = back_dot(values, grad_tile)
            mean = jnp.sum(probs * grad_probs, axis=0, keepdims=True)
            grad_scores = (probs * (grad_probs - mean)).astype(BF)
            value_acc[:, lanes] += jnp.dot(
                probs.astype(BF), grad_tile, preferred_element_type=F32
            )
            key_acc[:, lanes] += jnp.dot(grad_scores, query, preferred_element_type=F32)
            query_parts.append(
                jnp.dot(
                    key_t[64 * head : 64 * head + 64, :],
                    grad_scores,
                    preferred_element_type=F32,
                )
            )
        query_t = jnp.concatenate(query_parts + [jnp.zeros((64, share), F32)], axis=0) * 0.125
        query_grad = jnp.transpose(query_t).astype(BF)
        for tile in range(2):
            grads[rows, tile_lanes(0, tile)] = query_grad[:, 128 * tile : 128 * tile + 128]

        @pl.when(which == 3)
        def _():
            finish_micro(micro)

        def at(point, *events):
            @pl.when(index == point)
            def _():
                for event in events:
                    event()

        at(0, lambda: shared_sum.advance(1))
        at(1, lambda: down_sum.advance(1), lambda: in_sum.advance(1))
        at(2, lambda: shared_sum.advance(2))
        at(3, lambda: down_sum.advance(2), lambda: in_sum.advance(2))
        at(4, lambda: scatter_mid(pbuf, 0, 3), lambda: down_sum.advance(3))
        at(5, lambda: in_sum.advance(3), lambda: down_sum.advance(4))
        at(6, lambda: in_sum.advance(4), lambda: shared_sum.advance(3))
        return carry

    lax.fori_loop(0, 8, attend_back, 0)

    def weigh_qkv(index, carry):
        lanes = pl.ds(pl.multiple_of(index * 256, 256), 256)
        qkv_term[lanes, :] = cross_dot(tokens[:, lanes], grads[...])
        qkv_term[lanes, 448:512] = qkv_term[lanes, 512:576]
        qkv_term[lanes, 512:640] = qkv_term[lanes, 640:768]
        return carry

    lax.fori_loop(0, 3, weigh_qkv, 0)
    low_sum.advance(0)
    high_sum.advance(0)
    bias_sum.advance(0)
    scatter_mid(pbuf, 1, 3)

    def final_rows(micro):
        input_grad[micro] = input_grad[micro] + scatter_end(pbuf, micro, 3)

    last = 2 * batch_bits
    final_rows(0)
    out_sum.advance(1)
    queue = []
    for step in range(1, last + 1):
        queue.append((low_sum, step))
        queue.append((high_sum, step))
        if step < last:
            queue.append((out_sum, step + 1))
        if 4 + step <= last:
            queue.append((down_sum, 4 + step))
            queue.append((in_sum, 4 + step))
        if 1 <= step <= batch_bits:
            queue.append((bias_sum, step))
        if 3 + step <= batch_bits + 2:
            queue.append((shared_sum, 3 + step))
        if step == 3:
            queue.append((None, step))
    for owner, step in queue:
        if owner is None:
            final_rows(1)
        else:
            owner.advance(step)

    base = 8 * batch_bits
    sums_out[...] = vec_values[base + 16 : base + 24, :]
    sums_out[6:7, :] = vec_values[base + 6 : base + 7, :]
    bias_out[...] = bias_values[base : base + 8, :]
    for micro in range(2):
        scatter_drain(partials, micro, 0)
        scatter_drain(pbuf, micro, 3)
        gather_drain(grad_low, micro, 2)
    for owner in (down_sum, in_sum, low_sum, high_sum, out_sum, shared_sum, bias_sum):
        owner.drain()


def layer_call(
    live, partials, tokens, cotangent, qkv, in_weight, down_weight, weight_all, out_weight,
    context, log_total, segment, vectors,
):
    micro_count, rows_all, width = tokens.shape
    share = rows_all // 4
    rows = micro_count * rows_all
    units = in_weight.shape[1]
    batch_bits = lax.axis_size("batch").bit_length() - 1
    order = tuple(range(batch_bits))
    vmem = pl.BlockSpec(memory_space=pltpu.VMEM)
    hbm = pl.BlockSpec(memory_space=pl.ANY)
    smem = pl.BlockSpec(memory_space=pltpu.SMEM)

    def exchange(count, columns):
        total = reduce_plan(count, order)[1]
        return [pltpu.VMEM((total, columns), BF), pltpu.VMEM((count, columns), BF)]

    batch_sems = 7 * 2 * batch_bits + 2
    return pl.pallas_call(
        layer_kernel,
        in_specs=[smem, vmem, hbm, hbm, hbm] + [vmem] * 8,
        out_specs=[vmem] * 8,
        out_shape=[
            jax.ShapeDtypeStruct((micro_count, share, width), BF),
            jax.ShapeDtypeStruct((micro_count, share, width), F32),
            jax.ShapeDtypeStruct((width, units), F32),
            jax.ShapeDtypeStruct((units, width), F32),
            jax.ShapeDtypeStruct((width, 3 * WIDE), F32),
            jax.ShapeDtypeStruct((192, width), F32),
            jax.ShapeDtypeStruct((8, width), F32),
            jax.ShapeDtypeStruct((8, width), F32),
        ],
        scratch_shapes=[
            pltpu.VMEM((2 * share, width), BF),
            pltpu.VMEM((2 * share, width), BF),
            pltpu.VMEM((2 * share, width), BF),
            pltpu.VMEM((2 * share, width), BF),
            pltpu.VMEM((rows, width), BF),
            pltpu.VMEM((rows, width), BF),
            pltpu.VMEM((rows, units), BF),
            pltpu.VMEM((rows, units), BF),
            pltpu.VMEM((rows, units), BF),
            pltpu.VMEM((rows, width), BF),
            pltpu.VMEM((rows, width), BF),
            pltpu.VMEM((2 * share, width), F32),
            pltpu.VMEM((2 * share, width), F32),
            pltpu.VMEM((2 * share, 128), F32),
            pltpu.VMEM((WIDE, rows_all), BF),
            pltpu.VMEM((rows_all, WIDE), F32),
            pltpu.VMEM((rows_all, WIDE), F32),
            pltpu.VMEM((rows_all, 1), F32),
            pltpu.VMEM((WIDE, width), BF),
        ]
        + exchange(768, 768)
        + exchange(768, 768)
        + exchange(384, 640)
        + exchange(384, 640)
        + exchange(192, 768)
        + [
            pltpu.VMEM((8 * (batch_bits + 3), width), F32),
            pltpu.VMEM((8 * (batch_bits + 2), width), F32),
            pltpu.VMEM((8 * (batch_bits + 1), width), F32),
            pltpu.VMEM((8 * batch_bits, width), F32),
            pltpu.SemaphoreType.DMA((48,)),
            pltpu.SemaphoreType.DMA((48,)),
            pltpu.SemaphoreType.DMA((batch_sems,)),
            pltpu.SemaphoreType.DMA((batch_sems,)),
            pltpu.SemaphoreType.DMA((7,)),
        ],
        compiler_params=pltpu.CompilerParams(
            collective_id=1, has_side_effects=True, vmem_limit_bytes=67_043_328
        ),
        name="layer",
    )(
        live, partials, tokens, cotangent, qkv, in_weight, down_weight, weight_all, out_weight,
        context, log_total, segment, vectors,
    )


def local(
    tokens,
    lengths,
    quarters,
    query_weight,
    query_bias,
    key_weight,
    value_weight,
    value_bias,
    out_weight,
    out_bias,
    norm1_gain,
    norm1_shift,
    in_weight,
    in_bias,
    down_weight,
    down_bias,
    norm2_gain,
    norm2_shift,
    cotangent,
):
    place = lax.axis_index("tensor").astype(jnp.int32)
    live = (4 * place < 4 * quarters).astype(jnp.int32)
    qkv, log_total, context, partials, segment, weight_all = attend(
        place[None],
        live,
        tokens,
        lengths.reshape(lengths.shape[0], 1, lengths.shape[2]),
        query_weight,
        key_weight,
        value_weight,
        query_bias[None],
        value_bias[None],
        out_weight,
    )
    vectors = jnp.stack(
        [out_bias, norm1_gain, norm1_shift, in_bias, down_bias, norm2_gain, norm2_shift, out_bias]
    )
    result, input_grad, in_sum, down_sum, packed, out_sum, sums, bias = layer_call(
        live,
        partials,
        tokens,
        cotangent,
        qkv,
        in_weight,
        down_weight,
        weight_all,
        out_weight,
        context,
        log_total,
        segment,
        vectors,
    )
    query_sum = jnp.concatenate([packed[:, 0:128], packed[:, 384:448]], axis=1)
    key_sum = jnp.concatenate([packed[:, 128:256], packed[:, 448:512]], axis=1)
    value_sum = jnp.concatenate([packed[:, 256:384], packed[:, 512:576]], axis=1)
    query_bias_sum = jnp.concatenate([bias[0, 0:128], bias[0, 384:448]])
    value_bias_sum = jnp.concatenate([bias[0, 256:384], bias[0, 640:704]])
    return (
        result,
        input_grad,
        query_sum,
        query_bias_sum,
        key_sum,
        value_sum,
        value_bias_sum,
        out_sum,
        sums[0],
        sums[1],
        sums[2],
        in_sum,
        sums[6],
        down_sum,
        sums[3],
        sums[4],
        sums[5],
    )


def solution(mesh):
    in_specs = (
        P(None, "batch", None),
        P(None, "batch", None),
        P(),
        P(None, "tensor"),
        P("tensor"),
        P(None, "tensor"),
        P(None, "tensor"),
        P("tensor"),
        P("tensor", None),
        P(),
        P(),
        P(),
        P(None, "tensor"),
        P("tensor"),
        P("tensor", None),
        P(),
        P(),
        P(),
        P(None, "batch", None),
    )
    out_specs = (
        P(None, ("batch", "tensor"), None),
        P(None, ("batch", "tensor"), None),
        P(None, "tensor"),
        P("tensor"),
        P(None, "tensor"),
        P(None, "tensor"),
        P("tensor"),
        P("tensor", None),
        P(),
        P(),
        P(),
        P(None, "tensor"),
        P("tensor"),
        P("tensor", None),
        P(),
        P(),
        P(),
    )
    return jax.shard_map(local, mesh=mesh, in_specs=in_specs, out_specs=out_specs, check_vma=False)
```

```python
import functools

import jax
import jax.numpy as jnp
from jax import lax
from jax.experimental import pallas as pl
from jax.experimental.pallas import tpu as pltpu
from jax.sharding import PartitionSpec as P

HEADS = 12
HEAD_DIM = 64
FF = 3072
EPSILON = 1e-12
ROOT_HALF = 0.7071067811865476
DENSITY_SCALE = 0.3989422804014327
QB = 256
WIDE = 256

BF = jnp.bfloat16
F32 = jnp.float32
MESH = pl.DeviceIdType.MESH


def layer_norm(values_in, gain, shift):
    row_mean = jnp.mean(values_in, axis=-1, keepdims=True)
    centred = values_in - row_mean
    inverse = lax.rsqrt(jnp.mean(centred * centred, axis=-1, keepdims=True) + EPSILON)
    normed = centred * inverse
    return (normed * gain + shift, normed, inverse)


def norm_back(grad_in, normed, inverse, gain):
    spread = grad_in * gain
    return inverse * (
        spread
        - jnp.mean(spread, axis=-1, keepdims=True)
        - normed * jnp.mean(spread * normed, axis=-1, keepdims=True)
    )


def cross_dot(left, right):
    return lax.dot_general(left, right, (((0,), (0,)), ((), ())), preferred_element_type=F32)


def back_dot(left, right):
    return lax.dot_general(left, right, (((1,), (1,)), ((), ())), preferred_element_type=F32)


def lane_half(tile, which):
    lane = lax.broadcasted_iota(jnp.int32, tile.shape, 1)
    return jnp.where((lane >= HEAD_DIM) == (which == 1), tile, jnp.zeros_like(tile))


def tile_lanes(kind, tile):
    start = 128 * kind + 384 * tile
    return slice(start, start + 128)


def column_of(row):
    return jnp.transpose(jnp.broadcast_to(row, (8, row.shape[1])))[:, 0:1]


def attend_kernel(
    place, live, tokens, lengths, query_weight, key_weight, value_weight, query_bias,
    value_bias, out_weight,
    qkv, log_total, context, partial, segment,
    weight, value_t, bias, seg_col,
):
    micro, step = pl.program_id(0), pl.program_id(1)
    rows_all = tokens.shape[1]

    @pl.when((micro == 0) & (step == 0))
    def _():
        bias[...] = jnp.zeros_like(bias)
        for kind, ref in enumerate((query_weight, key_weight, value_weight)):
            weight[128 * kind : 128 * kind + 128, :] = ref[0:128, :]
            weight[384 + 128 * kind : 448 + 128 * kind, :] = ref[128:192, :]
            weight[448 + 128 * kind : 512 + 128 * kind, :] = jnp.zeros_like(ref[128:192, :])
        for kind, ref in ((0, query_bias), (2, value_bias)):
            bias[0:1, 128 * kind : 128 * kind + 128] = ref[0:1, 0:128]
            bias[0:1, 384 + 128 * kind : 448 + 128 * kind] = ref[0:1, 128:192]

    @pl.when(step == 0)
    def _():
        def project(index, carry):
            rows = pl.ds(pl.multiple_of(index * QB, QB), QB)
            qkv[rows, :] = (
                back_dot(tokens[0, rows, :], weight[...]) + bias[0:1, :]
            ).astype(BF)
            for tile in range(2):
                value_t[128 * tile : 128 * tile + 128, rows] = jnp.transpose(
                    qkv[rows, tile_lanes(2, tile)]
                )
            return carry

        lax.fori_loop(0, rows_all // QB, project, 0)
        ends = jnp.broadcast_to(lengths[0], (8, rows_all))
        lane = lax.broadcasted_iota(jnp.int32, (8, rows_all), 1)
        shift = 1
        while shift < rows_all:
            ends = ends + jnp.where(lane >= shift, pltpu.roll(ends, shift, 1), 0)
            shift *= 2
        ends_col = column_of(ends[0:1, :].astype(F32))
        places = lax.broadcasted_iota(jnp.int32, (rows_all, rows_all), 1).astype(F32)
        count = jnp.sum(jnp.where(ends_col <= places, 1.0, 0.0), axis=0, keepdims=True)
        segment[...] = jnp.broadcast_to(count, (8, rows_all))
        seg_col[...] = column_of(count)

    rows = pl.ds(pl.multiple_of(step * QB, QB), QB)
    same = seg_col[...] == segment[0:1, rows]
    outs = []
    logs = []
    for head in range(3):
        tile = head // 2
        query = qkv[rows, tile_lanes(0, tile)] * jnp.asarray(0.125, BF)
        query = lane_half(query, head % 2)
        keys = qkv[:, tile_lanes(1, tile)]
        scores = jnp.where(same, back_dot(keys, query), -1e30)
        top = jnp.max(scores, axis=0, keepdims=True)
        expo = jnp.exp(scores - top)
        total = jnp.sum(expo, axis=0, keepdims=True)
        probs = (expo * (1.0 / total)).astype(BF)
        outs.append(
            jnp.dot(
                value_t[64 * head : 64 * head + 64, :], probs, preferred_element_type=F32
            )
        )
        logs.append(top + jnp.log(total))
    context_t = jnp.concatenate(outs, axis=0) * live[micro].astype(F32)
    low = jnp.transpose(context_t).astype(BF)
    context[...] = low
    log_total[...] = jnp.concatenate(logs + [jnp.zeros((5, QB), F32)], axis=0)
    partial[...] = jnp.dot(low, out_weight[...], preferred_element_type=F32).astype(BF)


def attend(
    place, live, tokens, lengths, query_weight, key_weight, value_weight, query_bias,
    value_bias, out_weight,
):
    micro_count, rows, width = tokens.shape
    steps = rows // QB
    full = lambda array: pl.BlockSpec(array.shape, lambda m, i, *_: (0,) * array.ndim)
    return pl.pallas_call(
        attend_kernel,
        grid_spec=pltpu.PrefetchScalarGridSpec(
            num_scalar_prefetch=2,
            grid=(micro_count, steps),
            in_specs=[
                pl.BlockSpec((1, rows, width), lambda m, i, *_: (m, 0, 0)),
                pl.BlockSpec((1, 1, rows), lambda m, i, *_: (m, 0, 0)),
                full(query_weight),
                full(key_weight),
                full(value_weight),
                full(query_bias),
                full(value_bias),
                full(out_weight),
            ],
            out_specs=[
                pl.BlockSpec((rows, 3 * WIDE), lambda m, i, *_: (m, 0)),
                pl.BlockSpec((8, QB), lambda m, i, *_: (m, i)),
                pl.BlockSpec((QB, 192), lambda m, i, *_: (m * steps + i, 0)),
                pl.BlockSpec((QB, width), lambda m, i, p, l: (m * steps + (i ^ p[0]), 0)),
                pl.BlockSpec((8, rows), lambda m, i, *_: (m, 0)),
            ],
            scratch_shapes=[
                pltpu.VMEM((3 * WIDE, width), BF),
                pltpu.VMEM((WIDE, rows), BF),
                pltpu.VMEM((8, 3 * WIDE), F32),
                pltpu.VMEM((rows, 1), F32),
            ],
        ),
        out_shape=[
            jax.ShapeDtypeStruct((micro_count * rows, 3 * WIDE), BF),
            jax.ShapeDtypeStruct((micro_count * 8, rows), F32),
            jax.ShapeDtypeStruct((micro_count * rows, 192), BF),
            jax.ShapeDtypeStruct((micro_count * rows, width), BF),
            jax.ShapeDtypeStruct((micro_count * 8, rows), F32),
        ],
        compiler_params=pltpu.CompilerParams(
            dimension_semantics=("arbitrary", "arbitrary"), vmem_limit_bytes=48 << 20
        ),
        name="attend",
    )(
        place, live, tokens, lengths, query_weight, key_weight, value_weight, query_bias,
        value_bias, out_weight,
    )


CHUNK = 48


def by_chunks(count, body):
    def one(index, carry):
        body(pl.multiple_of(index * CHUNK, CHUNK))
        return carry

    lax.fori_loop(0, count // CHUNK, one, 0)


def reduce_plan(rows, order):
    plan = []
    length, offset = rows, 0
    for index, bit in enumerate(order):
        halving = index < len(order) - 1 and length % (2 * CHUNK) == 0
        if halving:
            length //= 2
        plan.append((bit, halving, length, offset))
        offset += length
    return plan, offset


class BatchSum:
    def __init__(self, term, first, rows, columns, order, give, take, whole, sems, base):
        self.term, self.first, self.rows, self.columns = term, first, rows, columns
        self.give, self.take, self.whole = give, take, whole
        self.send_sem, self.recv_sem = sems
        self.base = base
        self.plan, _ = reduce_plan(rows, order)
        self.place = lax.axis_index("batch")
        self.starts = [0]
        for bit, halving, length, _ in self.plan:
            start = self.starts[-1]
            if halving:
                start = start + ((self.place >> bit) & 1) * length
            self.starts.append(start)

    def rows_at(self, ref, start, length, lift=0):
        return ref.at[pl.ds(pl.multiple_of(start + lift, CHUNK), length), 0 : self.columns]

    def copy(self, src, dst, index, bit):
        return pltpu.make_async_remote_copy(
            src_ref=src,
            dst_ref=dst,
            send_sem=self.send_sem.at[self.base + index],
            recv_sem=self.recv_sem.at[self.base + index],
            device_id={"batch": self.place ^ (1 << bit)},
            device_id_type=MESH,
        )

    def reduce_copy(self, step):
        bit, _, length, offset = self.plan[step]
        return self.copy(
            self.rows_at(self.give, offset, length),
            self.rows_at(self.take, offset, length),
            step,
            bit,
        )

    def reduce_start(self, step):
        bit, halving, length, offset = self.plan[step]
        start = self.starts[step]
        if halving:
            start = start + (1 - ((self.place >> bit) & 1)) * length

        def pack(at):
            self.rows_at(self.give, offset + at, CHUNK)[...] = self.rows_at(
                self.term, start + at, CHUNK, self.first
            )[...].astype(BF)

        by_chunks(length, pack)
        self.reduce_copy(step).start()

    def reduce_finish(self, step):
        _, halving, length, offset = self.plan[step]
        self.reduce_copy(step).wait_recv()
        start = self.starts[step + 1]

        def merge(at):
            mine = self.rows_at(self.term, start + at, CHUNK, self.first)
            got = self.rows_at(self.take, offset + at, CHUNK)[...].astype(F32)
            if halving:
                mine[...] = mine[...] + got
            else:
                mine[...] = self.rows_at(self.give, offset + at, CHUNK)[...].astype(F32) + got

        by_chunks(length, merge)

    def settle(self):
        length, start = self.plan[-1][2], self.starts[-1]

        def pack(at):
            self.rows_at(self.whole, start + at, CHUNK, self.first)[...] = self.rows_at(
                self.term, start + at, CHUNK, self.first
            )[...].astype(BF)

        by_chunks(length, pack)

    def gather_copy(self, step):
        bit, _, length, _ = self.plan[step]
        region = self.rows_at(self.whole, self.starts[step + 1], length, self.first)
        return self.copy(region, region, len(self.plan) + step, bit)

    def gather_start(self, step):
        if self.plan[step][1]:
            self.gather_copy(step).start()

    def gather_finish(self, step):
        if self.plan[step][1]:
            self.gather_copy(step).wait_recv()

    def last(self):
        return 2 * len(self.plan) - 1

    def advance(self, index):
        count = len(self.plan)
        if index == 0:
            self.reduce_start(0)
        elif index < count:
            self.reduce_finish(index - 1)
            self.reduce_start(index)
        elif index == count:
            self.reduce_finish(count - 1)
            self.settle()
            self.gather_start(count - 2)
        else:
            self.gather_finish(2 * count - 1 - index)
            if index < 2 * count - 1:
                self.gather_start(2 * count - 2 - index)

    def drain(self):
        for step in range(len(self.plan)):
            self.reduce_copy(step).wait_send()
            if self.plan[step][1]:
                self.gather_copy(step).wait_send()


class VectorSum:
    def __init__(self, values, take, targets, sems, base):
        self.values, self.take, self.targets = values, take, targets
        self.send_sem, self.recv_sem = sems
        self.base = base

    def at(self, ref, step):
        return ref.at[8 * step : 8 * step + 8, :]

    def copy(self, step):
        return pltpu.make_async_remote_copy(
            src_ref=self.at(self.values, step),
            dst_ref=self.at(self.take, step),
            send_sem=self.send_sem.at[self.base + step],
            recv_sem=self.recv_sem.at[self.base + step],
            device_id=self.targets[step],
            device_id_type=MESH,
        )

    def advance(self, index):
        if index > 0:
            self.copy(index - 1).wait_recv()
            self.at(self.values, index)[...] = (
                self.at(self.values, index - 1)[...] + self.at(self.take, index - 1)[...]
            )
        if index < len(self.targets):
            self.copy(index).start()

    def drain(self):
        for step in range(len(self.targets)):
            self.copy(step).wait_send()


EVENTS = {
    "open": (
        "d0", "d2",
    ),
    "closing": (
        "d1", "d3",
    ),
    "closed": (
        "s",
    ),
    0: (
        "d0", "d2", "i0", "d1",
    ),
    1: (
        "s", "d3", "i1",
    ),
    2: (
        "i0", "i2", "d2", "i3",
    ),
    3: (
        "s", "i1", "d3", "d0", "d1", "i2",
    ),
    "between": (
        "i0", "d2", "i3",
    ),
    "weighed": (
        "i1",
    ),
    4: (
        "d3", "d2", "d0",
    ),
    5: (
        "s", "d1",
    ),
    6: (
        "s", "d3", "i0", "i2",
    ),
    7: (
        "s", "i1", "i3", "d0",
    ),
    "start": (
        "i0", "d1",
    ),
    "pre": (
        "i1", "i2",
    ),
    "mid": (
        "q0",
    ),
    "tail": (
        "o0", "i3", "q1", "q0", "o0", "q2", "q1", "q0",
    ),
    "end": (
        "i2", "q2", "q1", "i3", "q0", "o0", "q2", "q1", "q0", "o0",
        "q2", "q1", "o0", "q2",
    ),
}
Z_FIRST = ("d0", "d1", "o0",)
POINTS = (
    "open", "closing", "closed", 0, 1, 2, 3, "between", "weighed", 4, 5, 6, 7,
    "start", "pre", "mid", "tail", "end",
)


def layer_kernel(
    live, partial_hbm, token_hbm, cot_hbm, qkv_hbm, in_hbm, down_hbm, query_hbm, key_hbm,
    value_hbm, out_hbm, context_hbm, log_total, segment, *rest
):
    layer_body(
        live, partial_hbm, token_hbm, cot_hbm, qkv_hbm, in_hbm, down_hbm,
        (query_hbm, key_hbm, value_hbm), out_hbm, context_hbm, log_total, segment,
        rest[:7], *rest[7:]
    )


def layer_body(
    live, partial_hbm, token_hbm, cot_hbm, qkv_hbm, in_hbm, down_hbm, low_hbm, out_hbm,
    context_hbm, log_total, segment, vectors,
    result, input_grad, in_whole, down_whole, qkv_whole, out_whole, sums_out, bias_out,
    in_weight, down_weight, context,
    in_term, down_term, qkv_term, out_term, weight_all,
    far, near, cross, sums, hid, gm2, act, slope, gpre, pbuf, grad_low,
    hidden_rows, normed_rows, inverse_rows, key_t, key_acc, value_acc, seg_col, out_wide,
    down_take, in_take, qkv_take, out_take, vec_values, vec_take, bias_values, bias_take,
    send_sem, recv_sem, batch_send, batch_recv, load_sem,
):
    place = lax.axis_index("tensor")
    batch_place = lax.axis_index("batch")
    batch_bits = lax.axis_size("batch").bit_length() - 1
    core_id = {"tensor": place ^ 1}
    chip_id = {"tensor": place ^ 2}
    share = input_grad.shape[1]
    rows_all = 4 * share

    def slot(buf, micro, index):
        start = (micro * 4 + index) * share
        if not isinstance(start, int):
            start = pl.multiple_of(start, share)
        return buf.at[pl.ds(start, share), :]

    def own_rows(buf, micro):
        start = micro * share
        if not isinstance(start, int):
            start = pl.multiple_of(start, share)
        return buf.at[pl.ds(start, share), :]

    def copy(src, dst, micro, phase, kind, target):
        index = (micro * 4 + phase) * 6 + kind
        return pltpu.make_async_remote_copy(
            src_ref=src,
            dst_ref=dst,
            send_sem=send_sem.at[index],
            recv_sem=recv_sem.at[index],
            device_id=target,
            device_id_type=MESH,
        )

    def far_copy(parts, micro, phase):
        return copy(slot(parts, micro, 3), own_rows(far, micro), micro, phase, 0, core_id)

    def near_copy(parts, micro, phase):
        return copy(slot(parts, micro, 1), own_rows(near, micro), micro, phase, 1, core_id)

    def cross_copy(micro, phase):
        return copy(own_rows(sums, micro), own_rows(cross, micro), micro, phase, 2, chip_id)

    def crossing_copy(buf, micro, phase):
        return copy(slot(buf, micro, 0), slot(buf, micro, 2), micro, phase, 3, chip_id)

    def beside_copy(buf, micro, phase):
        return copy(slot(buf, micro, 0), slot(buf, micro, 1), micro, phase, 4, core_id)

    def onward_copy(buf, micro, phase):
        return copy(slot(buf, micro, 2), slot(buf, micro, 3), micro, phase, 5, core_id)

    def scatter_start(parts, micro, phase):
        far_copy(parts, micro, phase).start()
        near_copy(parts, micro, phase).start()

    def scatter_mid(parts, micro, phase):
        far_copy(parts, micro, phase).wait_recv()
        own_rows(sums, micro)[...] = (
            slot(parts, micro, 2)[...].astype(F32) + own_rows(far, micro)[...].astype(F32)
        ).astype(BF)
        cross_copy(micro, phase).start()

    def scatter_end(parts, micro, phase):
        near_copy(parts, micro, phase).wait_recv()
        cross_copy(micro, phase).wait_recv()
        cross_copy(micro, phase).wait_send()
        return (
            slot(parts, micro, 0)[...].astype(F32)
            + own_rows(near, micro)[...].astype(F32)
            + own_rows(cross, micro)[...].astype(F32)
        )

    def scatter_drain(parts, micro, phase):
        far_copy(parts, micro, phase).wait_send()
        near_copy(parts, micro, phase).wait_send()

    def gather_start(buf, micro, phase):
        crossing_copy(buf, micro, phase).start()
        beside_copy(buf, micro, phase).start()

    def gather_step(buf, micro, phase, which):
        @pl.when(which == 1)
        def _():
            beside_copy(buf, micro, phase).wait_recv()

        @pl.when(which == 2)
        def _():
            crossing_copy(buf, micro, phase).wait_recv()
            onward_copy(buf, micro, phase).start()

        @pl.when(which == 3)
        def _():
            onward_copy(buf, micro, phase).wait_recv()

    def gather_drain(buf, micro, phase):
        crossing_copy(buf, micro, phase).wait_send()
        beside_copy(buf, micro, phase).wait_send()
        onward_copy(buf, micro, phase).wait_send()

    def vector(index):
        return vectors[index][...].reshape(1, -1)

    def tally(index, value):
        vec_values[index : index + 1, :] += jnp.sum(value, axis=0, keepdims=True)

    taken = []

    def load(src, dst):
        taken.append(0)
        handle = pltpu.make_async_copy(src, dst, load_sem.at[len(taken) - 1])
        handle.start()
        return handle

    def micro_block(micro):
        return pl.ds(micro * rows_all, rows_all)

    first_row = pl.multiple_of(place * share, share)
    part_loads = [
        load(partial_hbm.at[micro_block(m), :], pbuf.at[micro_block(m), :]) for m in range(2)
    ]
    row_loads = [
        load(token_hbm.at[m, pl.ds(first_row, share), :], slot(grad_low, m, 0))
        for m in range(2)
    ] + [load(cot_hbm.at[m, pl.ds(first_row, share), :], result.at[m]) for m in range(2)]
    weight_loads = [load(in_hbm, in_weight), load(down_hbm, down_weight)]
    late_loads = [load(out_hbm, out_wide.at[0:192, :]), load(context_hbm, context)]
    for kind, ref in enumerate(low_hbm):
        late_loads.append(
            load(ref.at[0:128, :], weight_all.at[128 * kind : 128 * kind + 128, :])
        )
        late_loads.append(
            load(ref.at[128:192, :], weight_all.at[384 + 64 * kind : 448 + 64 * kind, :])
        )

    sems = (batch_send, batch_recv)
    up = tuple(range(batch_bits))
    turned = up[1:] + up[:1]
    stride = 2 * batch_bits
    chunks = []

    def chunk(term, first, count, order, give, give_at, take, take_at, whole):
        size = reduce_plan(count, order)[1]
        chunks.append(
            BatchSum(
                term, first, count, term.shape[1], order,
                give.at[give_at : give_at + size, :],
                take.at[take_at : take_at + size, :],
                whole, sems, len(chunks) * stride,
            )
        )
        return chunks[-1]

    small = reduce_plan(192, up)[1]
    named = {}

    def add_chunks(letter, count, term, give, give_at, take, whole):
        for k in range(count):
            name = letter + str(k)
            named[name] = chunk(
                term, 192 * k, 192, turned if name in Z_FIRST else up,
                *((slope, small * (4 + k)) if letter == "i" and k < 2 else (give, give_at + small * k)),
                take, small * k, whole,
            )

    add_chunks("d", 4, down_term, slope, 0, down_take, down_whole)
    add_chunks("i", 4, in_term, hid, small * 2, in_take, in_whole)
    add_chunks("q", 3, qkv_term, hid, 0, qkv_take, qkv_whole)
    add_chunks("o", 1, out_term, hid, small * 3, out_take, out_whole)
    batch_targets = [{"batch": batch_place ^ (1 << bit)} for bit in up]
    shared_sum = VectorSum(
        vec_values, vec_take, batch_targets + [core_id, chip_id], sems, 12 * stride
    )
    bias_sum = VectorSum(bias_values, bias_take, batch_targets, sems, 13 * stride + 2)

    barrier = pltpu.get_barrier_semaphore()
    partners = [core_id, chip_id] + batch_targets
    for target in partners:
        pl.semaphore_signal(barrier, inc=1, device_id=target, device_id_type=MESH)
    vec_values[0:8, :] = jnp.zeros((8, vec_values.shape[1]), F32)
    bias_values[0:8, :] = jnp.zeros((8, bias_values.shape[1]), F32)
    out_term[...] = jnp.zeros_like(out_term)
    out_wide[192:256, :] = jnp.zeros((64, out_wide.shape[1]), BF)
    weight_all[576:640, :] = jnp.zeros((64, weight_all.shape[1]), BF)
    pl.semaphore_wait(barrier, len(partners))

    for micro in range(2):
        part_loads[micro].wait()
        scatter_start(pbuf, micro, 0)
    for micro in range(2):
        scatter_mid(pbuf, micro, 0)
    for handle in row_loads + weight_loads:
        handle.wait()

    def opening(micro, carry):
        total = scatter_end(pbuf, micro, 0)
        hidden, normed, inverse = layer_norm(
            slot(grad_low, micro, 0)[...].astype(F32) + total + vector(0), vector(1), vector(2)
        )
        own_rows(hidden_rows, micro)[...] = hidden
        own_rows(normed_rows, micro)[...] = normed
        own_rows(inverse_rows, micro)[...] = jnp.broadcast_to(inverse, (share, 128))
        slot(hid, micro, 0)[...] = hidden.astype(BF)
        gather_start(hid, micro, 0)
        return carry

    lax.fori_loop(0, 2, opening, 0)
    for micro in range(2):
        scatter_drain(pbuf, micro, 0)

    def forward(index, carry):
        micro, which = index // 4, index % 4
        gather_step(hid, micro, 0, which)
        pre = (
            jnp.dot(slot(hid, micro, which)[...], in_weight[...], preferred_element_type=F32)
            + vector(3)
        )
        alive = live[micro].astype(F32)
        below = 0.5 * (1.0 + lax.erf(pre * ROOT_HALF)) * alive
        low = (pre * below).astype(BF)
        slot(act, micro, which)[...] = low
        slot(slope, micro, which)[...] = (
            below + pre * jnp.exp(-0.5 * pre * pre) * (DENSITY_SCALE * alive)
        ).astype(BF)
        slot(pbuf, micro, which)[...] = jnp.dot(
            low, down_weight[...], preferred_element_type=F32
        ).astype(BF)

        @pl.when(which == 3)
        def _():
            scatter_start(pbuf, micro, 1)

        @pl.when(index == 4)
        def _():
            scatter_mid(pbuf, 0, 1)

        return carry

    lax.fori_loop(0, 8, forward, 0)
    scatter_mid(pbuf, 1, 1)

    def middle(micro, carry):
        total = scatter_end(pbuf, micro, 1)
        final, normed, inverse = layer_norm(
            own_rows(hidden_rows, micro)[...] + total + vector(4), vector(5), vector(6)
        )
        grad_y = result[micro].astype(F32)
        result[micro] = final.astype(BF)
        grad_mid2 = norm_back(grad_y, normed, inverse, vector(5))
        own_rows(hidden_rows, micro)[...] = grad_mid2
        slot(gm2, micro, 0)[...] = grad_mid2.astype(BF)
        gather_start(gm2, micro, 1)
        tally(3, grad_mid2)
        tally(4, grad_y * normed)
        tally(5, grad_y)
        return carry

    lax.fori_loop(0, 2, middle, 0)
    for micro in range(2):
        scatter_drain(pbuf, micro, 1)

    def backward(index, carry):
        micro, which = index // 4, index % 4
        gather_step(gm2, micro, 1, which)
        grad_pre = (
            back_dot(slot(gm2, micro, which)[...], down_weight[...])
            * slot(slope, micro, which)[...].astype(F32)
        ).astype(BF)
        slot(gpre, micro, which)[...] = grad_pre
        tally(6, grad_pre.astype(F32))
        slot(pbuf, micro, which)[...] = back_dot(grad_pre, in_weight[...]).astype(BF)

        @pl.when(which == 3)
        def _():
            scatter_start(pbuf, micro, 2)

        @pl.when(index == 4)
        def _():
            scatter_mid(pbuf, 0, 2)

        return carry

    lax.fori_loop(0, 8, backward, 0)
    scatter_mid(pbuf, 1, 2)

    def weigh(left, right, out):
        def block(index, carry):
            lanes = pl.ds(pl.multiple_of(index * 256, 256), 256)
            out[lanes, :] = cross_dot(left[:, lanes], right[...])
            return carry

        lax.fori_loop(0, out.shape[0] // 256, block, 0)

    weigh(act, gm2, down_term)
    for k in range(4):
        named["d" + str(k)].advance(0)
    for micro in range(2):
        gather_drain(hid, micro, 0)
        gather_drain(gm2, micro, 1)
    late_loads.extend(
        load(token_hbm.at[m], act.at[micro_block(m), :]) for m in range(2)
    )
    late_loads.append(load(qkv_hbm, gm2))
    weigh(hid, gpre, in_term)
    for k in range(4):
        named["i" + str(k)].advance(0)

    def closing(micro):
        total = scatter_end(pbuf, micro, 2)
        grad_hidden = own_rows(hidden_rows, micro)[...] + total
        normed = own_rows(normed_rows, micro)[...]
        inverse = own_rows(inverse_rows, micro)[:, 0:1]
        grad = norm_back(grad_hidden, normed, inverse, vector(1))
        input_grad[micro] = grad
        slot(grad_low, micro, 0)[...] = grad.astype(BF)
        gather_start(grad_low, micro, 2)
        tally(0, grad)
        tally(1, grad_hidden * normed)
        tally(2, grad_hidden)

    reached = {name: 0 for name in named}
    reached["s"] = -1
    planned = {}
    for point in POINTS:
        planned[point] = []
        for name in EVENTS.get(point, ()):
            reached[name] += 1
            planned[point].append((name, reached[name]))

    def run(point):
        for name, step in planned[point]:
            (shared_sum if name == "s" else named[name]).advance(step)

    run("open")
    closing(0)
    run("closing")
    closing(1)
    for micro in range(2):
        scatter_drain(pbuf, micro, 2)
    run("closed")
    for handle in late_loads:
        handle.wait()
    qkv, tokens, grads = gm2, act, gpre

    def micro_rows(micro):
        return pl.ds(pl.multiple_of(micro * rows_all, rows_all), rows_all)

    def finish_grads(micro):
        block = micro_block(micro)
        grads[block, 128:256] = key_acc[:, 0:128].astype(BF)
        grads[block, 256:384] = value_acc[:, 0:128].astype(BF)
        grads[block, 448:512] = key_acc[:, 128:192].astype(BF)
        grads[block, 512:640] = value_acc[:, 128:256].astype(BF)
        bias_values[0:1, 0:640] += jnp.sum(
            grads[block, 0:640].astype(F32), axis=0, keepdims=True
        )


    def weigh_low(micro):
        block = micro_block(micro)
        for first, count in ((0, 256), (256, 256), (512, 64)):
            value = cross_dot(grads[block, first : first + count], tokens[block, :])
            if micro == 0:
                qkv_term[first : first + count, :] = value
            else:
                qkv_term[first : first + count, :] += value

    def send_input(micro):
        def send_slot(index, carry):
            start = pl.multiple_of(micro * rows_all + (index ^ place) * share, share)
            slot(pbuf, micro, index)[...] = jnp.dot(
                grads[pl.ds(start, share), 0:640], weight_all[...], preferred_element_type=F32
            ).astype(BF)
            return carry

        lax.fori_loop(0, 4, send_slot, 0)
        scatter_start(pbuf, micro, 3)

    def attend_back(index, carry):
        micro, which = index // 4, index % 4
        gather_step(grad_low, micro, 2, which)
        step = which ^ place
        block = micro_rows(micro)
        rows = pl.ds(pl.multiple_of(micro * rows_all + step * share, share), share)

        @pl.when(which == 0)
        def _():
            for tile in range(2):
                key_t[128 * tile : 128 * tile + 128, :] = jnp.transpose(
                    qkv[block, tile_lanes(1, tile)]
                )
            key_acc[...] = jnp.zeros_like(key_acc)
            value_acc[...] = jnp.zeros_like(value_acc)
            seg_col[...] = column_of(
                segment[pl.ds(pl.multiple_of(micro * 8, 8), 8), :][0:1, :]
            )

        eight = pl.ds(pl.multiple_of(micro * 8, 8), 8)
        columns = pl.ds(pl.multiple_of(step * share, share), share)
        seg_row = segment[eight, columns][0:1, :]
        logs = log_total[eight, columns]
        grad_slot = slot(grad_low, micro, which)[...]
        out_term[...] += cross_dot(context[rows, :], grad_slot)

        @pl.when(index == 7)
        def _():
            named["o0"].advance(0)

        alive = live[micro].astype(BF)
        grad_context = back_dot(grad_slot, out_wide[...]).astype(BF) * alive
        same = seg_col[...] == seg_row
        query_parts = []
        for head in range(3):
            tile = head // 2
            lanes = slice(128 * tile, 128 * tile + 128)
            query = qkv[rows, tile_lanes(0, tile)] * jnp.asarray(0.125, BF)
            query = lane_half(query, head % 2)
            grad_tile = lane_half(grad_context[:, lanes], head % 2)
            keys = qkv[block, tile_lanes(1, tile)]
            values = qkv[block, tile_lanes(2, tile)]
            scores = jnp.where(same, back_dot(keys, query), -1e30)
            probs = jnp.exp(scores - logs[head : head + 1, :])
            grad_probs = back_dot(values, grad_tile)
            mean = jnp.sum(probs * grad_probs, axis=0, keepdims=True)
            grad_scores = (probs * (grad_probs - mean)).astype(BF)
            value_acc[:, lanes] += jnp.dot(
                probs.astype(BF), grad_tile, preferred_element_type=F32
            )
            key_acc[:, lanes] += jnp.dot(grad_scores, query, preferred_element_type=F32)
            query_parts.append(
                jnp.dot(
                    key_t[64 * head : 64 * head + 64, :],
                    grad_scores,
                    preferred_element_type=F32,
                )
            )
        query_t = jnp.concatenate(query_parts + [jnp.zeros((64, share), F32)], axis=0) * 0.125
        query_grad = jnp.transpose(query_t).astype(BF)
        grads[rows, 0:128] = query_grad[:, 0:128]
        grads[rows, 384:448] = query_grad[:, 128:192]

        for point in range(8):
            if planned[point]:

                @pl.when(index == point)
                def _():
                    run(point)

        @pl.when(index == 3)
        def _():
            finish_grads(0)
            send_input(0)
            run("between")
            weigh_low(0)
            run("weighed")

        @pl.when(index == 4)
        def _():
            scatter_mid(pbuf, 0, 3)

        return carry

    lax.fori_loop(0, 8, attend_back, 0)
    finish_grads(1)
    weigh_low(1)
    for k in range(3):
        named["q" + str(k)].advance(0)
    bias_sum.advance(0)
    run("start")
    send_input(1)
    run("pre")
    scatter_mid(pbuf, 1, 3)
    run("mid")

    def final_rows(micro):
        input_grad[micro] = input_grad[micro] + scatter_end(pbuf, micro, 3)

    final_rows(0)
    run("tail")
    final_rows(1)
    for index in range(1, batch_bits + 1):
        bias_sum.advance(index)
    run("end")
    for name in sorted(named):
        while reached[name] < named[name].last():
            reached[name] += 1
            named[name].advance(reached[name])
    while reached["s"] < batch_bits + 2:
        reached["s"] += 1
        shared_sum.advance(reached["s"])

    base = 8 * batch_bits
    sums_out[...] = vec_values[base + 16 : base + 24, :]
    sums_out[6:7, :] = vec_values[base + 6 : base + 7, :]
    bias_out[...] = bias_values[base : base + 8, :]
    for micro in range(2):
        scatter_drain(pbuf, micro, 3)
        gather_drain(grad_low, micro, 2)
    for owner in chunks + [shared_sum, bias_sum]:
        owner.drain()


def layer_call(
    live, partials, tokens, cotangent, qkv, in_weight, down_weight, query_weight, key_weight,
    value_weight, out_weight, context, log_total, segment, *vectors
):
    micro_count, rows_all, width = tokens.shape
    share = rows_all // 4
    rows = micro_count * rows_all
    units = in_weight.shape[1]
    batch_bits = lax.axis_size("batch").bit_length() - 1
    order = tuple(range(batch_bits))
    small = reduce_plan(192, order)[1]
    vmem = pl.BlockSpec(memory_space=pltpu.VMEM)
    hbm = pl.BlockSpec(memory_space=pl.ANY)
    smem = pl.BlockSpec(memory_space=pltpu.SMEM)
    batch_sems = 14 * 2 * batch_bits + 2
    return pl.pallas_call(
        layer_kernel,
        in_specs=[smem] + [hbm] * 11 + [vmem] * (2 + len(vectors)),
        out_specs=[vmem] * 8,
        out_shape=[
            jax.ShapeDtypeStruct((micro_count, share, width), BF),
            jax.ShapeDtypeStruct((micro_count, share, width), F32),
            jax.ShapeDtypeStruct((width, units), BF),
            jax.ShapeDtypeStruct((units, width), BF),
            jax.ShapeDtypeStruct((576, width), BF),
            jax.ShapeDtypeStruct((192, width), BF),
            jax.ShapeDtypeStruct((8, width), F32),
            jax.ShapeDtypeStruct((8, width), F32),
        ],
        scratch_shapes=[
            pltpu.VMEM((width, units), BF),
            pltpu.VMEM((units, width), BF),
            pltpu.VMEM((rows, 192), BF),
            pltpu.VMEM((width, units), F32),
            pltpu.VMEM((units, width), F32),
            pltpu.VMEM((576, width), F32),
            pltpu.VMEM((192, width), F32),
            pltpu.VMEM((640, width), BF),
            pltpu.VMEM((2 * share, width), BF),
            pltpu.VMEM((2 * share, width), BF),
            pltpu.VMEM((2 * share, width), BF),
            pltpu.VMEM((2 * share, width), BF),
            pltpu.VMEM((rows, width), BF),
            pltpu.VMEM((rows, width), BF),
            pltpu.VMEM((rows, units), BF),
            pltpu.VMEM((rows, units), BF),
            pltpu.VMEM((rows, units), BF),
            pltpu.VMEM((rows, width), BF),
            pltpu.VMEM((rows, width), BF),
            pltpu.VMEM((2 * share, width), F32),
            pltpu.VMEM((2 * share, width), F32),
            pltpu.VMEM((2 * share, 128), F32),
            pltpu.VMEM((WIDE, rows_all), BF),
            pltpu.VMEM((rows_all, WIDE), F32),
            pltpu.VMEM((rows_all, WIDE), F32),
            pltpu.VMEM((rows_all, 1), F32),
            pltpu.VMEM((WIDE, width), BF),
            pltpu.VMEM((4 * small, width), BF),
            pltpu.VMEM((4 * small, width), BF),
            pltpu.VMEM((3 * small, width), BF),
            pltpu.VMEM((small, width), BF),
            pltpu.VMEM((8 * (batch_bits + 3), width), F32),
            pltpu.VMEM((8 * (batch_bits + 2), width), F32),
            pltpu.VMEM((8 * (batch_bits + 1), width), F32),
            pltpu.VMEM((8 * batch_bits, width), F32),
            pltpu.SemaphoreType.DMA((48,)),
            pltpu.SemaphoreType.DMA((48,)),
            pltpu.SemaphoreType.DMA((batch_sems,)),
            pltpu.SemaphoreType.DMA((batch_sems,)),
            pltpu.SemaphoreType.DMA((20,)),
        ],
        compiler_params=pltpu.CompilerParams(
            collective_id=1, has_side_effects=True, vmem_limit_bytes=67_043_328
        ),
        name="layer",
    )(
        live, partials, tokens, cotangent, qkv, in_weight, down_weight, query_weight,
        key_weight, value_weight, out_weight, context, log_total, segment, *vectors
    )


def local(
    tokens,
    lengths,
    quarters,
    query_weight,
    query_bias,
    key_weight,
    value_weight,
    value_bias,
    out_weight,
    out_bias,
    norm1_gain,
    norm1_shift,
    in_weight,
    in_bias,
    down_weight,
    down_bias,
    norm2_gain,
    norm2_shift,
    cotangent,
):
    place = lax.axis_index("tensor").astype(jnp.int32)
    live = (4 * place < 4 * quarters).astype(jnp.int32)
    low_weights = (query_weight.T, key_weight.T, value_weight.T)
    qkv, log_total, context, partials, segment = attend(
        place[None],
        live,
        tokens,
        lengths.reshape(lengths.shape[0], 1, lengths.shape[2]),
        *low_weights,
        query_bias[None],
        value_bias[None],
        out_weight,
    )
    result, input_grad, in_sum, down_sum, packed, out_sum, sums, bias = layer_call(
        live,
        partials,
        tokens,
        cotangent,
        qkv,
        in_weight,
        down_weight,
        *low_weights,
        out_weight,
        context,
        log_total,
        segment,
        out_bias,
        norm1_gain,
        norm1_shift,
        in_bias,
        down_bias,
        norm2_gain,
        norm2_shift,
    )

    def joined(kind):
        return jnp.concatenate(
            [
                packed[128 * kind : 128 * kind + 128],
                packed[384 + 64 * kind : 448 + 64 * kind],
            ]
        ).astype(F32).T

    def joined_bias(kind):
        return jnp.concatenate(
            [
                bias[0, 128 * kind : 128 * kind + 128],
                bias[0, 384 + 64 * kind : 448 + 64 * kind],
            ]
        )

    return (
        result,
        input_grad,
        joined(0),
        joined_bias(0),
        joined(1),
        joined(2),
        joined_bias(2),
        out_sum.astype(F32),
        sums[0],
        sums[1],
        sums[2],
        in_sum.astype(F32),
        sums[6],
        down_sum.astype(F32),
        sums[3],
        sums[4],
        sums[5],
    )


def solution(mesh):
    in_specs = (
        P(None, "batch", None),
        P(None, "batch", None),
        P(),
        P(None, "tensor"),
        P("tensor"),
        P(None, "tensor"),
        P(None, "tensor"),
        P("tensor"),
        P("tensor", None),
        P(),
        P(),
        P(),
        P(None, "tensor"),
        P("tensor"),
        P("tensor", None),
        P(),
        P(),
        P(),
        P(None, "batch", None),
    )
    out_specs = (
        P(None, ("batch", "tensor"), None),
        P(None, ("batch", "tensor"), None),
        P(None, "tensor"),
        P("tensor"),
        P(None, "tensor"),
        P(None, "tensor"),
        P("tensor"),
        P("tensor", None),
        P(),
        P(),
        P(),
        P(None, "tensor"),
        P("tensor"),
        P("tensor", None),
        P(),
        P(),
        P(),
    )
    return jax.shard_map(local, mesh=mesh, in_specs=in_specs, out_specs=out_specs, check_vma=False)
```

```python
import functools

import jax
import jax.numpy as jnp
from jax import lax
from jax.experimental import pallas as pl
from jax.experimental.pallas import tpu as pltpu
from jax.sharding import PartitionSpec as P

HEADS = 12
HEAD_DIM = 64
FF = 3072
EPSILON = 1e-12
ROOT_HALF = 0.7071067811865476
DENSITY_SCALE = 0.3989422804014327
QB = 256
WIDE = 256

BF = jnp.bfloat16
F32 = jnp.float32
MESH = pl.DeviceIdType.MESH


def layer_norm(values_in, gain, shift):
    row_mean = jnp.mean(values_in, axis=-1, keepdims=True)
    centred = values_in - row_mean
    inverse = lax.rsqrt(jnp.mean(centred * centred, axis=-1, keepdims=True) + EPSILON)
    normed = centred * inverse
    return (normed * gain + shift, normed, inverse)


def norm_back(grad_in, normed, inverse, gain):
    spread = grad_in * gain
    return inverse * (
        spread
        - jnp.mean(spread, axis=-1, keepdims=True)
        - normed * jnp.mean(spread * normed, axis=-1, keepdims=True)
    )


def cross_dot(left, right):
    return lax.dot_general(left, right, (((0,), (0,)), ((), ())), preferred_element_type=F32)


def back_dot(left, right):
    return lax.dot_general(left, right, (((1,), (1,)), ((), ())), preferred_element_type=F32)


def lane_half(tile, which):
    lane = lax.broadcasted_iota(jnp.int32, tile.shape, 1)
    return jnp.where((lane >= HEAD_DIM) == (which == 1), tile, jnp.zeros_like(tile))


def tile_lanes(kind, tile):
    start = 128 * kind + 384 * tile
    return slice(start, start + 128)


def column_of(row):
    return jnp.transpose(jnp.broadcast_to(row, (8, row.shape[1])))[:, 0:1]


CHUNK = 48


def by_chunks(count, body):
    def one(index, carry):
        body(pl.multiple_of(index * CHUNK, CHUNK))
        return carry

    lax.fori_loop(0, count // CHUNK, one, 0)


def reduce_plan(rows, order):
    plan = []
    length, offset = rows, 0
    for index, bit in enumerate(order):
        halving = index < len(order) - 1 and length % (2 * CHUNK) == 0
        if halving:
            length //= 2
        plan.append((bit, halving, length, offset))
        offset += length
    return plan, offset


class BatchSum:
    def __init__(self, term, first, rows, columns, order, give, take, whole, sems, base):
        self.term, self.first, self.rows, self.columns = term, first, rows, columns
        self.give, self.take, self.whole = give, take, whole
        self.send_sem, self.recv_sem = sems
        self.base = base
        self.plan, _ = reduce_plan(rows, order)
        self.place = lax.axis_index("batch")
        self.starts = [0]
        for bit, halving, length, _ in self.plan:
            start = self.starts[-1]
            if halving:
                start = start + ((self.place >> bit) & 1) * length
            self.starts.append(start)

    def rows_at(self, ref, start, length, lift=0):
        return ref.at[pl.ds(pl.multiple_of(start + lift, CHUNK), length), 0 : self.columns]

    def copy(self, src, dst, index, bit):
        return pltpu.make_async_remote_copy(
            src_ref=src,
            dst_ref=dst,
            send_sem=self.send_sem.at[self.base + index],
            recv_sem=self.recv_sem.at[self.base + index],
            device_id={"batch": self.place ^ (1 << bit)},
            device_id_type=MESH,
        )

    def reduce_copy(self, step):
        bit, _, length, offset = self.plan[step]
        return self.copy(
            self.rows_at(self.give, offset, length),
            self.rows_at(self.take, offset, length),
            step,
            bit,
        )

    def reduce_start(self, step):
        bit, halving, length, offset = self.plan[step]
        start = self.starts[step]
        if halving:
            start = start + (1 - ((self.place >> bit) & 1)) * length

        def pack(at):
            self.rows_at(self.give, offset + at, CHUNK)[...] = self.rows_at(
                self.term, start + at, CHUNK, self.first
            )[...].astype(BF)

        by_chunks(length, pack)
        self.reduce_copy(step).start()

    def reduce_finish(self, step):
        _, halving, length, offset = self.plan[step]
        self.reduce_copy(step).wait_recv()
        start = self.starts[step + 1]

        def merge(at):
            mine = self.rows_at(self.term, start + at, CHUNK, self.first)
            got = self.rows_at(self.take, offset + at, CHUNK)[...].astype(F32)
            if halving:
                mine[...] = mine[...] + got
            else:
                mine[...] = self.rows_at(self.give, offset + at, CHUNK)[...].astype(F32) + got

        by_chunks(length, merge)

    def settle(self):
        length, start = self.plan[-1][2], self.starts[-1]

        def pack(at):
            self.rows_at(self.whole, start + at, CHUNK, self.first)[...] = self.rows_at(
                self.term, start + at, CHUNK, self.first
            )[...].astype(BF)

        by_chunks(length, pack)

    def gather_copy(self, step):
        bit, _, length, _ = self.plan[step]
        region = self.rows_at(self.whole, self.starts[step + 1], length, self.first)
        return self.copy(region, region, len(self.plan) + step, bit)

    def gather_start(self, step):
        if self.plan[step][1]:
            self.gather_copy(step).start()

    def gather_finish(self, step):
        if self.plan[step][1]:
            self.gather_copy(step).wait_recv()

    def last(self):
        return 2 * len(self.plan) - 1

    def advance(self, index):
        count = len(self.plan)
        if index == 0:
            self.reduce_start(0)
        elif index < count:
            self.reduce_finish(index - 1)
            self.reduce_start(index)
        elif index == count:
            self.reduce_finish(count - 1)
            self.settle()
            self.gather_start(count - 2)
        else:
            self.gather_finish(2 * count - 1 - index)
            if index < 2 * count - 1:
                self.gather_start(2 * count - 2 - index)

    def drain(self):
        for step in range(len(self.plan)):
            self.reduce_copy(step).wait_send()
            if self.plan[step][1]:
                self.gather_copy(step).wait_send()


class VectorSum:
    def __init__(self, values, take, targets, sems, base):
        self.values, self.take, self.targets = values, take, targets
        self.send_sem, self.recv_sem = sems
        self.base = base

    def at(self, ref, step):
        return ref.at[8 * step : 8 * step + 8, :]

    def copy(self, step):
        return pltpu.make_async_remote_copy(
            src_ref=self.at(self.values, step),
            dst_ref=self.at(self.take, step),
            send_sem=self.send_sem.at[self.base + step],
            recv_sem=self.recv_sem.at[self.base + step],
            device_id=self.targets[step],
            device_id_type=MESH,
        )

    def advance(self, index):
        if index > 0:
            self.copy(index - 1).wait_recv()
            self.at(self.values, index)[...] = (
                self.at(self.values, index - 1)[...] + self.at(self.take, index - 1)[...]
            )
        if index < len(self.targets):
            self.copy(index).start()

    def drain(self):
        for step in range(len(self.targets)):
            self.copy(step).wait_send()


EVENTS = {
    "open": (
        "d0", "d2",
    ),
    "closing": (
        "d1", "d3",
    ),
    "closed": (
        "s",
    ),
    0: (
        "d0", "d2", "i0", "d1",
    ),
    1: (
        "s", "d3", "i1",
    ),
    2: (
        "i0", "i2", "d2", "i3",
    ),
    3: (
        "s", "i1", "d3", "d0", "d1", "i2",
    ),
    "between": (
        "i0", "d2", "i3",
    ),
    "weighed": (
        "i1",
    ),
    4: (
        "d3", "d2", "d0",
    ),
    5: (
        "s", "d1",
    ),
    6: (
        "s", "d3", "i0", "i2",
    ),
    7: (
        "s", "i1", "i3", "d0",
    ),
    "start": (
        "i0", "d1",
    ),
    "pre": (
        "i1", "i2",
    ),
    "mid": (
        "q0",
    ),
    "tail": (
        "o0", "i3", "q1", "q0", "o0", "q2", "q1", "q0",
    ),
    "end": (
        "i2", "q2", "q1", "i3", "q0", "o0", "q2", "q1", "q0", "o0",
        "q2", "q1", "o0", "q2",
    ),
}
Z_FIRST = ("d0", "d1", "o0",)
POINTS = (
    "open", "closing", "closed", 0, 1, 2, 3, "between", "weighed", 4, 5, 6, 7,
    "start", "pre", "mid", "tail", "end",
)


def layer_kernel(
    quarters, token_hbm, cot_hbm, in_hbm, down_hbm, query_hbm, key_hbm, value_hbm, out_hbm,
    lengths, query_bias, value_bias, *rest
):
    layer_body(
        quarters, token_hbm, cot_hbm, in_hbm, down_hbm, (query_hbm, key_hbm, value_hbm), out_hbm,
        lengths, query_bias, value_bias, rest[:7], *rest[7:]
    )


def layer_body(
    quarters, token_hbm, cot_hbm, in_hbm, down_hbm, low_hbm, out_hbm, lengths, query_bias,
    value_bias, vectors,
    result, input_grad, in_whole, down_whole, qkv_whole, out_whole, sums_out, bias_out, qkv_hbm,
    in_weight, down_weight, context, log_total, segment, low_bias,
    in_term, down_term, qkv_term, out_term, weight_all,
    far, near, cross, sums, hid, gm2, act, slope, gpre, pbuf, grad_low,
    hidden_rows, normed_rows, inverse_rows, key_t, key_acc, value_acc, seg_col, out_wide,
    down_take, in_take, qkv_take, out_take, vec_values, vec_take, bias_values, bias_take,
    send_sem, recv_sem, batch_send, batch_recv, load_sem,
):
    place = lax.axis_index("tensor")
    batch_place = lax.axis_index("batch")
    batch_bits = lax.axis_size("batch").bit_length() - 1
    core_id = {"tensor": place ^ 1}
    chip_id = {"tensor": place ^ 2}
    share = input_grad.shape[1]
    rows_all = 4 * share

    def slot(buf, micro, index):
        start = (micro * 4 + index) * share
        if not isinstance(start, int):
            start = pl.multiple_of(start, share)
        return buf.at[pl.ds(start, share), :]

    def own_rows(buf, micro):
        start = micro * share
        if not isinstance(start, int):
            start = pl.multiple_of(start, share)
        return buf.at[pl.ds(start, share), :]

    def copy(src, dst, micro, phase, kind, target):
        index = (micro * 4 + phase) * 6 + kind
        return pltpu.make_async_remote_copy(
            src_ref=src,
            dst_ref=dst,
            send_sem=send_sem.at[index],
            recv_sem=recv_sem.at[index],
            device_id=target,
            device_id_type=MESH,
        )

    def far_copy(parts, micro, phase):
        return copy(slot(parts, micro, 3), own_rows(far, micro), micro, phase, 0, core_id)

    def near_copy(parts, micro, phase):
        return copy(slot(parts, micro, 1), own_rows(near, micro), micro, phase, 1, core_id)

    def cross_copy(micro, phase):
        return copy(own_rows(sums, micro), own_rows(cross, micro), micro, phase, 2, chip_id)

    def crossing_copy(buf, micro, phase):
        return copy(slot(buf, micro, 0), slot(buf, micro, 2), micro, phase, 3, chip_id)

    def beside_copy(buf, micro, phase):
        return copy(slot(buf, micro, 0), slot(buf, micro, 1), micro, phase, 4, core_id)

    def onward_copy(buf, micro, phase):
        return copy(slot(buf, micro, 2), slot(buf, micro, 3), micro, phase, 5, core_id)

    def scatter_start(parts, micro, phase):
        far_copy(parts, micro, phase).start()
        near_copy(parts, micro, phase).start()

    def scatter_mid(parts, micro, phase):
        far_copy(parts, micro, phase).wait_recv()
        own_rows(sums, micro)[...] = (
            slot(parts, micro, 2)[...].astype(F32) + own_rows(far, micro)[...].astype(F32)
        ).astype(BF)
        cross_copy(micro, phase).start()

    def scatter_end(parts, micro, phase):
        near_copy(parts, micro, phase).wait_recv()
        cross_copy(micro, phase).wait_recv()
        cross_copy(micro, phase).wait_send()
        return (
            slot(parts, micro, 0)[...].astype(F32)
            + own_rows(near, micro)[...].astype(F32)
            + own_rows(cross, micro)[...].astype(F32)
        )

    def scatter_drain(parts, micro, phase):
        far_copy(parts, micro, phase).wait_send()
        near_copy(parts, micro, phase).wait_send()

    def gather_start(buf, micro, phase):
        crossing_copy(buf, micro, phase).start()
        beside_copy(buf, micro, phase).start()

    def gather_step(buf, micro, phase, which):
        @pl.when(which == 1)
        def _():
            beside_copy(buf, micro, phase).wait_recv()

        @pl.when(which == 2)
        def _():
            crossing_copy(buf, micro, phase).wait_recv()
            onward_copy(buf, micro, phase).start()

        @pl.when(which == 3)
        def _():
            onward_copy(buf, micro, phase).wait_recv()

    def gather_drain(buf, micro, phase):
        crossing_copy(buf, micro, phase).wait_send()
        beside_copy(buf, micro, phase).wait_send()
        onward_copy(buf, micro, phase).wait_send()

    def vector(index):
        return vectors[index][...].reshape(1, -1)

    def tally(index, value):
        vec_values[index : index + 1, :] += jnp.sum(value, axis=0, keepdims=True)

    taken = []

    def load(src, dst):
        taken.append(0)
        handle = pltpu.make_async_copy(src, dst, load_sem.at[len(taken) - 1])
        handle.start()
        return handle

    def micro_block(micro):
        return pl.ds(micro * rows_all, rows_all)

    def alive_of(micro):
        return jnp.clip(quarters[micro] - place, 0, 1).astype(F32)

    first_row = pl.multiple_of(place * share, share)
    low_loads = [
        load(ref.at[lanes, :], gpre.at[start + 128 * kind : start + 128 * kind + size, :])
        for kind, ref in enumerate(low_hbm)
        for lanes, start, size in ((slice(0, 128), 0, 128), (slice(128, 192), 384, 64))
    ]
    micro_loads = [load(token_hbm.at[m], act.at[micro_block(m), :]) for m in range(2)]
    out_load = load(out_hbm, out_wide.at[0:192, :])
    row_loads = [
        load(token_hbm.at[m, pl.ds(first_row, share), :], slot(grad_low, m, 0))
        for m in range(2)
    ] + [load(cot_hbm.at[m, pl.ds(first_row, share), :], result.at[m]) for m in range(2)]
    weight_loads = [load(in_hbm, in_weight), load(down_hbm, down_weight)]
    late_loads = []
    for kind, ref in enumerate(low_hbm):
        late_loads.append(
            load(ref.at[0:128, :], weight_all.at[128 * kind : 128 * kind + 128, :])
        )
        late_loads.append(
            load(ref.at[128:192, :], weight_all.at[384 + 64 * kind : 448 + 64 * kind, :])
        )

    sems = (batch_send, batch_recv)
    up = tuple(range(batch_bits))
    turned = up[1:] + up[:1]
    stride = 2 * batch_bits
    chunks = []

    def chunk(term, first, count, order, give, give_at, take, take_at, whole):
        size = reduce_plan(count, order)[1]
        chunks.append(
            BatchSum(
                term, first, count, term.shape[1], order,
                give.at[give_at : give_at + size, :],
                take.at[take_at : take_at + size, :],
                whole, sems, len(chunks) * stride,
            )
        )
        return chunks[-1]

    small = reduce_plan(192, up)[1]
    named = {}

    def add_chunks(letter, count, term, give, give_at, take, whole):
        for k in range(count):
            name = letter + str(k)
            named[name] = chunk(
                term, 192 * k, 192, turned if name in Z_FIRST else up,
                *((slope, small * (4 + k)) if letter == "i" and k < 2 else (give, give_at + small * k)),
                take, small * k, whole,
            )

    add_chunks("d", 4, down_term, slope, 0, down_take, down_whole)
    add_chunks("i", 4, in_term, hid, small * 2, in_take, in_whole)
    add_chunks("q", 3, qkv_term, hid, 0, qkv_take, qkv_whole)
    add_chunks("o", 1, out_term, hid, small * 3, out_take, out_whole)
    batch_targets = [{"batch": batch_place ^ (1 << bit)} for bit in up]
    shared_sum = VectorSum(
        vec_values, vec_take, batch_targets + [core_id, chip_id], sems, 12 * stride
    )
    bias_sum = VectorSum(bias_values, bias_take, batch_targets, sems, 13 * stride + 2)

    barrier = pltpu.get_barrier_semaphore()
    partners = [core_id, chip_id] + batch_targets
    for target in partners:
        pl.semaphore_signal(barrier, inc=1, device_id=target, device_id_type=MESH)
    vec_values[0:8, :] = jnp.zeros((8, vec_values.shape[1]), F32)
    bias_values[0:8, :] = jnp.zeros((8, bias_values.shape[1]), F32)
    out_term[...] = jnp.zeros_like(out_term)
    out_wide[192:256, :] = jnp.zeros((64, out_wide.shape[1]), BF)
    weight_all[576:640, :] = jnp.zeros((64, weight_all.shape[1]), BF)
    pl.semaphore_wait(barrier, len(partners))

    def opening(micro):
        total = scatter_end(pbuf, micro, 0)
        hidden, normed, inverse = layer_norm(
            slot(grad_low, micro, 0)[...].astype(F32) + total + vector(0), vector(1), vector(2)
        )
        own_rows(hidden_rows, micro)[...] = hidden
        own_rows(normed_rows, micro)[...] = normed
        own_rows(inverse_rows, micro)[...] = jnp.broadcast_to(inverse, (share, 128))
        slot(hid, micro, 0)[...] = hidden.astype(BF)
        gather_start(hid, micro, 0)

    low_bias[...] = jnp.zeros_like(low_bias)
    for kind, ref in ((0, query_bias), (2, value_bias)):
        row = ref[...].reshape(1, -1)
        low_bias[0:1, 128 * kind : 128 * kind + 128] = row[:, 0:128]
        low_bias[0:1, 384 + 128 * kind : 448 + 128 * kind] = row[:, 128:192]
    for kind in range(3):
        gpre[448 + 128 * kind : 512 + 128 * kind, :] = jnp.zeros((64, gpre.shape[1]), BF)
    for handle in low_loads + micro_loads + [out_load] + row_loads:
        handle.wait()
    qkv, value_t = gm2, key_t

    def project(micro):
        def one(index, carry):
            at = pl.multiple_of(index * share, share)
            rows = pl.ds(pl.multiple_of(micro * rows_all + index * share, share), share)
            qkv[rows, :] = (back_dot(act[rows, :], gpre[0:768, :]) + low_bias[0:1, :]).astype(BF)
            for tile in range(2):
                value_t[128 * tile : 128 * tile + 128, pl.ds(at, share)] = jnp.transpose(
                    qkv[rows, tile_lanes(2, tile)]
                )
            return carry

        lax.fori_loop(0, 4, one, 0)
        ends = jnp.broadcast_to(lengths[micro], (8, rows_all))
        lane = lax.broadcasted_iota(jnp.int32, (8, rows_all), 1)
        shift = 1
        while shift < rows_all:
            ends = ends + jnp.where(lane >= shift, pltpu.roll(ends, shift, 1), 0)
            shift *= 2
        ends_col = column_of(ends[0:1, :].astype(F32))
        places = lax.broadcasted_iota(jnp.int32, (rows_all, rows_all), 1).astype(F32)
        count = jnp.sum(jnp.where(ends_col <= places, 1.0, 0.0), axis=0, keepdims=True)
        segment[pl.ds(pl.multiple_of(micro * 8, 8), 8), :] = jnp.broadcast_to(count, (8, rows_all))
        seg_col[...] = column_of(count)

    def attend(index, carry):
        micro, turn = index // 4, index % 4
        which = 3 - turn

        @pl.when(turn == 0)
        def _():
            project(micro)

        step = which ^ place
        block = pl.ds(pl.multiple_of(micro * rows_all, rows_all), rows_all)
        rows = pl.ds(pl.multiple_of(micro * rows_all + step * share, share), share)
        eight = pl.ds(pl.multiple_of(micro * 8, 8), 8)
        columns = pl.ds(pl.multiple_of(step * share, share), share)
        same = seg_col[...] == segment[eight, columns][0:1, :]
        outs = []
        logs = []
        for head in range(3):
            tile = head // 2
            query = qkv[rows, tile_lanes(0, tile)] * jnp.asarray(0.125, BF)
            query = lane_half(query, head % 2)
            keys = qkv[block, tile_lanes(1, tile)]
            scores = jnp.where(same, back_dot(keys, query), -1e30)
            top = jnp.max(scores, axis=0, keepdims=True)
            expo = jnp.exp(scores - top)
            total = jnp.sum(expo, axis=0, keepdims=True)
            probs = (expo * (1.0 / total)).astype(BF)
            outs.append(
                jnp.dot(
                    value_t[64 * head : 64 * head + 64, :], probs, preferred_element_type=F32
                )
            )
            logs.append(top + jnp.log(total))
        context_t = jnp.concatenate(outs, axis=0) * alive_of(micro)
        low = jnp.transpose(context_t).astype(BF)
        context[rows, :] = low
        log_total[eight, columns] = jnp.concatenate(logs + [jnp.zeros((5, share), F32)], axis=0)
        slot(pbuf, micro, which)[...] = jnp.dot(
            low, out_wide[0:192, :], preferred_element_type=F32
        ).astype(BF)

        @pl.when(turn == 0)
        def _():
            far_copy(pbuf, micro, 0).start()

        @pl.when(turn == 1)
        def _():
            scatter_mid(pbuf, micro, 0)

        @pl.when(turn == 2)
        def _():
            near_copy(pbuf, micro, 0).start()

        @pl.when(index == 4)
        def _():
            opening(0)

        return carry

    lax.fori_loop(0, 8, attend, 0)
    qkv_store = load(gm2, qkv_hbm)
    for handle in weight_loads:
        handle.wait()
    scatter_drain(pbuf, 0, 0)
    scatter_drain(pbuf, 1, 0)

    def forward(index, carry):
        micro, which = index // 4, index % 4
        gather_step(hid, micro, 0, which)
        pre = (
            jnp.dot(slot(hid, micro, which)[...], in_weight[...], preferred_element_type=F32)
            + vector(3)
        )
        alive = alive_of(micro)
        below = 0.5 * (1.0 + lax.erf(pre * ROOT_HALF)) * alive
        low = (pre * below).astype(BF)
        slot(act, micro, which)[...] = low
        slot(slope, micro, which)[...] = (
            below + pre * jnp.exp(-0.5 * pre * pre) * (DENSITY_SCALE * alive)
        ).astype(BF)
        slot(pbuf, micro, which)[...] = jnp.dot(
            low, down_weight[...], preferred_element_type=F32
        ).astype(BF)

        @pl.when(which == 3)
        def _():
            scatter_start(pbuf, micro, 1)

        @pl.when(index == 1)
        def _():
            opening(1)
            qkv_store.wait()

        @pl.when(index == 4)
        def _():
            scatter_mid(pbuf, 0, 1)

        return carry

    lax.fori_loop(0, 8, forward, 0)
    scatter_mid(pbuf, 1, 1)

    def middle(micro, carry):
        total = scatter_end(pbuf, micro, 1)
        final, normed, inverse = layer_norm(
            own_rows(hidden_rows, micro)[...] + total + vector(4), vector(5), vector(6)
        )
        grad_y = result[micro].astype(F32)
        result[micro] = final.astype(BF)
        grad_mid2 = norm_back(grad_y, normed, inverse, vector(5))
        own_rows(hidden_rows, micro)[...] = grad_mid2
        slot(gm2, micro, 0)[...] = grad_mid2.astype(BF)
        gather_start(gm2, micro, 1)
        tally(3, grad_mid2)
        tally(4, grad_y * normed)
        tally(5, grad_y)
        return carry

    lax.fori_loop(0, 2, middle, 0)
    for micro in range(2):
        scatter_drain(pbuf, micro, 1)

    def backward(index, carry):
        micro, which = index // 4, index % 4
        gather_step(gm2, micro, 1, which)
        grad_pre = (
            back_dot(slot(gm2, micro, which)[...], down_weight[...])
            * slot(slope, micro, which)[...].astype(F32)
        ).astype(BF)
        slot(gpre, micro, which)[...] = grad_pre
        tally(6, grad_pre.astype(F32))
        slot(pbuf, micro, which)[...] = back_dot(grad_pre, in_weight[...]).astype(BF)

        @pl.when(which == 3)
        def _():
            scatter_start(pbuf, micro, 2)

        @pl.when(index == 4)
        def _():
            scatter_mid(pbuf, 0, 2)

        return carry

    lax.fori_loop(0, 8, backward, 0)
    scatter_mid(pbuf, 1, 2)

    def weigh(left, right, out):
        def block(index, carry):
            lanes = pl.ds(pl.multiple_of(index * 256, 256), 256)
            out[lanes, :] = cross_dot(left[:, lanes], right[...])
            return carry

        lax.fori_loop(0, out.shape[0] // 256, block, 0)

    weigh(act, gm2, down_term)
    for k in range(4):
        named["d" + str(k)].advance(0)
    for micro in range(2):
        gather_drain(hid, micro, 0)
        gather_drain(gm2, micro, 1)
    late_loads.extend(
        load(token_hbm.at[m], act.at[micro_block(m), :]) for m in range(2)
    )
    late_loads.append(load(qkv_hbm, gm2))
    weigh(hid, gpre, in_term)
    for k in range(4):
        named["i" + str(k)].advance(0)

    def closing(micro):
        total = scatter_end(pbuf, micro, 2)
        grad_hidden = own_rows(hidden_rows, micro)[...] + total
        normed = own_rows(normed_rows, micro)[...]
        inverse = own_rows(inverse_rows, micro)[:, 0:1]
        grad = norm_back(grad_hidden, normed, inverse, vector(1))
        input_grad[micro] = grad
        slot(grad_low, micro, 0)[...] = grad.astype(BF)
        gather_start(grad_low, micro, 2)
        tally(0, grad)
        tally(1, grad_hidden * normed)
        tally(2, grad_hidden)

    reached = {name: 0 for name in named}
    reached["s"] = -1
    planned = {}
    for point in POINTS:
        planned[point] = []
        for name in EVENTS.get(point, ()):
            reached[name] += 1
            planned[point].append((name, reached[name]))

    def run(point):
        for name, step in planned[point]:
            (shared_sum if name == "s" else named[name]).advance(step)

    run("open")
    closing(0)
    run("closing")
    closing(1)
    for micro in range(2):
        scatter_drain(pbuf, micro, 2)
    run("closed")
    for handle in late_loads:
        handle.wait()
    qkv, tokens, grads = gm2, act, gpre

    def micro_rows(micro):
        return pl.ds(pl.multiple_of(micro * rows_all, rows_all), rows_all)

    def finish_grads(micro):
        block = micro_block(micro)
        grads[block, 128:256] = key_acc[:, 0:128].astype(BF)
        grads[block, 256:384] = value_acc[:, 0:128].astype(BF)
        grads[block, 448:512] = key_acc[:, 128:192].astype(BF)
        grads[block, 512:640] = value_acc[:, 128:256].astype(BF)
        bias_values[0:1, 0:640] += jnp.sum(
            grads[block, 0:640].astype(F32), axis=0, keepdims=True
        )


    def weigh_low(micro):
        block = micro_block(micro)
        for first, count in ((0, 256), (256, 256), (512, 64)):
            value = cross_dot(grads[block, first : first + count], tokens[block, :])
            if micro == 0:
                qkv_term[first : first + count, :] = value
            else:
                qkv_term[first : first + count, :] += value

    def send_input(micro):
        def send_slot(index, carry):
            start = pl.multiple_of(micro * rows_all + (index ^ place) * share, share)
            slot(pbuf, micro, index)[...] = jnp.dot(
                grads[pl.ds(start, share), 0:640], weight_all[...], preferred_element_type=F32
            ).astype(BF)
            return carry

        lax.fori_loop(0, 4, send_slot, 0)
        scatter_start(pbuf, micro, 3)

    def attend_back(index, carry):
        micro, which = index // 4, index % 4
        gather_step(grad_low, micro, 2, which)
        step = which ^ place
        block = micro_rows(micro)
        rows = pl.ds(pl.multiple_of(micro * rows_all + step * share, share), share)

        @pl.when(which == 0)
        def _():
            for tile in range(2):
                key_t[128 * tile : 128 * tile + 128, :] = jnp.transpose(
                    qkv[block, tile_lanes(1, tile)]
                )
            key_acc[...] = jnp.zeros_like(key_acc)
            value_acc[...] = jnp.zeros_like(value_acc)
            seg_col[...] = column_of(
                segment[pl.ds(pl.multiple_of(micro * 8, 8), 8), :][0:1, :]
            )

        eight = pl.ds(pl.multiple_of(micro * 8, 8), 8)
        columns = pl.ds(pl.multiple_of(step * share, share), share)
        seg_row = segment[eight, columns][0:1, :]
        logs = log_total[eight, columns]
        grad_slot = slot(grad_low, micro, which)[...]
        out_term[...] += cross_dot(context[rows, :], grad_slot)

        @pl.when(index == 7)
        def _():
            named["o0"].advance(0)

        alive = alive_of(micro).astype(BF)
        grad_context = back_dot(grad_slot, out_wide[...]).astype(BF) * alive
        same = seg_col[...] == seg_row
        query_parts = []
        for head in range(3):
            tile = head // 2
            lanes = slice(128 * tile, 128 * tile + 128)
            query = qkv[rows, tile_lanes(0, tile)] * jnp.asarray(0.125, BF)
            query = lane_half(query, head % 2)
            grad_tile = lane_half(grad_context[:, lanes], head % 2)
            keys = qkv[block, tile_lanes(1, tile)]
            values = qkv[block, tile_lanes(2, tile)]
            scores = jnp.where(same, back_dot(keys, query), -1e30)
            probs = jnp.exp(scores - logs[head : head + 1, :])
            grad_probs = back_dot(values, grad_tile)
            mean = jnp.sum(probs * grad_probs, axis=0, keepdims=True)
            grad_scores = (probs * (grad_probs - mean)).astype(BF)
            value_acc[:, lanes] += jnp.dot(
                probs.astype(BF), grad_tile, preferred_element_type=F32
            )
            key_acc[:, lanes] += jnp.dot(grad_scores, query, preferred_element_type=F32)
            query_parts.append(
                jnp.dot(
                    key_t[64 * head : 64 * head + 64, :],
                    grad_scores,
                    preferred_element_type=F32,
                )
            )
        query_t = jnp.concatenate(query_parts + [jnp.zeros((64, share), F32)], axis=0) * 0.125
        query_grad = jnp.transpose(query_t).astype(BF)
        grads[rows, 0:128] = query_grad[:, 0:128]
        grads[rows, 384:448] = query_grad[:, 128:192]

        for point in range(8):
            if planned[point]:

                @pl.when(index == point)
                def _():
                    run(point)

        @pl.when(index == 3)
        def _():
            finish_grads(0)
            send_input(0)
            run("between")
            weigh_low(0)
            run("weighed")

        @pl.when(index == 4)
        def _():
            scatter_mid(pbuf, 0, 3)

        return carry

    lax.fori_loop(0, 8, attend_back, 0)
    finish_grads(1)
    weigh_low(1)
    for k in range(3):
        named["q" + str(k)].advance(0)
    bias_sum.advance(0)
    run("start")
    send_input(1)
    run("pre")
    scatter_mid(pbuf, 1, 3)
    run("mid")

    def final_rows(micro):
        input_grad[micro] = input_grad[micro] + scatter_end(pbuf, micro, 3)

    final_rows(0)
    run("tail")
    final_rows(1)
    for index in range(1, batch_bits + 1):
        bias_sum.advance(index)
    run("end")
    for name in sorted(named):
        while reached[name] < named[name].last():
            reached[name] += 1
            named[name].advance(reached[name])
    while reached["s"] < batch_bits + 2:
        reached["s"] += 1
        shared_sum.advance(reached["s"])

    base = 8 * batch_bits
    sums_out[...] = vec_values[base + 16 : base + 24, :]
    sums_out[6:7, :] = vec_values[base + 6 : base + 7, :]
    bias_out[...] = bias_values[base : base + 8, :]
    for micro in range(2):
        scatter_drain(pbuf, micro, 3)
        gather_drain(grad_low, micro, 2)
    for owner in chunks + [shared_sum, bias_sum]:
        owner.drain()


def layer_call(
    quarters, tokens, cotangent, in_weight, down_weight, query_weight, key_weight, value_weight,
    out_weight, lengths, query_bias, value_bias, *vectors
):
    micro_count, rows_all, width = tokens.shape
    share = rows_all // 4
    rows = micro_count * rows_all
    units = in_weight.shape[1]
    batch_bits = lax.axis_size("batch").bit_length() - 1
    order = tuple(range(batch_bits))
    small = reduce_plan(192, order)[1]
    vmem = pl.BlockSpec(memory_space=pltpu.VMEM)
    hbm = pl.BlockSpec(memory_space=pl.ANY)
    smem = pl.BlockSpec(memory_space=pltpu.SMEM)
    batch_sems = 14 * 2 * batch_bits + 2
    return pl.pallas_call(
        layer_kernel,
        in_specs=[smem] + [hbm] * 8 + [vmem] * (3 + len(vectors)),
        out_specs=[vmem] * 8 + [hbm],
        out_shape=[
            jax.ShapeDtypeStruct((micro_count, share, width), BF),
            jax.ShapeDtypeStruct((micro_count, share, width), F32),
            jax.ShapeDtypeStruct((width, units), BF),
            jax.ShapeDtypeStruct((units, width), BF),
            jax.ShapeDtypeStruct((576, width), BF),
            jax.ShapeDtypeStruct((192, width), BF),
            jax.ShapeDtypeStruct((8, width), F32),
            jax.ShapeDtypeStruct((8, width), F32),
            jax.ShapeDtypeStruct((rows, 3 * WIDE), BF),
        ],
        scratch_shapes=[
            pltpu.VMEM((width, units), BF),
            pltpu.VMEM((units, width), BF),
            pltpu.VMEM((rows, 192), BF),
            pltpu.VMEM((8 * micro_count, rows_all), F32),
            pltpu.VMEM((8 * micro_count, rows_all), F32),
            pltpu.VMEM((8, 3 * WIDE), F32),
            pltpu.VMEM((width, units), F32),
            pltpu.VMEM((units, width), F32),
            pltpu.VMEM((576, width), F32),
            pltpu.VMEM((192, width), F32),
            pltpu.VMEM((640, width), BF),
            pltpu.VMEM((2 * share, width), BF),
            pltpu.VMEM((2 * share, width), BF),
            pltpu.VMEM((2 * share, width), BF),
            pltpu.VMEM((2 * share, width), BF),
            pltpu.VMEM((rows, width), BF),
            pltpu.VMEM((rows, width), BF),
            pltpu.VMEM((rows, units), BF),
            pltpu.VMEM((rows, units), BF),
            pltpu.VMEM((rows, units), BF),
            pltpu.VMEM((rows, width), BF),
            pltpu.VMEM((rows, width), BF),
            pltpu.VMEM((2 * share, width), F32),
            pltpu.VMEM((2 * share, width), F32),
            pltpu.VMEM((2 * share, 128), F32),
            pltpu.VMEM((WIDE, rows_all), BF),
            pltpu.VMEM((rows_all, WIDE), F32),
            pltpu.VMEM((rows_all, WIDE), F32),
            pltpu.VMEM((rows_all, 1), F32),
            pltpu.VMEM((WIDE, width), BF),
            pltpu.VMEM((4 * small, width), BF),
            pltpu.VMEM((4 * small, width), BF),
            pltpu.VMEM((3 * small, width), BF),
            pltpu.VMEM((small, width), BF),
            pltpu.VMEM((8 * (batch_bits + 3), width), F32),
            pltpu.VMEM((8 * (batch_bits + 2), width), F32),
            pltpu.VMEM((8 * (batch_bits + 1), width), F32),
            pltpu.VMEM((8 * batch_bits, width), F32),
            pltpu.SemaphoreType.DMA((48,)),
            pltpu.SemaphoreType.DMA((48,)),
            pltpu.SemaphoreType.DMA((batch_sems,)),
            pltpu.SemaphoreType.DMA((batch_sems,)),
            pltpu.SemaphoreType.DMA((32,)),
        ],
        compiler_params=pltpu.CompilerParams(
            collective_id=1, has_side_effects=True, vmem_limit_bytes=67_043_328
        ),
        name="layer",
    )(
        quarters, tokens, cotangent, in_weight, down_weight, query_weight, key_weight,
        value_weight, out_weight, lengths, query_bias, value_bias, *vectors
    )


def local(
    tokens,
    lengths,
    quarters,
    query_weight,
    query_bias,
    key_weight,
    value_weight,
    value_bias,
    out_weight,
    out_bias,
    norm1_gain,
    norm1_shift,
    in_weight,
    in_bias,
    down_weight,
    down_bias,
    norm2_gain,
    norm2_shift,
    cotangent,
):
    result, input_grad, in_sum, down_sum, packed, out_sum, sums, bias, _ = layer_call(
        quarters,
        tokens,
        cotangent,
        in_weight,
        down_weight,
        query_weight.T,
        key_weight.T,
        value_weight.T,
        out_weight,
        lengths.reshape(lengths.shape[0], 1, lengths.shape[2]),
        query_bias,
        value_bias,
        out_bias,
        norm1_gain,
        norm1_shift,
        in_bias,
        down_bias,
        norm2_gain,
        norm2_shift,
    )

    def joined(kind):
        return jnp.concatenate(
            [
                packed[128 * kind : 128 * kind + 128],
                packed[384 + 64 * kind : 448 + 64 * kind],
            ]
        ).astype(F32).T

    def joined_bias(kind):
        return jnp.concatenate(
            [
                bias[0, 128 * kind : 128 * kind + 128],
                bias[0, 384 + 64 * kind : 448 + 64 * kind],
            ]
        )

    return (
        result,
        input_grad,
        joined(0),
        joined_bias(0),
        joined(1),
        joined(2),
        joined_bias(2),
        out_sum.astype(F32),
        sums[0],
        sums[1],
        sums[2],
        in_sum.astype(F32),
        sums[6],
        down_sum.astype(F32),
        sums[3],
        sums[4],
        sums[5],
    )


def solution(mesh):
    in_specs = (
        P(None, "batch", None),
        P(None, "batch", None),
        P(),
        P(None, "tensor"),
        P("tensor"),
        P(None, "tensor"),
        P(None, "tensor"),
        P("tensor"),
        P("tensor", None),
        P(),
        P(),
        P(),
        P(None, "tensor"),
        P("tensor"),
        P("tensor", None),
        P(),
        P(),
        P(),
        P(None, "batch", None),
    )
    out_specs = (
        P(None, ("batch", "tensor"), None),
        P(None, ("batch", "tensor"), None),
        P(None, "tensor"),
        P("tensor"),
        P(None, "tensor"),
        P(None, "tensor"),
        P("tensor"),
        P("tensor", None),
        P(),
        P(),
        P(),
        P(None, "tensor"),
        P("tensor"),
        P("tensor", None),
        P(),
        P(),
        P(),
    )
    return jax.shard_map(local, mesh=mesh, in_specs=in_specs, out_specs=out_specs, check_vma=False)
```

```python
import functools

import jax
import jax.numpy as jnp
from jax import lax
from jax.experimental import pallas as pl
from jax.experimental.pallas import tpu as pltpu
from jax.sharding import PartitionSpec as P

HEADS = 12
HEAD_DIM = 64
FF = 3072
EPSILON = 1e-12
ROOT_HALF = 0.7071067811865476
DENSITY_SCALE = 0.3989422804014327
QB = 256
WIDE = 256

BF = jnp.bfloat16
F32 = jnp.float32
MESH = pl.DeviceIdType.MESH


def layer_norm(values_in, gain, shift):
    row_mean = jnp.mean(values_in, axis=-1, keepdims=True)
    centred = values_in - row_mean
    inverse = lax.rsqrt(jnp.mean(centred * centred, axis=-1, keepdims=True) + EPSILON)
    normed = centred * inverse
    return (normed * gain + shift, normed, inverse)


def norm_back(grad_in, normed, inverse, gain):
    spread = grad_in * gain
    return inverse * (
        spread
        - jnp.mean(spread, axis=-1, keepdims=True)
        - normed * jnp.mean(spread * normed, axis=-1, keepdims=True)
    )


def cross_dot(left, right):
    return lax.dot_general(left, right, (((0,), (0,)), ((), ())), preferred_element_type=F32)


def back_dot(left, right):
    return lax.dot_general(left, right, (((1,), (1,)), ((), ())), preferred_element_type=F32)


def lane_half(tile, which):
    lane = lax.broadcasted_iota(jnp.int32, tile.shape, 1)
    return jnp.where((lane >= HEAD_DIM) == (which == 1), tile, jnp.zeros_like(tile))


def tile_lanes(kind, tile):
    start = 128 * kind + 384 * tile
    return slice(start, start + 128)


def column_of(row):
    return jnp.transpose(jnp.broadcast_to(row, (8, row.shape[1])))[:, 0:1]


CHUNK = 48


def by_chunks(count, body):
    def one(index, carry):
        body(pl.multiple_of(index * CHUNK, CHUNK))
        return carry

    lax.fori_loop(0, count // CHUNK, one, 0)


def reduce_plan(rows, order):
    plan = []
    length, offset = rows, 0
    for index, bit in enumerate(order):
        halving = index < len(order) - 1 and length % (2 * CHUNK) == 0
        if halving:
            length //= 2
        plan.append((bit, halving, length, offset))
        offset += length
    return plan, offset


class BatchSum:
    def __init__(self, term, first, rows, columns, order, give, take, whole, sems, base):
        self.term, self.first, self.rows, self.columns = term, first, rows, columns
        self.give, self.take, self.whole = give, take, whole
        self.send_sem, self.recv_sem = sems
        self.base = base
        self.plan, _ = reduce_plan(rows, order)
        self.place = lax.axis_index("batch")
        self.starts = [0]
        for bit, halving, length, _ in self.plan:
            start = self.starts[-1]
            if halving:
                start = start + ((self.place >> bit) & 1) * length
            self.starts.append(start)

    def rows_at(self, ref, start, length, lift=0):
        return ref.at[pl.ds(pl.multiple_of(start + lift, CHUNK), length), 0 : self.columns]

    def copy(self, src, dst, index, bit):
        return pltpu.make_async_remote_copy(
            src_ref=src,
            dst_ref=dst,
            send_sem=self.send_sem.at[self.base + index],
            recv_sem=self.recv_sem.at[self.base + index],
            device_id={"batch": self.place ^ (1 << bit)},
            device_id_type=MESH,
        )

    def reduce_copy(self, step):
        bit, _, length, offset = self.plan[step]
        return self.copy(
            self.rows_at(self.give, offset, length),
            self.rows_at(self.take, offset, length),
            step,
            bit,
        )

    def reduce_start(self, step):
        bit, halving, length, offset = self.plan[step]
        start = self.starts[step]
        if halving:
            start = start + (1 - ((self.place >> bit) & 1)) * length

        def pack(at):
            self.rows_at(self.give, offset + at, CHUNK)[...] = self.rows_at(
                self.term, start + at, CHUNK, self.first
            )[...].astype(BF)

        by_chunks(length, pack)
        self.reduce_copy(step).start()

    def reduce_finish(self, step):
        _, halving, length, offset = self.plan[step]
        self.reduce_copy(step).wait_recv()
        start = self.starts[step + 1]

        def merge(at):
            mine = self.rows_at(self.term, start + at, CHUNK, self.first)
            got = self.rows_at(self.take, offset + at, CHUNK)[...].astype(F32)
            if halving:
                mine[...] = mine[...] + got
            else:
                mine[...] = self.rows_at(self.give, offset + at, CHUNK)[...].astype(F32) + got

        by_chunks(length, merge)

    def settle(self):
        length, start = self.plan[-1][2], self.starts[-1]

        def pack(at):
            self.rows_at(self.whole, start + at, CHUNK, self.first)[...] = self.rows_at(
                self.term, start + at, CHUNK, self.first
            )[...].astype(BF)

        by_chunks(length, pack)

    def gather_copy(self, step):
        bit, _, length, _ = self.plan[step]
        region = self.rows_at(self.whole, self.starts[step + 1], length, self.first)
        return self.copy(region, region, len(self.plan) + step, bit)

    def gather_start(self, step):
        if self.plan[step][1]:
            self.gather_copy(step).start()

    def gather_finish(self, step):
        if self.plan[step][1]:
            self.gather_copy(step).wait_recv()

    def last(self):
        return 2 * len(self.plan) - 1

    def advance(self, index):
        count = len(self.plan)
        if index == 0:
            self.reduce_start(0)
        elif index < count:
            self.reduce_finish(index - 1)
            self.reduce_start(index)
        elif index == count:
            self.reduce_finish(count - 1)
            self.settle()
            self.gather_start(count - 2)
        else:
            self.gather_finish(2 * count - 1 - index)
            if index < 2 * count - 1:
                self.gather_start(2 * count - 2 - index)

    def drain(self):
        for step in range(len(self.plan)):
            self.reduce_copy(step).wait_send()
            if self.plan[step][1]:
                self.gather_copy(step).wait_send()


class VectorSum:
    def __init__(self, values, take, targets, sems, base):
        self.values, self.take, self.targets = values, take, targets
        self.send_sem, self.recv_sem = sems
        self.base = base

    def at(self, ref, step):
        return ref.at[8 * step : 8 * step + 8, :]

    def copy(self, step):
        return pltpu.make_async_remote_copy(
            src_ref=self.at(self.values, step),
            dst_ref=self.at(self.take, step),
            send_sem=self.send_sem.at[self.base + step],
            recv_sem=self.recv_sem.at[self.base + step],
            device_id=self.targets[step],
            device_id_type=MESH,
        )

    def advance(self, index):
        if index > 0:
            self.copy(index - 1).wait_recv()
            self.at(self.values, index)[...] = (
                self.at(self.values, index - 1)[...] + self.at(self.take, index - 1)[...]
            )
        if index < len(self.targets):
            self.copy(index).start()

    def drain(self):
        for step in range(len(self.targets)):
            self.copy(step).wait_send()


EVENTS = {
    "closing": ("d0",),
    1: ("i1", "d1",),
    3: ("i3", "d2",),
    4: ("d0",),
    "closed": ("s", "d3", "i1", "d1",),
    7: ("i0", "i3",),
    8: ("d2",),
    9: ("s", "i2", "d0", "d3",),
    10: ("i1",),
    11: ("i3", "d1",),
    12: ("s", "i0",),
    13: ("d2",),
    14: ("i2",),
    15: ("s", "d0",),
    17: ("d3",),
    "between": ("i1", "d0", "i3", "d1",),
    18: ("s", "i0", "d2",),
    20: ("d1", "i2",),
    21: ("s", "d3",),
    22: ("d2", "i1",),
    "start": ("i3", "d3",),
    "pre": ("i0", "i2",),
    "tail": ("q0", "o0", "q1", "q0", "o0", "q2", "q1",),
    "end": (
        "q0", "i0", "q2", "q1", "i2", "q0", "o0", "q2", "q1", "q0",
        "q2", "o0", "q1", "q2", "o0",
    ),
}
Z_FIRST = ("i1", "i3", "o0",)
POINTS = (
    "open", "closing", *range(6), "closed", *range(6, 18), "between", "weighed",
    *range(18, 24), "start", "pre", "mid", "tail", "end",
)


def layer_kernel(
    quarters, token_hbm, cot_hbm, in_hbm, down_hbm, query_hbm, key_hbm, value_hbm, out_hbm,
    lengths, query_bias, value_bias, *rest
):
    layer_body(
        quarters, token_hbm, cot_hbm, in_hbm, down_hbm, (query_hbm, key_hbm, value_hbm), out_hbm,
        lengths, query_bias, value_bias, rest[:7], *rest[7:]
    )


def layer_body(
    quarters, token_hbm, cot_hbm, in_hbm, down_hbm, low_hbm, out_hbm, lengths, query_bias,
    value_bias, vectors,
    result, input_grad, in_whole, down_whole, qkv_whole, out_whole, sums_out, bias_out, qkv_hbm,
    in_weight, down_weight, context, log_total, segment, low_bias,
    in_term, down_term, qkv_term, out_term, weight_all,
    far, near, cross, sums, hid, gm2, act, slope, gpre, pbuf, grad_low,
    hidden_rows, normed_rows, inverse_rows, key_t, key_acc, value_acc, out_wide,
    down_take, in_take, qkv_take, out_take, vec_values, vec_take, bias_values, bias_take,
    send_sem, recv_sem, batch_send, batch_recv, load_sem,
):
    place = lax.axis_index("tensor")
    batch_place = lax.axis_index("batch")
    batch_bits = lax.axis_size("batch").bit_length() - 1
    core_id = {"tensor": place ^ 1}
    chip_id = {"tensor": place ^ 2}
    share = input_grad.shape[1]
    rows_all = 4 * share

    def slot(buf, micro, index):
        start = (micro * 4 + index) * share
        if not isinstance(start, int):
            start = pl.multiple_of(start, share)
        return buf.at[pl.ds(start, share), :]

    def own_rows(buf, micro):
        start = micro * share
        if not isinstance(start, int):
            start = pl.multiple_of(start, share)
        return buf.at[pl.ds(start, share), :]

    def copy(src, dst, micro, phase, kind, target):
        index = (micro * 4 + phase) * 6 + kind
        return pltpu.make_async_remote_copy(
            src_ref=src,
            dst_ref=dst,
            send_sem=send_sem.at[index],
            recv_sem=recv_sem.at[index],
            device_id=target,
            device_id_type=MESH,
        )

    def far_copy(parts, micro, phase):
        return copy(slot(parts, micro, 3), own_rows(far, micro), micro, phase, 0, core_id)

    def near_copy(parts, micro, phase):
        return copy(slot(parts, micro, 1), own_rows(near, micro), micro, phase, 1, core_id)

    def cross_copy(micro, phase):
        return copy(own_rows(sums, micro), own_rows(cross, micro), micro, phase, 2, chip_id)

    def crossing_copy(buf, micro, phase):
        return copy(slot(buf, micro, 0), slot(buf, micro, 2), micro, phase, 3, chip_id)

    def beside_copy(buf, micro, phase):
        return copy(slot(buf, micro, 0), slot(buf, micro, 1), micro, phase, 4, core_id)

    def onward_copy(buf, micro, phase):
        return copy(slot(buf, micro, 2), slot(buf, micro, 3), micro, phase, 5, core_id)

    def scatter_start(parts, micro, phase):
        far_copy(parts, micro, phase).start()
        near_copy(parts, micro, phase).start()

    def scatter_mid(parts, micro, phase):
        far_copy(parts, micro, phase).wait_recv()
        own_rows(sums, micro)[...] = (
            slot(parts, micro, 2)[...].astype(F32) + own_rows(far, micro)[...].astype(F32)
        ).astype(BF)
        cross_copy(micro, phase).start()

    def scatter_end(parts, micro, phase):
        near_copy(parts, micro, phase).wait_recv()
        cross_copy(micro, phase).wait_recv()
        cross_copy(micro, phase).wait_send()
        return (
            slot(parts, micro, 0)[...].astype(F32)
            + own_rows(near, micro)[...].astype(F32)
            + own_rows(cross, micro)[...].astype(F32)
        )

    def scatter_drain(parts, micro, phase):
        far_copy(parts, micro, phase).wait_send()
        near_copy(parts, micro, phase).wait_send()

    def gather_start(buf, micro, phase):
        crossing_copy(buf, micro, phase).start()
        beside_copy(buf, micro, phase).start()

    def gather_step(buf, micro, phase, which):
        @pl.when(which == 1)
        def _():
            beside_copy(buf, micro, phase).wait_recv()

        @pl.when(which == 2)
        def _():
            crossing_copy(buf, micro, phase).wait_recv()
            onward_copy(buf, micro, phase).start()

        @pl.when(which == 3)
        def _():
            onward_copy(buf, micro, phase).wait_recv()

    def gather_drain(buf, micro, phase):
        crossing_copy(buf, micro, phase).wait_send()
        beside_copy(buf, micro, phase).wait_send()
        onward_copy(buf, micro, phase).wait_send()

    def vector(index):
        return vectors[index][...].reshape(1, -1)

    def tally(index, value):
        vec_values[index : index + 1, :] += jnp.sum(value, axis=0, keepdims=True)

    taken = []

    def load(src, dst):
        taken.append(0)
        handle = pltpu.make_async_copy(src, dst, load_sem.at[len(taken) - 1])
        handle.start()
        return handle

    def micro_block(micro):
        return pl.ds(micro * rows_all, rows_all)

    def alive_of(micro):
        return jnp.clip(quarters[micro] - place, 0, 1).astype(F32)

    first_row = pl.multiple_of(place * share, share)
    low_loads = [
        load(ref.at[lanes, :], gpre.at[start + 128 * kind : start + 128 * kind + size, :])
        for kind, ref in enumerate(low_hbm)
        for lanes, start, size in ((slice(0, 128), 0, 128), (slice(128, 192), 384, 64))
    ]
    micro_loads = [load(token_hbm.at[m], act.at[micro_block(m), :]) for m in range(2)]
    out_load = load(out_hbm, out_wide.at[0:192, :])
    row_loads = [
        load(token_hbm.at[m, pl.ds(first_row, share), :], slot(grad_low, m, 0))
        for m in range(2)
    ] + [load(cot_hbm.at[m, pl.ds(first_row, share), :], result.at[m]) for m in range(2)]
    weight_loads = [load(in_hbm, in_weight), load(down_hbm, down_weight)]
    late_loads = []
    for kind, ref in enumerate(low_hbm):
        late_loads.append(
            load(ref.at[0:128, :], weight_all.at[128 * kind : 128 * kind + 128, :])
        )
        late_loads.append(
            load(ref.at[128:192, :], weight_all.at[384 + 64 * kind : 448 + 64 * kind, :])
        )

    sems = (batch_send, batch_recv)
    up = tuple(range(batch_bits))
    turned = up[1:] + up[:1]
    stride = 2 * batch_bits
    chunks = []

    def chunk(term, first, count, order, give, give_at, take, take_at, whole):
        size = reduce_plan(count, order)[1]
        chunks.append(
            BatchSum(
                term, first, count, term.shape[1], order,
                give.at[give_at : give_at + size, :],
                take.at[take_at : take_at + size, :],
                whole, sems, len(chunks) * stride,
            )
        )
        return chunks[-1]

    small = reduce_plan(192, up)[1]
    named = {}

    def add_chunks(letter, count, term, give, give_at, take, whole):
        for k in range(count):
            name = letter + str(k)
            named[name] = chunk(
                term, 192 * k, 192, turned if name in Z_FIRST else up,
                *((slope, small * (4 + k)) if letter == "i" and k < 2 else (give, give_at + small * k)),
                take, small * k, whole,
            )

    add_chunks("d", 4, down_term, slope, 0, down_take, down_whole)
    add_chunks("i", 4, in_term, hid, small * 2, in_take, in_whole)
    add_chunks("q", 3, qkv_term, hid, 0, qkv_take, qkv_whole)
    add_chunks("o", 1, out_term, hid, small * 3, out_take, out_whole)
    batch_targets = [{"batch": batch_place ^ (1 << bit)} for bit in up]
    shared_sum = VectorSum(
        vec_values, vec_take, batch_targets + [core_id, chip_id], sems, 12 * stride
    )
    bias_sum = VectorSum(bias_values, bias_take, batch_targets, sems, 13 * stride + 2)

    barrier = pltpu.get_barrier_semaphore()
    partners = [core_id, chip_id] + batch_targets
    for target in partners:
        pl.semaphore_signal(barrier, inc=1, device_id=target, device_id_type=MESH)
    vec_values[0:8, :] = jnp.zeros((8, vec_values.shape[1]), F32)
    bias_values[0:8, :] = jnp.zeros((8, bias_values.shape[1]), F32)
    out_term[...] = jnp.zeros_like(out_term)
    out_wide[192:256, :] = jnp.zeros((64, out_wide.shape[1]), BF)
    weight_all[576:640, :] = jnp.zeros((64, weight_all.shape[1]), BF)

    def opening(micro):
        total = scatter_end(pbuf, micro, 0)
        hidden, normed, inverse = layer_norm(
            slot(grad_low, micro, 0)[...].astype(F32) + total + vector(0), vector(1), vector(2)
        )
        own_rows(hidden_rows, micro)[...] = hidden
        own_rows(normed_rows, micro)[...] = normed
        own_rows(inverse_rows, micro)[...] = jnp.broadcast_to(inverse, (share, 128))
        slot(hid, micro, 0)[...] = hidden.astype(BF)
        gather_start(hid, micro, 0)

    low_bias[...] = jnp.zeros_like(low_bias)
    for kind, ref in ((0, query_bias), (2, value_bias)):
        row = ref[...].reshape(1, -1)
        low_bias[0:1, 128 * kind : 128 * kind + 128] = row[:, 0:128]
        low_bias[0:1, 384 + 128 * kind : 448 + 128 * kind] = row[:, 128:192]
    for kind in range(3):
        gpre[448 + 128 * kind : 512 + 128 * kind, :] = jnp.zeros((64, gpre.shape[1]), BF)
    def find_segments(micro, carry):
        ends = jnp.broadcast_to(lengths[micro], (8, rows_all))
        lane = lax.broadcasted_iota(jnp.int32, (8, rows_all), 1)
        shift = 1
        while shift < rows_all:
            ends = ends + jnp.where(lane >= shift, pltpu.roll(ends, shift, 1), 0)
            shift *= 2
        ends_col = column_of(ends[0:1, :].astype(F32))
        places = lax.broadcasted_iota(jnp.int32, (rows_all, rows_all), 1).astype(F32)
        count = jnp.sum(jnp.where(ends_col <= places, 1.0, 0.0), axis=0, keepdims=True)
        segment[pl.ds(pl.multiple_of(micro * 8, 8), 8), :] = jnp.broadcast_to(count, (8, rows_all))
        return carry

    lax.fori_loop(0, 2, find_segments, 0)
    pl.semaphore_wait(barrier, len(partners))
    for handle in low_loads + [micro_loads[0], out_load]:
        handle.wait()
    qkv, value_t = gm2, key_t

    def project(micro):
        def one(index, carry):
            at = pl.multiple_of(index * share, share)
            rows = pl.ds(pl.multiple_of(micro * rows_all + index * share, share), share)
            qkv[rows, :] = (back_dot(act[rows, :], gpre[0:768, :]) + low_bias[0:1, :]).astype(BF)
            for tile in range(2):
                value_t[128 * tile : 128 * tile + 128, pl.ds(at, share)] = jnp.transpose(
                    qkv[rows, tile_lanes(2, tile)]
                )
            return carry

        lax.fori_loop(0, 4, one, 0)

    def attend(index, carry):
        micro, turn = index // 4, index % 4
        which = 3 - turn

        @pl.when(index == 4)
        def _():
            micro_loads[1].wait()

        @pl.when(turn == 0)
        def _():
            project(micro)

        @pl.when(index == 4)
        def _():
            for handle in row_loads:
                handle.wait()
            opening(0)

        step = which ^ place
        block = pl.ds(pl.multiple_of(micro * rows_all, rows_all), rows_all)
        rows = pl.ds(pl.multiple_of(micro * rows_all + step * share, share), share)
        eight = pl.ds(pl.multiple_of(micro * 8, 8), 8)
        columns = pl.ds(pl.multiple_of(step * share, share), share)
        same = column_of(segment[eight, :][0:1, :]) == segment[eight, columns][0:1, :]
        outs = []
        logs = []
        for head in range(3):
            tile = head // 2
            query = qkv[rows, tile_lanes(0, tile)] * jnp.asarray(0.125, BF)
            query = lane_half(query, head % 2)
            keys = qkv[block, tile_lanes(1, tile)]
            scores = jnp.where(same, back_dot(keys, query), -1e30)
            top = jnp.max(scores, axis=0, keepdims=True)
            expo = jnp.exp(scores - top)
            total = jnp.sum(expo, axis=0, keepdims=True)
            probs = (expo * (1.0 / total)).astype(BF)
            outs.append(
                jnp.dot(
                    value_t[64 * head : 64 * head + 64, :], probs, preferred_element_type=F32
                )
            )
            logs.append(top + jnp.log(total))
        context_t = jnp.concatenate(outs, axis=0) * alive_of(micro)
        low = jnp.transpose(context_t).astype(BF)
        context[rows, :] = low
        log_total[eight, columns] = jnp.concatenate(logs + [jnp.zeros((5, share), F32)], axis=0)
        slot(pbuf, micro, which)[...] = jnp.dot(
            low, out_wide[0:192, :], preferred_element_type=F32
        ).astype(BF)

        @pl.when(turn == 0)
        def _():
            far_copy(pbuf, micro, 0).start()

        @pl.when(turn == 1)
        def _():
            scatter_mid(pbuf, micro, 0)

        @pl.when(turn == 2)
        def _():
            near_copy(pbuf, micro, 0).start()

        return carry

    lax.fori_loop(0, 8, attend, 0)
    qkv_store = load(gm2, qkv_hbm)
    for handle in weight_loads:
        handle.wait()
    scatter_drain(pbuf, 0, 0)
    scatter_drain(pbuf, 1, 0)

    def middle(micro):
        total = scatter_end(pbuf, micro, 1)
        final, normed, inverse = layer_norm(
            own_rows(hidden_rows, micro)[...] + total + vector(4), vector(5), vector(6)
        )
        grad_y = result[micro].astype(F32)
        result[micro] = final.astype(BF)
        grad_mid2 = norm_back(grad_y, normed, inverse, vector(5))
        own_rows(hidden_rows, micro)[...] = grad_mid2
        slot(gm2, micro, 0)[...] = grad_mid2.astype(BF)
        gather_start(gm2, micro, 1)
        tally(3, grad_mid2)
        tally(4, grad_y * normed)
        tally(5, grad_y)

    def forward(index, carry):
        micro, which = index // 4, index % 4

        @pl.when(index == 1)
        def _():
            qkv_store.wait()

        @pl.when(index == 4)
        def _():
            scatter_mid(pbuf, 0, 1)
            opening(1)

        @pl.when(index == 6)
        def _():
            middle(0)

        gather_step(hid, micro, 0, which)
        pre = (
            jnp.dot(slot(hid, micro, which)[...], in_weight[...], preferred_element_type=F32)
            + vector(3)
        )
        alive = alive_of(micro)
        below = 0.5 * (1.0 + lax.erf(pre * ROOT_HALF)) * alive
        low = (pre * below).astype(BF)
        slot(act, micro, which)[...] = low
        slot(slope, micro, which)[...] = (
            below + pre * jnp.exp(-0.5 * pre * pre) * (DENSITY_SCALE * alive)
        ).astype(BF)
        slot(pbuf, micro, which)[...] = jnp.dot(
            low, down_weight[...], preferred_element_type=F32
        ).astype(BF)

        @pl.when(which == 3)
        def _():
            scatter_start(pbuf, micro, 1)

        return carry

    lax.fori_loop(0, 8, forward, 0)
    scatter_mid(pbuf, 1, 1)
    scatter_drain(pbuf, 0, 1)

    def weigh(left, right, out, micro):
        rows = micro_block(micro)

        def block(index, carry):
            lanes = pl.ds(pl.multiple_of(index * 256, 256), 256)
            value = cross_dot(left[rows, lanes], right[rows, :])
            if micro == 0:
                out[lanes, :] = value
            else:
                out[lanes, :] += value
            return carry

        lax.fori_loop(0, out.shape[0] // 256, block, 0)

    def backward(index, carry):
        micro, which = index // 4, index % 4

        @pl.when(index == 4)
        def _():
            middle(1)
            scatter_drain(pbuf, 1, 1)
            scatter_mid(pbuf, 0, 2)
            weigh(act, gm2, down_term, 0)
            weigh(hid, gpre, in_term, 0)

        gather_step(gm2, micro, 1, which)
        grad_pre = (
            back_dot(slot(gm2, micro, which)[...], down_weight[...])
            * slot(slope, micro, which)[...].astype(F32)
        ).astype(BF)
        slot(gpre, micro, which)[...] = grad_pre
        tally(6, grad_pre.astype(F32))
        slot(pbuf, micro, which)[...] = back_dot(grad_pre, in_weight[...]).astype(BF)

        @pl.when(which == 3)
        def _():
            scatter_start(pbuf, micro, 2)

        return carry

    lax.fori_loop(0, 8, backward, 0)

    weigh(act, gm2, down_term, 1)
    for k in range(4):
        named["d" + str(k)].advance(0)
    scatter_mid(pbuf, 1, 2)
    for micro in range(2):
        gather_drain(hid, micro, 0)
        gather_drain(gm2, micro, 1)
    late_loads.extend(
        load(token_hbm.at[m], act.at[micro_block(m), :]) for m in range(2)
    )
    late_loads.append(load(qkv_hbm, gm2))
    weigh(hid, gpre, in_term, 1)
    for k in range(4):
        named["i" + str(k)].advance(0)

    def closing(micro):
        total = scatter_end(pbuf, micro, 2)
        grad_hidden = own_rows(hidden_rows, micro)[...] + total
        normed = own_rows(normed_rows, micro)[...]
        inverse = own_rows(inverse_rows, micro)[:, 0:1]
        grad = norm_back(grad_hidden, normed, inverse, vector(1))
        input_grad[micro] = grad
        slot(grad_low, micro, 0)[...] = grad.astype(BF)
        gather_start(grad_low, micro, 2)
        tally(0, grad)
        tally(1, grad_hidden * normed)
        tally(2, grad_hidden)

    reached = {name: 0 for name in named}
    reached["s"] = -1
    planned = {}
    for point in POINTS:
        planned[point] = []
        for name in EVENTS.get(point, ()):
            reached[name] += 1
            planned[point].append((name, reached[name]))

    def run(point):
        for name, step in planned[point]:
            (shared_sum if name == "s" else named[name]).advance(step)

    run("open")
    for handle in late_loads:
        handle.wait()
    closing(0)
    run("closing")
    qkv, tokens, grads = gm2, act, gpre

    def micro_rows(micro):
        return pl.ds(pl.multiple_of(micro * rows_all, rows_all), rows_all)

    def finish_grads(micro):
        block = micro_block(micro)
        grads[block, 128:256] = key_acc[block, 0:128].astype(BF)
        grads[block, 256:384] = value_acc[block, 0:128].astype(BF)
        grads[block, 448:512] = key_acc[block, 128:192].astype(BF)
        grads[block, 512:640] = value_acc[block, 128:256].astype(BF)
        bias_values[0:1, 0:640] += jnp.sum(
            grads[block, 0:640].astype(F32), axis=0, keepdims=True
        )


    def weigh_low(micro):
        block = micro_block(micro)
        for first, count in ((0, 256), (256, 256), (512, 64)):
            value = cross_dot(grads[block, first : first + count], tokens[block, :])
            if micro == 0:
                qkv_term[first : first + count, :] = value
            else:
                qkv_term[first : first + count, :] += value

    def send_input(micro):
        def send_slot(index, carry):
            start = pl.multiple_of(micro * rows_all + (index ^ place) * share, share)
            slot(pbuf, micro, index)[...] = jnp.dot(
                grads[pl.ds(start, share), 0:640], weight_all[...], preferred_element_type=F32
            ).astype(BF)
            return carry

        lax.fori_loop(0, 4, send_slot, 0)
        scatter_start(pbuf, micro, 3)

    def progress(index, head):
        for turn in range(8):
            if planned[3 * turn + head]:

                @pl.when(index == turn)
                def _():
                    run(3 * turn + head)

    def attend_back(index, carry):
        micro, which = (index // 2) % 2, (index // 4) * 2 + index % 2
        gather_step(grad_low, micro, 2, which)
        step = which ^ place
        block = micro_rows(micro)
        rows = pl.ds(pl.multiple_of(micro * rows_all + step * share, share), share)
        key_at = pl.multiple_of(micro * WIDE, WIDE)

        @pl.when(which == 0)
        def _():
            for tile in range(2):
                key_t[pl.ds(pl.multiple_of(key_at + 128 * tile, 128), 128), :] = jnp.transpose(
                    qkv[block, tile_lanes(1, tile)]
                )
            key_acc[block, :] = jnp.zeros((rows_all, WIDE), F32)
            value_acc[block, :] = jnp.zeros((rows_all, WIDE), F32)

        eight = pl.ds(pl.multiple_of(micro * 8, 8), 8)
        columns = pl.ds(pl.multiple_of(step * share, share), share)
        seg_row = segment[eight, columns][0:1, :]
        logs = log_total[eight, columns]
        grad_slot = slot(grad_low, micro, which)[...]
        out_term[...] += cross_dot(context[rows, :], grad_slot)

        @pl.when(index == 7)
        def _():
            named["o0"].advance(0)

        alive = alive_of(micro).astype(BF)
        grad_context = back_dot(grad_slot, out_wide[...]).astype(BF) * alive
        same = column_of(segment[eight, :][0:1, :]) == seg_row
        query_parts = []
        for head in range(3):
            tile = head // 2
            lanes = slice(128 * tile, 128 * tile + 128)
            query = qkv[rows, tile_lanes(0, tile)] * jnp.asarray(0.125, BF)
            query = lane_half(query, head % 2)
            grad_tile = lane_half(grad_context[:, lanes], head % 2)
            keys = qkv[block, tile_lanes(1, tile)]
            values = qkv[block, tile_lanes(2, tile)]
            scores = jnp.where(same, back_dot(keys, query), -1e30)
            probs = jnp.exp(scores - logs[head : head + 1, :])
            grad_probs = back_dot(values, grad_tile)
            mean = jnp.sum(probs * grad_probs, axis=0, keepdims=True)
            grad_scores = (probs * (grad_probs - mean)).astype(BF)
            value_acc[block, lanes] += jnp.dot(
                probs.astype(BF), grad_tile, preferred_element_type=F32
            )
            key_acc[block, lanes] += jnp.dot(grad_scores, query, preferred_element_type=F32)
            query_parts.append(
                jnp.dot(
                    key_t[pl.ds(pl.multiple_of(key_at + 64 * head, 64), 64), :],
                    grad_scores,
                    preferred_element_type=F32,
                )
            )
            if head < 2:
                progress(index, head)
        query_t = jnp.concatenate(query_parts + [jnp.zeros((64, share), F32)], axis=0) * 0.125
        query_grad = jnp.transpose(query_t).astype(BF)
        grads[rows, 0:128] = query_grad[:, 0:128]
        grads[rows, 384:448] = query_grad[:, 128:192]

        progress(index, 2)

        @pl.when(index == 1)
        def _():
            closing(1)
            run("closed")

        @pl.when(index == 5)
        def _():
            for micro in range(2):
                scatter_drain(pbuf, micro, 2)
            finish_grads(0)
            send_input(0)
            run("between")
            weigh_low(0)
            run("weighed")

        @pl.when(index == 6)
        def _():
            scatter_mid(pbuf, 0, 3)

        return carry

    lax.fori_loop(0, 8, attend_back, 0)
    finish_grads(1)
    weigh_low(1)
    for k in range(3):
        named["q" + str(k)].advance(0)
    bias_sum.advance(0)
    run("start")
    send_input(1)
    run("pre")
    scatter_mid(pbuf, 1, 3)
    run("mid")

    def final_rows(micro):
        input_grad[micro] = input_grad[micro] + scatter_end(pbuf, micro, 3)

    final_rows(0)
    run("tail")
    final_rows(1)
    for index in range(1, batch_bits + 1):
        bias_sum.advance(index)
    run("end")
    for name in sorted(named):
        while reached[name] < named[name].last():
            reached[name] += 1
            named[name].advance(reached[name])
    while reached["s"] < batch_bits + 2:
        reached["s"] += 1
        shared_sum.advance(reached["s"])

    base = 8 * batch_bits
    sums_out[...] = vec_values[base + 16 : base + 24, :]
    sums_out[6:7, :] = vec_values[base + 6 : base + 7, :]
    bias_out[...] = bias_values[base : base + 8, :]
    for micro in range(2):
        scatter_drain(pbuf, micro, 3)
        gather_drain(grad_low, micro, 2)
    for owner in chunks + [shared_sum, bias_sum]:
        owner.drain()


def layer_call(
    quarters, tokens, cotangent, in_weight, down_weight, query_weight, key_weight, value_weight,
    out_weight, lengths, query_bias, value_bias, *vectors
):
    micro_count, rows_all, width = tokens.shape
    share = rows_all // 4
    rows = micro_count * rows_all
    units = in_weight.shape[1]
    batch_bits = lax.axis_size("batch").bit_length() - 1
    order = tuple(range(batch_bits))
    small = reduce_plan(192, order)[1]
    vmem = pl.BlockSpec(memory_space=pltpu.VMEM)
    hbm = pl.BlockSpec(memory_space=pl.ANY)
    smem = pl.BlockSpec(memory_space=pltpu.SMEM)
    batch_sems = 14 * 2 * batch_bits + 2
    return pl.pallas_call(
        layer_kernel,
        in_specs=[smem] + [hbm] * 8 + [vmem] * (3 + len(vectors)),
        out_specs=[vmem] * 8 + [hbm],
        out_shape=[
            jax.ShapeDtypeStruct((micro_count, share, width), BF),
            jax.ShapeDtypeStruct((micro_count, share, width), F32),
            jax.ShapeDtypeStruct((width, units), BF),
            jax.ShapeDtypeStruct((units, width), BF),
            jax.ShapeDtypeStruct((576, width), BF),
            jax.ShapeDtypeStruct((192, width), BF),
            jax.ShapeDtypeStruct((8, width), F32),
            jax.ShapeDtypeStruct((8, width), F32),
            jax.ShapeDtypeStruct((rows, 3 * WIDE), BF),
        ],
        scratch_shapes=[
            pltpu.VMEM((width, units), BF),
            pltpu.VMEM((units, width), BF),
            pltpu.VMEM((rows, 192), BF),
            pltpu.VMEM((8 * micro_count, rows_all), F32),
            pltpu.VMEM((8 * micro_count, rows_all), F32),
            pltpu.VMEM((8, 3 * WIDE), F32),
            pltpu.VMEM((width, units), F32),
            pltpu.VMEM((units, width), F32),
            pltpu.VMEM((576, width), F32),
            pltpu.VMEM((192, width), F32),
            pltpu.VMEM((640, width), BF),
            pltpu.VMEM((2 * share, width), BF),
            pltpu.VMEM((2 * share, width), BF),
            pltpu.VMEM((2 * share, width), BF),
            pltpu.VMEM((2 * share, width), BF),
            pltpu.VMEM((rows, width), BF),
            pltpu.VMEM((rows, width), BF),
            pltpu.VMEM((rows, units), BF),
            pltpu.VMEM((rows, units), BF),
            pltpu.VMEM((rows, units), BF),
            pltpu.VMEM((rows, width), BF),
            pltpu.VMEM((rows, width), BF),
            pltpu.VMEM((2 * share, width), F32),
            pltpu.VMEM((2 * share, width), F32),
            pltpu.VMEM((2 * share, 128), F32),
            pltpu.VMEM((micro_count * WIDE, rows_all), BF),
            pltpu.VMEM((rows, WIDE), F32),
            pltpu.VMEM((rows, WIDE), F32),
            pltpu.VMEM((WIDE, width), BF),
            pltpu.VMEM((4 * small, width), BF),
            pltpu.VMEM((4 * small, width), BF),
            pltpu.VMEM((3 * small, width), BF),
            pltpu.VMEM((small, width), BF),
            pltpu.VMEM((8 * (batch_bits + 3), width), F32),
            pltpu.VMEM((8 * (batch_bits + 2), width), F32),
            pltpu.VMEM((8 * (batch_bits + 1), width), F32),
            pltpu.VMEM((8 * batch_bits, width), F32),
            pltpu.SemaphoreType.DMA((48,)),
            pltpu.SemaphoreType.DMA((48,)),
            pltpu.SemaphoreType.DMA((batch_sems,)),
            pltpu.SemaphoreType.DMA((batch_sems,)),
            pltpu.SemaphoreType.DMA((32,)),
        ],
        compiler_params=pltpu.CompilerParams(
            collective_id=1, has_side_effects=True, vmem_limit_bytes=67_043_328
        ),
        name="layer",
    )(
        quarters, tokens, cotangent, in_weight, down_weight, query_weight, key_weight,
        value_weight, out_weight, lengths, query_bias, value_bias, *vectors
    )


def finish_kernel(
    result_in, grad_in, in_low, down_low, packed, out_low, sums, bias,
    result, input_grad, query, query_bias, key, value, value_bias, out, out_bias, gain1, shift1,
    in_out, in_bias, down, down_bias, gain2, shift2,
    result_buf, grad_buf, in_buf, down_buf, packed_buf, out_buf, in_wide, down_wide, packed_wide,
    out_wide, sems,
):
    taken = []

    def move(src, dst):
        taken.append(0)
        handle = pltpu.make_async_copy(src, dst, sems.at[len(taken) - 1])
        handle.start()
        return handle

    inner = out_low.shape[0]
    low = (
        (in_low, in_buf, in_wide, ((0, in_low.shape[0], in_out, 0),)),
        (down_low, down_buf, down_wide, ((0, down_low.shape[0], down, 0),)),
        (
            packed, packed_buf, packed_wide,
            tuple(
                part
                for kind, ref in enumerate((query, key, value))
                for part in ((128 * kind, 128, ref, 0), (384 + 64 * kind, 64, ref, 128))
            ),
        ),
        (out_low, out_buf, out_wide, ((0, inner, out, 0),)),
    )
    loads = [move(src, buf) for src, buf, _, _ in low]
    through = [(move(grad_in, grad_buf), grad_buf, input_grad)]
    through.append((move(result_in, result_buf), result_buf, result))
    stores = []
    for load, (_, buf, wide, parts) in zip(loads, low):
        load.wait()
        wide[...] = buf[...].astype(F32)
        for start, size, ref, at in parts:
            stores.append(move(wide.at[start : start + size, :], ref.at[at : at + size, :]))
    for load, buf, ref in through:
        load.wait()
        stores.append(move(buf, ref))
    for index, ref in ((0, out_bias), (1, gain1), (2, shift1), (3, down_bias), (4, gain2), (5, shift2), (6, in_bias)):
        ref[...] = sums[index, :]
    for kind, ref in ((0, query_bias), (2, value_bias)):
        row = bias[0:1, 128 * kind : 128 * kind + 128]
        tail = bias[0:1, 384 + 64 * kind : 448 + 64 * kind]
        ref[...] = jnp.concatenate([row, tail], axis=1).reshape(inner)
    for store in stores:
        store.wait()


def finish(result, input_grad, in_sum, down_sum, packed, out_sum, sums, bias):
    width, units = in_sum.shape
    inner = out_sum.shape[0]
    hbm = pl.BlockSpec(memory_space=pl.ANY)
    vmem = pl.BlockSpec(memory_space=pltpu.VMEM)
    shape = jax.ShapeDtypeStruct
    wide = shape((inner, width), F32)
    row = shape((width,), F32)
    short = shape((inner,), F32)
    outs = pl.pallas_call(
        finish_kernel,
        in_specs=[hbm] * 6 + [vmem] * 2,
        out_specs=[
            hbm, hbm, hbm, vmem, hbm, hbm, vmem, hbm, vmem, vmem, vmem, hbm, vmem, hbm, vmem,
            vmem, vmem,
        ],
        out_shape=[
            shape(result.shape, BF), shape(input_grad.shape, F32), wide, short, wide, wide,
            short, wide, row, row, row, shape((width, units), F32), shape((units,), F32),
            shape((units, width), F32), row, row, row,
        ],
        scratch_shapes=[
            pltpu.VMEM(result.shape, BF),
            pltpu.VMEM(input_grad.shape, F32),
            pltpu.VMEM(in_sum.shape, BF),
            pltpu.VMEM(down_sum.shape, BF),
            pltpu.VMEM(packed.shape, BF),
            pltpu.VMEM(out_sum.shape, BF),
            pltpu.VMEM(in_sum.shape, F32),
            pltpu.VMEM(down_sum.shape, F32),
            pltpu.VMEM(packed.shape, F32),
            pltpu.VMEM(out_sum.shape, F32),
            pltpu.SemaphoreType.DMA((18,)),
        ],
        compiler_params=pltpu.CompilerParams(vmem_limit_bytes=67_043_328),
        name="finish",
    )(result, input_grad, in_sum, down_sum, packed, out_sum, sums, bias)
    outs = list(outs)
    for index in (2, 4, 5):
        outs[index] = outs[index].T
    return tuple(outs)


def local(
    tokens,
    lengths,
    quarters,
    query_weight,
    query_bias,
    key_weight,
    value_weight,
    value_bias,
    out_weight,
    out_bias,
    norm1_gain,
    norm1_shift,
    in_weight,
    in_bias,
    down_weight,
    down_bias,
    norm2_gain,
    norm2_shift,
    cotangent,
):
    result, input_grad, in_sum, down_sum, packed, out_sum, sums, bias, _ = layer_call(
        quarters,
        tokens,
        cotangent,
        in_weight,
        down_weight,
        query_weight.T,
        key_weight.T,
        value_weight.T,
        out_weight,
        lengths.reshape(lengths.shape[0], 1, lengths.shape[2]),
        query_bias,
        value_bias,
        out_bias,
        norm1_gain,
        norm1_shift,
        in_bias,
        down_bias,
        norm2_gain,
        norm2_shift,
    )

    return finish(result, input_grad, in_sum, down_sum, packed, out_sum, sums, bias)


def solution(mesh):
    in_specs = (
        P(None, "batch", None),
        P(None, "batch", None),
        P(),
        P(None, "tensor"),
        P("tensor"),
        P(None, "tensor"),
        P(None, "tensor"),
        P("tensor"),
        P("tensor", None),
        P(),
        P(),
        P(),
        P(None, "tensor"),
        P("tensor"),
        P("tensor", None),
        P(),
        P(),
        P(),
        P(None, "batch", None),
    )
    out_specs = (
        P(None, ("batch", "tensor"), None),
        P(None, ("batch", "tensor"), None),
        P(None, "tensor"),
        P("tensor"),
        P(None, "tensor"),
        P(None, "tensor"),
        P("tensor"),
        P("tensor", None),
        P(),
        P(),
        P(),
        P(None, "tensor"),
        P("tensor"),
        P("tensor", None),
        P(),
        P(),
        P(),
    )
    return jax.shard_map(local, mesh=mesh, in_specs=in_specs, out_specs=out_specs, check_vma=False)
```

```python
import functools

import jax
import jax.numpy as jnp
from jax import lax
from jax.experimental import pallas as pl
from jax.experimental.pallas import tpu as pltpu
from jax.sharding import PartitionSpec as P

HEADS = 12
HEAD_DIM = 64
FF = 3072
EPSILON = 1e-12
ROOT_HALF = 0.7071067811865476
DENSITY_SCALE = 0.3989422804014327
QB = 256
WIDE = 256

BF = jnp.bfloat16
F32 = jnp.float32
MESH = pl.DeviceIdType.MESH


def layer_norm(values_in, gain, shift):
    row_mean = jnp.mean(values_in, axis=-1, keepdims=True)
    centred = values_in - row_mean
    inverse = lax.rsqrt(jnp.mean(centred * centred, axis=-1, keepdims=True) + EPSILON)
    normed = centred * inverse
    return (normed * gain + shift, normed, inverse)


def norm_back(grad_in, normed, inverse, gain):
    spread = grad_in * gain
    return inverse * (
        spread
        - jnp.mean(spread, axis=-1, keepdims=True)
        - normed * jnp.mean(spread * normed, axis=-1, keepdims=True)
    )


def cross_dot(left, right):
    return lax.dot_general(left, right, (((0,), (0,)), ((), ())), preferred_element_type=F32)


def back_dot(left, right):
    return lax.dot_general(left, right, (((1,), (1,)), ((), ())), preferred_element_type=F32)


def lane_half(tile, which):
    lane = lax.broadcasted_iota(jnp.int32, tile.shape, 1)
    return jnp.where((lane >= HEAD_DIM) == (which == 1), tile, jnp.zeros_like(tile))


def tile_lanes(kind, tile):
    start = 128 * kind + 384 * tile
    return slice(start, start + 128)


def column_of(row):
    return jnp.transpose(jnp.broadcast_to(row, (8, row.shape[1])))[:, 0:1]


CHUNK = 48


def by_chunks(count, body):
    def one(index, carry):
        body(pl.multiple_of(index * CHUNK, CHUNK))
        return carry

    lax.fori_loop(0, count // CHUNK, one, 0)


def reduce_plan(rows, order):
    plan = []
    length, offset = rows, 0
    for index, bit in enumerate(order):
        halving = index < len(order) - 1 and length % (2 * CHUNK) == 0
        if halving:
            length //= 2
        plan.append((bit, halving, length, offset))
        offset += length
    return plan, offset


class BatchSum:
    def __init__(self, term, first, rows, columns, order, give, take, whole, sems, base):
        self.term, self.first, self.rows, self.columns = term, first, rows, columns
        self.give, self.take, self.whole = give, take, whole
        self.send_sem, self.recv_sem = sems
        self.base = base
        self.plan, _ = reduce_plan(rows, order)
        self.place = lax.axis_index("batch")
        self.starts = [0]
        for bit, halving, length, _ in self.plan:
            start = self.starts[-1]
            if halving:
                start = start + ((self.place >> bit) & 1) * length
            self.starts.append(start)

    def rows_at(self, ref, start, length, lift=0):
        return ref.at[pl.ds(pl.multiple_of(start + lift, CHUNK), length), 0 : self.columns]

    def copy(self, src, dst, index, bit):
        return pltpu.make_async_remote_copy(
            src_ref=src,
            dst_ref=dst,
            send_sem=self.send_sem.at[self.base + index],
            recv_sem=self.recv_sem.at[self.base + index],
            device_id={"batch": self.place ^ (1 << bit)},
            device_id_type=MESH,
        )

    def reduce_copy(self, step):
        bit, _, length, offset = self.plan[step]
        return self.copy(
            self.rows_at(self.give, offset, length),
            self.rows_at(self.take, offset, length),
            step,
            bit,
        )

    def reduce_start(self, step):
        bit, halving, length, offset = self.plan[step]
        start = self.starts[step]
        if halving:
            start = start + (1 - ((self.place >> bit) & 1)) * length

        def pack(at):
            self.rows_at(self.give, offset + at, CHUNK)[...] = self.rows_at(
                self.term, start + at, CHUNK, self.first
            )[...].astype(BF)

        by_chunks(length, pack)
        self.reduce_copy(step).start()

    def reduce_finish(self, step):
        _, halving, length, offset = self.plan[step]
        self.reduce_copy(step).wait_recv()
        start = self.starts[step + 1]

        def merge(at):
            mine = self.rows_at(self.term, start + at, CHUNK, self.first)
            got = self.rows_at(self.take, offset + at, CHUNK)[...].astype(F32)
            if halving:
                mine[...] = mine[...] + got
            else:
                mine[...] = self.rows_at(self.give, offset + at, CHUNK)[...].astype(F32) + got

        by_chunks(length, merge)

    def settle(self):
        length, start = self.plan[-1][2], self.starts[-1]

        def pack(at):
            self.rows_at(self.whole, start + at, CHUNK, self.first)[...] = self.rows_at(
                self.term, start + at, CHUNK, self.first
            )[...].astype(BF)

        by_chunks(length, pack)

    def gather_copy(self, step):
        bit, _, length, _ = self.plan[step]
        region = self.rows_at(self.whole, self.starts[step + 1], length, self.first)
        return self.copy(region, region, len(self.plan) + step, bit)

    def gather_start(self, step):
        if self.plan[step][1]:
            self.gather_copy(step).start()

    def gather_finish(self, step):
        if self.plan[step][1]:
            self.gather_copy(step).wait_recv()

    def last(self):
        return 2 * len(self.plan) - 1

    def advance(self, index):
        count = len(self.plan)
        if index == 0:
            self.reduce_start(0)
        elif index < count:
            self.reduce_finish(index - 1)
            self.reduce_start(index)
        elif index == count:
            self.reduce_finish(count - 1)
            self.settle()
            self.gather_start(count - 2)
        else:
            self.gather_finish(2 * count - 1 - index)
            if index < 2 * count - 1:
                self.gather_start(2 * count - 2 - index)

    def drain(self):
        for step in range(len(self.plan)):
            self.reduce_copy(step).wait_send()
            if self.plan[step][1]:
                self.gather_copy(step).wait_send()


class VectorSum:
    def __init__(self, values, take, targets, sems, base):
        self.values, self.take, self.targets = values, take, targets
        self.send_sem, self.recv_sem = sems
        self.base = base

    def at(self, ref, step):
        return ref.at[8 * step : 8 * step + 8, :]

    def copy(self, step):
        return pltpu.make_async_remote_copy(
            src_ref=self.at(self.values, step),
            dst_ref=self.at(self.take, step),
            send_sem=self.send_sem.at[self.base + step],
            recv_sem=self.recv_sem.at[self.base + step],
            device_id=self.targets[step],
            device_id_type=MESH,
        )

    def advance(self, index):
        if index > 0:
            self.copy(index - 1).wait_recv()
            self.at(self.values, index)[...] = (
                self.at(self.values, index - 1)[...] + self.at(self.take, index - 1)[...]
            )
        if index < len(self.targets):
            self.copy(index).start()

    def drain(self):
        for step in range(len(self.targets)):
            self.copy(step).wait_send()


EVENTS = {
    0: ("d0",),
    2: ("i1", "d1",),
    4: ("i3", "d2",),
    5: ("d0",),
    "closed": ("s", "d3",),
    6: ("i1", "d1",),
    8: ("i0", "i3",),
    9: ("s", "d2",),
    10: ("i2", "d0", "d3",),
    11: ("i1",),
    12: ("s", "i3", "d1", "i0",),
    14: ("d2",),
    15: ("s", "i2", "d0",),
    "between": ("d3", "i1", "d0",),
    "weighed": ("d1", "i3",),
    18: ("s",),
    19: ("d2",),
    20: ("i0",),
    21: ("s", "d3", "i2", "d1",),
    23: ("i1",),
    "start": ("d2", "i3",),
    "pre": ("d3", "i0",),
    "tail": ("o0", "q0", "i2", "q1", "q0", "o0", "q2", "q1",),
    "end": (
        "i0", "q2", "q0", "i2", "q1", "o0", "q0", "q2", "q1", "o0",
        "q0", "q2", "q1", "o0", "q2",
    ),
}
Z_FIRST = ("i1", "i3", "o0",)
POINTS = (
    "open", "closing", *range(6), "closed", *range(6, 18), "between", "weighed",
    *range(18, 24), "start", "pre", "mid", "tail", "end",
)


def layer_kernel(
    quarters, token_hbm, cot_hbm, in_hbm, down_hbm, query_hbm, key_hbm, value_hbm, out_hbm,
    lengths, query_bias, value_bias, *rest
):
    layer_body(
        quarters, token_hbm, cot_hbm, in_hbm, down_hbm, (query_hbm, key_hbm, value_hbm), out_hbm,
        lengths, query_bias, value_bias, rest[:7], *rest[7:]
    )


def layer_body(
    quarters, token_hbm, cot_hbm, in_hbm, down_hbm, low_hbm, out_hbm, lengths, query_bias,
    value_bias, vectors,
    result_hbm, input_hbm, in_out, down_out, qkv_out, out_out, sums_out, bias_out, qkv_hbm,
    result, input_grad, in_whole, down_whole, qkv_whole, out_whole,
    in_weight, down_weight, context, log_total, segment, low_bias,
    in_term, down_term, qkv_term, out_term, weight_all,
    far, near, cross, sums, hid, gm2, act, slope, gpre, pbuf, grad_low,
    hidden_rows, normed_rows, inverse_rows, key_t, key_acc, value_acc, out_wide,
    down_take, in_take, qkv_take, out_take, vec_values, vec_take, bias_values, bias_take,
    send_sem, recv_sem, batch_send, batch_recv, load_sem,
):
    place = lax.axis_index("tensor")
    batch_place = lax.axis_index("batch")
    batch_bits = lax.axis_size("batch").bit_length() - 1
    core_id = {"tensor": place ^ 1}
    chip_id = {"tensor": place ^ 2}
    share = input_grad.shape[1]
    rows_all = 4 * share

    def slot(buf, micro, index):
        start = (micro * 4 + index) * share
        if not isinstance(start, int):
            start = pl.multiple_of(start, share)
        return buf.at[pl.ds(start, share), :]

    def own_rows(buf, micro):
        start = micro * share
        if not isinstance(start, int):
            start = pl.multiple_of(start, share)
        return buf.at[pl.ds(start, share), :]

    def copy(src, dst, micro, phase, kind, target):
        index = (micro * 4 + phase) * 6 + kind
        return pltpu.make_async_remote_copy(
            src_ref=src,
            dst_ref=dst,
            send_sem=send_sem.at[index],
            recv_sem=recv_sem.at[index],
            device_id=target,
            device_id_type=MESH,
        )

    def far_copy(parts, micro, phase):
        return copy(slot(parts, micro, 3), own_rows(far, micro), micro, phase, 0, core_id)

    def near_copy(parts, micro, phase):
        return copy(slot(parts, micro, 1), own_rows(near, micro), micro, phase, 1, core_id)

    def cross_copy(micro, phase):
        return copy(own_rows(sums, micro), own_rows(cross, micro), micro, phase, 2, chip_id)

    def crossing_copy(buf, micro, phase):
        return copy(slot(buf, micro, 0), slot(buf, micro, 2), micro, phase, 3, chip_id)

    def beside_copy(buf, micro, phase):
        return copy(slot(buf, micro, 0), slot(buf, micro, 1), micro, phase, 4, core_id)

    def onward_copy(buf, micro, phase):
        return copy(slot(buf, micro, 2), slot(buf, micro, 3), micro, phase, 5, core_id)

    def scatter_start(parts, micro, phase):
        far_copy(parts, micro, phase).start()
        near_copy(parts, micro, phase).start()

    def scatter_mid(parts, micro, phase):
        far_copy(parts, micro, phase).wait_recv()
        own_rows(sums, micro)[...] = (
            slot(parts, micro, 2)[...].astype(F32) + own_rows(far, micro)[...].astype(F32)
        ).astype(BF)
        cross_copy(micro, phase).start()

    def scatter_end(parts, micro, phase):
        near_copy(parts, micro, phase).wait_recv()
        cross_copy(micro, phase).wait_recv()
        cross_copy(micro, phase).wait_send()
        return (
            slot(parts, micro, 0)[...].astype(F32)
            + own_rows(near, micro)[...].astype(F32)
            + own_rows(cross, micro)[...].astype(F32)
        )

    def scatter_drain(parts, micro, phase):
        far_copy(parts, micro, phase).wait_send()
        near_copy(parts, micro, phase).wait_send()

    def gather_start(buf, micro, phase):
        crossing_copy(buf, micro, phase).start()
        beside_copy(buf, micro, phase).start()

    def gather_step(buf, micro, phase, which):
        @pl.when(which == 1)
        def _():
            beside_copy(buf, micro, phase).wait_recv()

        @pl.when(which == 2)
        def _():
            crossing_copy(buf, micro, phase).wait_recv()
            onward_copy(buf, micro, phase).start()

        @pl.when(which == 3)
        def _():
            onward_copy(buf, micro, phase).wait_recv()

    def gather_drain(buf, micro, phase):
        crossing_copy(buf, micro, phase).wait_send()
        beside_copy(buf, micro, phase).wait_send()
        onward_copy(buf, micro, phase).wait_send()

    def vector(index):
        return vectors[index][...].reshape(1, -1)

    def tally(index, value):
        vec_values[index : index + 1, :] += jnp.sum(value, axis=0, keepdims=True)

    taken = []

    def load(src, dst):
        taken.append(0)
        handle = pltpu.make_async_copy(src, dst, load_sem.at[len(taken) - 1])
        handle.start()
        return handle

    def micro_block(micro):
        return pl.ds(micro * rows_all, rows_all)

    def alive_of(micro):
        return jnp.clip(quarters[micro] - place, 0, 1).astype(F32)

    first_row = pl.multiple_of(place * share, share)
    low_loads = [
        load(ref.at[lanes, :], gpre.at[start + 128 * kind : start + 128 * kind + size, :])
        for kind, ref in enumerate(low_hbm)
        for lanes, start, size in ((slice(0, 128), 0, 128), (slice(128, 192), 384, 64))
    ]
    micro_loads = [load(token_hbm.at[m], act.at[micro_block(m), :]) for m in range(2)]
    out_load = load(out_hbm, out_wide.at[0:192, :])
    row_loads = [
        load(token_hbm.at[m, pl.ds(first_row, share), :], slot(grad_low, m, 0))
        for m in range(2)
    ] + [load(cot_hbm.at[m, pl.ds(first_row, share), :], result.at[m]) for m in range(2)]
    weight_loads = [load(in_hbm, in_weight), load(down_hbm, down_weight)]
    late_loads = []
    for kind, ref in enumerate(low_hbm):
        late_loads.append(
            load(ref.at[0:128, :], weight_all.at[128 * kind : 128 * kind + 128, :])
        )
        late_loads.append(
            load(ref.at[128:192, :], weight_all.at[384 + 64 * kind : 448 + 64 * kind, :])
        )

    sems = (batch_send, batch_recv)
    up = tuple(range(batch_bits))
    turned = up[1:] + up[:1]
    stride = 2 * batch_bits
    chunks = []

    def chunk(term, first, count, order, give, give_at, take, take_at, whole, home):
        size = reduce_plan(count, order)[1]
        chunks.append(
            BatchSum(
                term, first, count, term.shape[1], order,
                give.at[give_at : give_at + size, :],
                take.at[take_at : take_at + size, :],
                whole, sems, len(chunks) * stride,
            )
        )
        chunks[-1].home = pltpu.make_async_copy(
            whole.at[first : first + count, :],
            home.at[first : first + count, :],
            load_sem.at[40 + len(chunks)],
        )
        return chunks[-1]

    small = reduce_plan(192, up)[1]
    named = {}

    def add_chunks(letter, count, term, give, give_at, take, whole, home):
        for k in range(count):
            name = letter + str(k)
            named[name] = chunk(
                term, 192 * k, 192, turned if name in Z_FIRST else up,
                *((slope, small * (4 + k)) if letter == "i" and k < 2 else (give, give_at + small * k)),
                take, small * k, whole, home,
            )

    add_chunks("d", 4, down_term, slope, 0, down_take, down_whole, down_out)
    add_chunks("i", 4, in_term, hid, small * 2, in_take, in_whole, in_out)
    add_chunks("q", 3, qkv_term, hid, 0, qkv_take, qkv_whole, qkv_out)
    add_chunks("o", 1, out_term, hid, small * 3, out_take, out_whole, out_out)
    batch_targets = [{"batch": batch_place ^ (1 << bit)} for bit in up]
    shared_sum = VectorSum(
        vec_values, vec_take, batch_targets + [core_id, chip_id], sems, 12 * stride
    )
    bias_sum = VectorSum(bias_values, bias_take, batch_targets, sems, 13 * stride + 2)

    barrier = pltpu.get_barrier_semaphore()
    partners = [core_id, chip_id] + batch_targets
    for target in partners:
        pl.semaphore_signal(barrier, inc=1, device_id=target, device_id_type=MESH)
    vec_values[0:8, :] = jnp.zeros((8, vec_values.shape[1]), F32)
    bias_values[0:8, :] = jnp.zeros((8, bias_values.shape[1]), F32)
    out_term[...] = jnp.zeros_like(out_term)
    out_wide[192:256, :] = jnp.zeros((64, out_wide.shape[1]), BF)
    weight_all[576:640, :] = jnp.zeros((64, weight_all.shape[1]), BF)

    def opening(micro):
        total = scatter_end(pbuf, micro, 0)
        hidden, normed, inverse = layer_norm(
            slot(grad_low, micro, 0)[...].astype(F32) + total + vector(0), vector(1), vector(2)
        )
        own_rows(hidden_rows, micro)[...] = hidden
        own_rows(normed_rows, micro)[...] = normed
        own_rows(inverse_rows, micro)[...] = jnp.broadcast_to(inverse, (share, 128))
        slot(hid, micro, 0)[...] = hidden.astype(BF)
        gather_start(hid, micro, 0)

    low_bias[...] = jnp.zeros_like(low_bias)
    for kind, ref in ((0, query_bias), (2, value_bias)):
        row = ref[...].reshape(1, -1)
        low_bias[0:1, 128 * kind : 128 * kind + 128] = row[:, 0:128]
        low_bias[0:1, 384 + 128 * kind : 448 + 128 * kind] = row[:, 128:192]
    for kind in range(3):
        gpre[448 + 128 * kind : 512 + 128 * kind, :] = jnp.zeros((64, gpre.shape[1]), BF)
    def find_segments(micro):
        ends = jnp.broadcast_to(lengths[micro], (8, rows_all))
        lane = lax.broadcasted_iota(jnp.int32, (8, rows_all), 1)
        shift = 1
        while shift < rows_all:
            ends = ends + jnp.where(lane >= shift, pltpu.roll(ends, shift, 1), 0)
            shift *= 2
        ends_col = column_of(ends[0:1, :].astype(F32))
        places = lax.broadcasted_iota(jnp.int32, (rows_all, rows_all), 1).astype(F32)
        count = jnp.sum(jnp.where(ends_col <= places, 1.0, 0.0), axis=0, keepdims=True)
        segment[8 * micro : 8 * micro + 8, :] = jnp.broadcast_to(count, (8, rows_all))

    find_segments(0)
    pl.semaphore_wait(barrier, len(partners))
    for handle in low_loads + [micro_loads[0], out_load]:
        handle.wait()
    qkv, value_t = gm2, key_t

    def project(micro):
        def one(index, carry):
            at = pl.multiple_of(index * share, share)
            rows = pl.ds(pl.multiple_of(micro * rows_all + index * share, share), share)
            qkv[rows, :] = (back_dot(act[rows, :], gpre[0:768, :]) + low_bias[0:1, :]).astype(BF)
            for tile in range(2):
                value_t[128 * tile : 128 * tile + 128, pl.ds(at, share)] = jnp.transpose(
                    qkv[rows, tile_lanes(2, tile)]
                )
            return carry

        lax.fori_loop(0, 4, one, 0)

    def attend(index, carry):
        micro, turn = index // 4, index % 4
        which = 3 - turn

        @pl.when(index == 4)
        def _():
            find_segments(1)
            micro_loads[1].wait()

        @pl.when(turn == 0)
        def _():
            project(micro)

        @pl.when(index == 4)
        def _():
            for handle in row_loads:
                handle.wait()
            opening(0)

        step = which ^ place
        block = pl.ds(pl.multiple_of(micro * rows_all, rows_all), rows_all)
        rows = pl.ds(pl.multiple_of(micro * rows_all + step * share, share), share)
        eight = pl.ds(pl.multiple_of(micro * 8, 8), 8)
        columns = pl.ds(pl.multiple_of(step * share, share), share)
        same = column_of(segment[eight, :][0:1, :]) == segment[eight, columns][0:1, :]
        outs = []
        logs = []
        for head in range(3):
            tile = head // 2
            query = qkv[rows, tile_lanes(0, tile)] * jnp.asarray(0.125, BF)
            query = lane_half(query, head % 2)
            keys = qkv[block, tile_lanes(1, tile)]
            scores = jnp.where(same, back_dot(keys, query), -1e30)
            top = jnp.max(scores, axis=0, keepdims=True)
            expo = jnp.exp(scores - top)
            total = jnp.sum(expo, axis=0, keepdims=True)
            probs = (expo * (1.0 / total)).astype(BF)
            outs.append(
                jnp.dot(
                    value_t[64 * head : 64 * head + 64, :], probs, preferred_element_type=F32
                )
            )
            logs.append(top + jnp.log(total))
        context_t = jnp.concatenate(outs, axis=0) * alive_of(micro)
        low = jnp.transpose(context_t).astype(BF)
        context[rows, :] = low
        log_total[eight, columns] = jnp.concatenate(logs + [jnp.zeros((5, share), F32)], axis=0)
        slot(pbuf, micro, which)[...] = jnp.dot(
            low, out_wide[0:192, :], preferred_element_type=F32
        ).astype(BF)

        @pl.when(turn == 0)
        def _():
            far_copy(pbuf, micro, 0).start()

        @pl.when(turn == 1)
        def _():
            scatter_mid(pbuf, micro, 0)

        @pl.when(turn == 2)
        def _():
            near_copy(pbuf, micro, 0).start()

        return carry

    lax.fori_loop(0, 8, attend, 0)
    qkv_store = load(gm2, qkv_hbm)
    for handle in weight_loads:
        handle.wait()
    scatter_drain(pbuf, 0, 0)
    scatter_drain(pbuf, 1, 0)

    def middle(micro):
        total = scatter_end(pbuf, micro, 1)
        final, normed, inverse = layer_norm(
            own_rows(hidden_rows, micro)[...] + total + vector(4), vector(5), vector(6)
        )
        grad_y = result[micro].astype(F32)
        result[micro] = final.astype(BF)
        grad_mid2 = norm_back(grad_y, normed, inverse, vector(5))
        own_rows(hidden_rows, micro)[...] = grad_mid2
        slot(gm2, micro, 0)[...] = grad_mid2.astype(BF)
        gather_start(gm2, micro, 1)
        tally(3, grad_mid2)
        tally(4, grad_y * normed)
        tally(5, grad_y)

    def forward(index, carry):
        micro, which = index // 4, index % 4

        @pl.when(index == 1)
        def _():
            qkv_store.wait()

        @pl.when(index == 4)
        def _():
            scatter_mid(pbuf, 0, 1)
            opening(1)

        @pl.when(index == 6)
        def _():
            middle(0)

        gather_step(hid, micro, 0, which)
        pre = (
            jnp.dot(slot(hid, micro, which)[...], in_weight[...], preferred_element_type=F32)
            + vector(3)
        )
        alive = alive_of(micro)
        below = 0.5 * (1.0 + lax.erf(pre * ROOT_HALF)) * alive
        low = (pre * below).astype(BF)
        slot(act, micro, which)[...] = low
        slot(slope, micro, which)[...] = (
            below + pre * jnp.exp(-0.5 * pre * pre) * (DENSITY_SCALE * alive)
        ).astype(BF)
        slot(pbuf, micro, which)[...] = jnp.dot(
            low, down_weight[...], preferred_element_type=F32
        ).astype(BF)

        @pl.when(which == 3)
        def _():
            scatter_start(pbuf, micro, 1)

        return carry

    lax.fori_loop(0, 8, forward, 0)
    scatter_mid(pbuf, 1, 1)
    scatter_drain(pbuf, 0, 1)

    def weigh(left, right, out, micro):
        rows = micro_block(micro)

        def block(index, carry):
            lanes = pl.ds(pl.multiple_of(index * 256, 256), 256)
            value = cross_dot(left[rows, lanes], right[rows, :])
            if micro == 0:
                out[lanes, :] = value
            else:
                out[lanes, :] += value
            return carry

        lax.fori_loop(0, out.shape[0] // 256, block, 0)

    def backward(index, carry):
        micro, which = index // 4, index % 4

        @pl.when(index == 4)
        def _():
            middle(1)
            scatter_drain(pbuf, 1, 1)
            scatter_mid(pbuf, 0, 2)
            weigh(act, gm2, down_term, 0)
            weigh(hid, gpre, in_term, 0)

        gather_step(gm2, micro, 1, which)
        grad_pre = (
            back_dot(slot(gm2, micro, which)[...], down_weight[...])
            * slot(slope, micro, which)[...].astype(F32)
        ).astype(BF)
        slot(gpre, micro, which)[...] = grad_pre
        tally(6, grad_pre.astype(F32))
        slot(pbuf, micro, which)[...] = back_dot(grad_pre, in_weight[...]).astype(BF)

        @pl.when(which == 3)
        def _():
            scatter_start(pbuf, micro, 2)

        return carry

    lax.fori_loop(0, 8, backward, 0)

    weigh(act, gm2, down_term, 1)
    for k in range(4):
        named["d" + str(k)].advance(0)
    scatter_mid(pbuf, 1, 2)
    for micro in range(2):
        gather_drain(hid, micro, 0)
        gather_drain(gm2, micro, 1)
    late_loads.extend(
        load(token_hbm.at[m], act.at[micro_block(m), :]) for m in range(2)
    )
    late_loads.append(load(qkv_hbm, gm2))
    weigh(hid, gpre, in_term, 1)
    for k in range(4):
        named["i" + str(k)].advance(0)

    def closing(micro):
        total = scatter_end(pbuf, micro, 2)
        grad_hidden = own_rows(hidden_rows, micro)[...] + total
        normed = own_rows(normed_rows, micro)[...]
        inverse = own_rows(inverse_rows, micro)[:, 0:1]
        grad = norm_back(grad_hidden, normed, inverse, vector(1))
        input_grad[micro] = grad
        slot(grad_low, micro, 0)[...] = grad.astype(BF)
        gather_start(grad_low, micro, 2)
        tally(0, grad)
        tally(1, grad_hidden * normed)
        tally(2, grad_hidden)

    reached = {name: 0 for name in named}
    reached["s"] = -1
    planned = {}
    for point in POINTS:
        planned[point] = []
        for name in EVENTS.get(point, ()):
            reached[name] += 1
            planned[point].append((name, reached[name]))

    def run(point):
        for name, step in planned[point]:
            (shared_sum if name == "s" else named[name]).advance(step)
            if name != "s" and step == named[name].last():
                named[name].home.start()

    run("open")
    for handle in late_loads:
        handle.wait()
    closing(0)
    run("closing")
    qkv, tokens, grads = gm2, act, gpre
    homes = [load(result.at[m], result_hbm.at[m]) for m in range(2)]

    def micro_rows(micro):
        return pl.ds(pl.multiple_of(micro * rows_all, rows_all), rows_all)

    def finish_grads(micro):
        block = micro_block(micro)
        grads[block, 128:256] = key_acc[block, 0:128].astype(BF)
        grads[block, 256:384] = value_acc[block, 0:128].astype(BF)
        grads[block, 448:512] = key_acc[block, 128:192].astype(BF)
        grads[block, 512:640] = value_acc[block, 128:256].astype(BF)
        bias_values[0:1, 0:640] += jnp.sum(
            grads[block, 0:640].astype(F32), axis=0, keepdims=True
        )


    def weigh_low(micro):
        block = micro_block(micro)
        for first, count in ((0, 256), (256, 256), (512, 64)):
            value = cross_dot(grads[block, first : first + count], tokens[block, :])
            if micro == 0:
                qkv_term[first : first + count, :] = value
            else:
                qkv_term[first : first + count, :] += value

    def send_input(micro):
        def send_slot(index, carry):
            start = pl.multiple_of(micro * rows_all + (index ^ place) * share, share)
            slot(pbuf, micro, index)[...] = jnp.dot(
                grads[pl.ds(start, share), 0:640], weight_all[...], preferred_element_type=F32
            ).astype(BF)
            return carry

        lax.fori_loop(0, 4, send_slot, 0)
        scatter_start(pbuf, micro, 3)

    def progress(index, head):
        for turn in range(8):
            if planned[3 * turn + head]:

                @pl.when(index == turn)
                def _():
                    run(3 * turn + head)

    def attend_back(index, carry):
        micro, which = (index // 2) % 2, (index // 4) * 2 + index % 2
        gather_step(grad_low, micro, 2, which)
        step = which ^ place
        block = micro_rows(micro)
        rows = pl.ds(pl.multiple_of(micro * rows_all + step * share, share), share)
        key_at = pl.multiple_of(micro * WIDE, WIDE)

        @pl.when(which == 0)
        def _():
            for tile in range(2):
                key_t[pl.ds(pl.multiple_of(key_at + 128 * tile, 128), 128), :] = jnp.transpose(
                    qkv[block, tile_lanes(1, tile)]
                )
            key_acc[block, :] = jnp.zeros((rows_all, WIDE), F32)
            value_acc[block, :] = jnp.zeros((rows_all, WIDE), F32)

        eight = pl.ds(pl.multiple_of(micro * 8, 8), 8)
        columns = pl.ds(pl.multiple_of(step * share, share), share)
        seg_row = segment[eight, columns][0:1, :]
        logs = log_total[eight, columns]
        grad_slot = slot(grad_low, micro, which)[...]
        out_term[...] += cross_dot(context[rows, :], grad_slot)

        @pl.when(index == 7)
        def _():
            named["o0"].advance(0)

        alive = alive_of(micro).astype(BF)
        grad_context = back_dot(grad_slot, out_wide[...]).astype(BF) * alive
        same = column_of(segment[eight, :][0:1, :]) == seg_row
        query_parts = []
        for head in range(3):
            tile = head // 2
            lanes = slice(128 * tile, 128 * tile + 128)
            query = qkv[rows, tile_lanes(0, tile)] * jnp.asarray(0.125, BF)
            query = lane_half(query, head % 2)
            grad_tile = lane_half(grad_context[:, lanes], head % 2)
            keys = qkv[block, tile_lanes(1, tile)]
            values = qkv[block, tile_lanes(2, tile)]
            scores = jnp.where(same, back_dot(keys, query), -1e30)
            probs = jnp.exp(scores - logs[head : head + 1, :])
            grad_probs = back_dot(values, grad_tile)
            mean = jnp.sum(probs * grad_probs, axis=0, keepdims=True)
            grad_scores = (probs * (grad_probs - mean)).astype(BF)
            value_acc[block, lanes] += jnp.dot(
                probs.astype(BF), grad_tile, preferred_element_type=F32
            )
            key_acc[block, lanes] += jnp.dot(grad_scores, query, preferred_element_type=F32)
            query_parts.append(
                jnp.dot(
                    key_t[pl.ds(pl.multiple_of(key_at + 64 * head, 64), 64), :],
                    grad_scores,
                    preferred_element_type=F32,
                )
            )
            if head < 2:
                progress(index, head)
        query_t = jnp.concatenate(query_parts + [jnp.zeros((64, share), F32)], axis=0) * 0.125
        query_grad = jnp.transpose(query_t).astype(BF)
        grads[rows, 0:128] = query_grad[:, 0:128]
        grads[rows, 384:448] = query_grad[:, 128:192]

        progress(index, 2)

        @pl.when(index == 1)
        def _():
            closing(1)
            run("closed")

        @pl.when(index == 5)
        def _():
            for micro in range(2):
                scatter_drain(pbuf, micro, 2)
            finish_grads(0)
            send_input(0)
            run("between")
            weigh_low(0)
            run("weighed")

        @pl.when(index == 6)
        def _():
            scatter_mid(pbuf, 0, 3)

        return carry

    lax.fori_loop(0, 8, attend_back, 0)
    finish_grads(1)
    weigh_low(1)
    for k in range(3):
        named["q" + str(k)].advance(0)
    bias_sum.advance(0)
    run("start")
    send_input(1)
    run("pre")
    scatter_mid(pbuf, 1, 3)
    run("mid")

    def final_rows(micro):
        input_grad[micro] = input_grad[micro] + scatter_end(pbuf, micro, 3)
        homes.append(load(input_grad.at[micro], input_hbm.at[micro]))

    final_rows(0)
    run("tail")
    final_rows(1)
    for index in range(1, batch_bits + 1):
        bias_sum.advance(index)
    run("end")
    for name in sorted(named):
        while reached[name] < named[name].last():
            reached[name] += 1
            named[name].advance(reached[name])
            if reached[name] == named[name].last():
                named[name].home.start()
    while reached["s"] < batch_bits + 2:
        reached["s"] += 1
        shared_sum.advance(reached["s"])

    base = 8 * batch_bits
    sums_out[...] = vec_values[base + 16 : base + 24, :]
    sums_out[6:7, :] = vec_values[base + 6 : base + 7, :]
    bias_out[...] = bias_values[base : base + 8, :]
    for micro in range(2):
        scatter_drain(pbuf, micro, 3)
        gather_drain(grad_low, micro, 2)
    for owner in chunks + [shared_sum, bias_sum]:
        owner.drain()
    for owner in chunks:
        owner.home.wait()
    for handle in homes:
        handle.wait()


def layer_call(
    quarters, tokens, cotangent, in_weight, down_weight, query_weight, key_weight, value_weight,
    out_weight, lengths, query_bias, value_bias, *vectors
):
    micro_count, rows_all, width = tokens.shape
    share = rows_all // 4
    rows = micro_count * rows_all
    units = in_weight.shape[1]
    batch_bits = lax.axis_size("batch").bit_length() - 1
    order = tuple(range(batch_bits))
    small = reduce_plan(192, order)[1]
    vmem = pl.BlockSpec(memory_space=pltpu.VMEM)
    hbm = pl.BlockSpec(memory_space=pl.ANY)
    smem = pl.BlockSpec(memory_space=pltpu.SMEM)
    batch_sems = 14 * 2 * batch_bits + 2
    return pl.pallas_call(
        layer_kernel,
        in_specs=[smem] + [hbm] * 8 + [vmem] * (3 + len(vectors)),
        out_specs=[hbm] * 6 + [vmem] * 2 + [hbm],
        out_shape=[
            jax.ShapeDtypeStruct((micro_count, share, width), BF),
            jax.ShapeDtypeStruct((micro_count, share, width), F32),
            jax.ShapeDtypeStruct((width, units), BF),
            jax.ShapeDtypeStruct((units, width), BF),
            jax.ShapeDtypeStruct((576, width), BF),
            jax.ShapeDtypeStruct((192, width), BF),
            jax.ShapeDtypeStruct((8, width), F32),
            jax.ShapeDtypeStruct((8, width), F32),
            jax.ShapeDtypeStruct((rows, 3 * WIDE), BF),
        ],
        scratch_shapes=[
            pltpu.VMEM((micro_count, share, width), BF),
            pltpu.VMEM((micro_count, share, width), F32),
            pltpu.VMEM((width, units), BF),
            pltpu.VMEM((units, width), BF),
            pltpu.VMEM((576, width), BF),
            pltpu.VMEM((192, width), BF),
            pltpu.VMEM((width, units), BF),
            pltpu.VMEM((units, width), BF),
            pltpu.VMEM((rows, 192), BF),
            pltpu.VMEM((8 * micro_count, rows_all), F32),
            pltpu.VMEM((8 * micro_count, rows_all), F32),
            pltpu.VMEM((8, 3 * WIDE), F32),
            pltpu.VMEM((width, units), F32),
            pltpu.VMEM((units, width), F32),
            pltpu.VMEM((576, width), F32),
            pltpu.VMEM((192, width), F32),
            pltpu.VMEM((640, width), BF),
            pltpu.VMEM((2 * share, width), BF),
            pltpu.VMEM((2 * share, width), BF),
            pltpu.VMEM((2 * share, width), BF),
            pltpu.VMEM((2 * share, width), BF),
            pltpu.VMEM((rows, width), BF),
            pltpu.VMEM((rows, width), BF),
            pltpu.VMEM((rows, units), BF),
            pltpu.VMEM((rows, units), BF),
            pltpu.VMEM((rows, units), BF),
            pltpu.VMEM((rows, width), BF),
            pltpu.VMEM((rows, width), BF),
            pltpu.VMEM((2 * share, width), F32),
            pltpu.VMEM((2 * share, width), F32),
            pltpu.VMEM((2 * share, 128), F32),
            pltpu.VMEM((micro_count * WIDE, rows_all), BF),
            pltpu.VMEM((rows, WIDE), F32),
            pltpu.VMEM((rows, WIDE), F32),
            pltpu.VMEM((WIDE, width), BF),
            pltpu.VMEM((4 * small, width), BF),
            pltpu.VMEM((4 * small, width), BF),
            pltpu.VMEM((3 * small, width), BF),
            pltpu.VMEM((small, width), BF),
            pltpu.VMEM((8 * (batch_bits + 3), width), F32),
            pltpu.VMEM((8 * (batch_bits + 2), width), F32),
            pltpu.VMEM((8 * (batch_bits + 1), width), F32),
            pltpu.VMEM((8 * batch_bits, width), F32),
            pltpu.SemaphoreType.DMA((48,)),
            pltpu.SemaphoreType.DMA((48,)),
            pltpu.SemaphoreType.DMA((batch_sems,)),
            pltpu.SemaphoreType.DMA((batch_sems,)),
            pltpu.SemaphoreType.DMA((56,)),
        ],
        compiler_params=pltpu.CompilerParams(
            collective_id=1, has_side_effects=True, vmem_limit_bytes=67_043_328
        ),
        name="layer",
    )(
        quarters, tokens, cotangent, in_weight, down_weight, query_weight, key_weight,
        value_weight, out_weight, lengths, query_bias, value_bias, *vectors
    )


def finish_kernel(
    result_in, grad_in, in_low, down_low, packed, out_low, sums, bias,
    result, input_grad, query, query_bias, key, value, value_bias, out, out_bias, gain1, shift1,
    in_out, in_bias, down, down_bias, gain2, shift2,
    result_buf, grad_buf, in_buf, down_buf, packed_buf, out_buf, in_wide, down_wide, packed_wide,
    out_wide, sems,
):
    taken = []

    def move(src, dst):
        taken.append(0)
        handle = pltpu.make_async_copy(src, dst, sems.at[len(taken) - 1])
        handle.start()
        return handle

    inner = out_low.shape[0]
    low = (
        (in_low, in_buf, in_wide, ((0, in_low.shape[0], in_out, 0),)),
        (down_low, down_buf, down_wide, ((0, down_low.shape[0], down, 0),)),
        (
            packed, packed_buf, packed_wide,
            tuple(
                part
                for kind, ref in enumerate((query, key, value))
                for part in ((128 * kind, 128, ref, 0), (384 + 64 * kind, 64, ref, 128))
            ),
        ),
        (out_low, out_buf, out_wide, ((0, inner, out, 0),)),
    )
    loads = [move(src, buf) for src, buf, _, _ in low]
    through = [(move(grad_in, grad_buf), grad_buf, input_grad)]
    through.append((move(result_in, result_buf), result_buf, result))
    stores = []
    for load, (_, buf, wide, parts) in zip(loads, low):
        load.wait()
        wide[...] = buf[...].astype(F32)
        for start, size, ref, at in parts:
            stores.append(move(wide.at[start : start + size, :], ref.at[at : at + size, :]))
    for load, buf, ref in through:
        load.wait()
        stores.append(move(buf, ref))
    for index, ref in ((0, out_bias), (1, gain1), (2, shift1), (3, down_bias), (4, gain2), (5, shift2), (6, in_bias)):
        ref[...] = sums[index, :]
    for kind, ref in ((0, query_bias), (2, value_bias)):
        row = bias[0:1, 128 * kind : 128 * kind + 128]
        tail = bias[0:1, 384 + 64 * kind : 448 + 64 * kind]
        ref[...] = jnp.concatenate([row, tail], axis=1).reshape(inner)
    for store in stores:
        store.wait()


def finish(result, input_grad, in_sum, down_sum, packed, out_sum, sums, bias):
    width, units = in_sum.shape
    inner = out_sum.shape[0]
    hbm = pl.BlockSpec(memory_space=pl.ANY)
    vmem = pl.BlockSpec(memory_space=pltpu.VMEM)
    shape = jax.ShapeDtypeStruct
    wide = shape((inner, width), F32)
    row = shape((width,), F32)
    short = shape((inner,), F32)
    outs = pl.pallas_call(
        finish_kernel,
        in_specs=[hbm] * 6 + [vmem] * 2,
        out_specs=[
            hbm, hbm, hbm, vmem, hbm, hbm, vmem, hbm, vmem, vmem, vmem, hbm, vmem, hbm, vmem,
            vmem, vmem,
        ],
        out_shape=[
            shape(result.shape, BF), shape(input_grad.shape, F32), wide, short, wide, wide,
            short, wide, row, row, row, shape((width, units), F32), shape((units,), F32),
            shape((units, width), F32), row, row, row,
        ],
        scratch_shapes=[
            pltpu.VMEM(result.shape, BF),
            pltpu.VMEM(input_grad.shape, F32),
            pltpu.VMEM(in_sum.shape, BF),
            pltpu.VMEM(down_sum.shape, BF),
            pltpu.VMEM(packed.shape, BF),
            pltpu.VMEM(out_sum.shape, BF),
            pltpu.VMEM(in_sum.shape, F32),
            pltpu.VMEM(down_sum.shape, F32),
            pltpu.VMEM(packed.shape, F32),
            pltpu.VMEM(out_sum.shape, F32),
            pltpu.SemaphoreType.DMA((18,)),
        ],
        compiler_params=pltpu.CompilerParams(vmem_limit_bytes=67_043_328),
        name="finish",
    )(result, input_grad, in_sum, down_sum, packed, out_sum, sums, bias)
    outs = list(outs)
    for index in (2, 4, 5):
        outs[index] = outs[index].T
    return tuple(outs)


def local(
    tokens,
    lengths,
    quarters,
    query_weight,
    query_bias,
    key_weight,
    value_weight,
    value_bias,
    out_weight,
    out_bias,
    norm1_gain,
    norm1_shift,
    in_weight,
    in_bias,
    down_weight,
    down_bias,
    norm2_gain,
    norm2_shift,
    cotangent,
):
    result, input_grad, in_sum, down_sum, packed, out_sum, sums, bias, _ = layer_call(
        quarters,
        tokens,
        cotangent,
        in_weight,
        down_weight,
        query_weight.T,
        key_weight.T,
        value_weight.T,
        out_weight,
        lengths.reshape(lengths.shape[0], 1, lengths.shape[2]),
        query_bias,
        value_bias,
        out_bias,
        norm1_gain,
        norm1_shift,
        in_bias,
        down_bias,
        norm2_gain,
        norm2_shift,
    )

    return finish(result, input_grad, in_sum, down_sum, packed, out_sum, sums, bias)


def solution(mesh):
    in_specs = (
        P(None, "batch", None),
        P(None, "batch", None),
        P(),
        P(None, "tensor"),
        P("tensor"),
        P(None, "tensor"),
        P(None, "tensor"),
        P("tensor"),
        P("tensor", None),
        P(),
        P(),
        P(),
        P(None, "tensor"),
        P("tensor"),
        P("tensor", None),
        P(),
        P(),
        P(),
        P(None, "batch", None),
    )
    out_specs = (
        P(None, ("batch", "tensor"), None),
        P(None, ("batch", "tensor"), None),
        P(None, "tensor"),
        P("tensor"),
        P(None, "tensor"),
        P(None, "tensor"),
        P("tensor"),
        P("tensor", None),
        P(),
        P(),
        P(),
        P(None, "tensor"),
        P("tensor"),
        P("tensor", None),
        P(),
        P(),
        P(),
    )
    return jax.shard_map(local, mesh=mesh, in_specs=in_specs, out_specs=out_specs, check_vma=False)
```
